128 devices in a mesh: dp: 32 (over y, x, core), head: 4 (over z).
Axes of the slice: x: 4, y: 4, z: 4, core: 2. Of those that a mesh axis runs over, the one named last changes fastest.
Arguments:
- feats: bfloat16 [4, 65536, 384], P('head', 'dp'), may hold values from -6 to 6
- valid: int32 [256], P('dp'), may hold values from 1 to 256
- owner_map: int32 [256], P('dp'), may hold values from 0 to 31, as said below
- w_conv: bfloat16 [4, 3, 384, 384], P('head', None, 'dp'), may hold values from -0.11785113 to 0.11785113
- w_mid: bfloat16 [4, 384, 384], P('head', 'dp'), may hold values from -0.20412415 to 0.20412415
- w_out: bfloat16 [4, 384], P('head', 'dp'), may hold values from -0.20412415 to 0.20412415
Outputs:
- grad_feats: bfloat16 [4, 131072, 384], P('head', 'dp')
- grad_conv: float32 [4, 3, 384, 384], P('head', None, 'dp')
- grad_mid: float32 [4, 384, 384], P('head', 'dp')
- grad_out: float32 [4, 384], P('head', 'dp')
The draws below stay inside these ranges and needn't reach their ends.
Inputs may be any that keep to these rules, and one draw needn't show every extreme that they name: `owner_map`: image o is held by index o of dp. Every image owns 1 to 16 blocks; a quarter of the images own exactly 16. The 8 blocks of one index of dp belong to 8 different images.
All inputs are finite; a program needn't handle non-finite values.
Results may differ from the reference program's by a relative error of at most 0.019.
Values may be sent and summed in bfloat16 or wider, within the bound.
No kernel may reach another device: no remote copies, remote signals or barrier semaphores. Data moves between devices by JAX's collectives and lax.ppermute only.
A program may use at most 128 MiB of HBM per device.

```python
import jax
import jax.numpy as jnp
from jax import lax

D = 384
TAPS = 4
BT = 256
BLK_DEV = 8
CAP = 16
NB = 256
N_DP = 32


def draw_owner_map(key, part):
    devices = NB // BLK_DEV
    per_device = BLK_DEV
    first, second, third = jax.random.split(jax.random.fold_in(key, 7), 3)
    labels = jax.random.permutation(first, devices).astype(jnp.int32)
    position = jax.random.permutation(second, devices).astype(jnp.int32)
    member = jnp.where(position < devices // 2, 0, jnp.where(position < 3 * devices // 4, 1, jnp.where(position < 7 * devices // 8, 2, 3))).astype(jnp.int32)
    table = 4 * jnp.arange(per_device, dtype=jnp.int32)[None, :] + member[:, None]
    scores = jax.random.randint(third, (devices, per_device), 0, 1 << 20) * per_device + jnp.arange(per_device, dtype=jnp.int32)[None, :]
    order = jnp.argsort(scores, axis=1)
    table = jnp.take_along_axis(table, order, 1)
    return labels[table].reshape(-1).astype(jnp.int32)


def centered(values, spread, column_axis):
    values = values - jnp.mean(values, axis=column_axis, keepdims=True)
    return jnp.clip(values, -4.0 * spread, 4.0 * spread)


def draw_feats(key, part):
    first = jax.random.fold_in(jax.random.fold_in(key, 11), 0)
    shape = (TAPS, NB * BT, D)
    values = jax.random.normal(first, shape, jnp.float32)
    return jnp.clip(values, -6.0, 6.0).astype(jnp.bfloat16)


def draw_w_conv(key, part):
    first = jax.random.fold_in(key, 13)
    spread = (3.0 * D) ** (-0.5)
    shape = (TAPS, 3, D, D)
    values = jax.random.normal(first, shape, jnp.float32) * spread
    return jnp.clip(values, -4.0 * spread, 4.0 * spread).astype(jnp.bfloat16)


def draw_w_mid(key, part):
    first = jax.random.fold_in(key, 17)
    spread = D ** (-0.5)
    shape = (TAPS, D, D)
    values = jnp.clip(jax.random.normal(first, shape, jnp.float32), -4.0, 4.0) * spread
    return centered(values, spread, 1).astype(jnp.bfloat16)


def draw_w_out(key, part):
    first = jax.random.fold_in(key, 19)
    spread = D ** (-0.5)
    shape = (TAPS, D)
    values = jnp.clip(jax.random.normal(first, shape, jnp.float32), -4.0, 4.0) * spread
    return centered(values, spread, 1).astype(jnp.bfloat16)


def plant(drawn, key, smallest, top_value):
    spot = [jax.random.randint(jax.random.fold_in(key, axis), (), 0, length) for axis, length in enumerate(drawn.shape)]
    longest = drawn.shape.index(max(drawn.shape))
    beside = spot[:longest] + [(spot[longest] + 1) % drawn.shape[longest]] + spot[longest + 1:]
    return drawn.at[tuple(spot)].set(smallest).at[tuple(beside)].set(top_value)


def setup_inputs(seed: int = 0) -> dict:
    arg_keys = jax.random.split(jax.random.key(seed), 7)
    return {
        "feats": draw_feats(jax.random.fold_in(arg_keys[6], 71), 0),
        "valid": plant(jax.random.randint(arg_keys[1], (NB,), 1, BT + 1), jax.random.fold_in(arg_keys[1], 1), 1, BT).astype(jnp.int32),
        "owner_map": draw_owner_map(jax.random.fold_in(arg_keys[6], 71), 0),
        "w_conv": draw_w_conv(jax.random.fold_in(arg_keys[6], 71), 0),
        "w_mid": draw_w_mid(jax.random.fold_in(arg_keys[6], 71), 0),
        "w_out": draw_w_out(jax.random.fold_in(arg_keys[6], 71), 0),
    }


def activate(value):
    return 0.2 * value + 0.8 * jax.nn.softplus(value)

def derivative(value):
    return 0.2 + 0.8 * jax.nn.sigmoid(value)

def flatten(array):
    return array.reshape(-1, array.shape[-1])

def forward_pass(blocks, mask, conv_w, mid_w, out_w):
    count = blocks.shape[0]
    width = blocks.shape[2]
    masked = (blocks * mask[:, :, None]).astype(jnp.bfloat16)
    zero_row = jnp.zeros((count, 1, width), jnp.bfloat16)
    previous = jnp.concatenate([zero_row, masked[:, :-1]], 1)
    following = jnp.concatenate([masked[:, 1:], zero_row], 1)
    first_pre = jnp.dot(flatten(previous), conv_w[0], preferred_element_type=jnp.float32)
    first_pre = first_pre + jnp.dot(flatten(masked), conv_w[1], preferred_element_type=jnp.float32)
    first_pre = first_pre + jnp.dot(flatten(following), conv_w[2], preferred_element_type=jnp.float32)
    first_act = activate(first_pre)
    first_low = first_act.astype(jnp.bfloat16)
    second_pre = jnp.dot(first_low, mid_w, preferred_element_type=jnp.float32)
    second_act = activate(second_pre) + first_act
    logits = jnp.dot(second_act, out_w.astype(jnp.float32), precision=lax.Precision.HIGHEST)
    return ((previous, masked, following, first_pre, first_low, second_pre, second_act), logits)

def backward_pass(saved, upstream, mask, conv_w, mid_w, out_w):
    previous, masked, following, first_pre, first_low, second_pre, second_act = saved
    count, length, width = masked.shape
    grad_second = upstream[:, None] * out_w.astype(jnp.float32)[None, :]
    grad_mid_pre = (grad_second * derivative(second_pre)).astype(jnp.bfloat16)
    grad_first = jnp.dot(grad_mid_pre, mid_w.T, preferred_element_type=jnp.float32) + grad_second
    grad_first_pre = (grad_first * derivative(first_pre)).astype(jnp.bfloat16)

    def through(index):
        return jnp.dot(grad_first_pre, conv_w[index].T, preferred_element_type=jnp.float32).reshape(count, length, width)
    zero_row = jnp.zeros((count, 1, width), jnp.float32)
    from_next = through(0)
    from_prev = through(2)
    total = through(1) + jnp.concatenate([from_next[:, 1:], zero_row], 1) + jnp.concatenate([zero_row, from_prev[:, :-1]], 1)
    grad_input = (total * mask[:, :, None]).astype(jnp.bfloat16)
    grad_conv = jnp.stack([jnp.dot(flatten(previous).T, grad_first_pre, preferred_element_type=jnp.float32), jnp.dot(flatten(masked).T, grad_first_pre, preferred_element_type=jnp.float32), jnp.dot(flatten(following).T, grad_first_pre, preferred_element_type=jnp.float32)])
    grad_mid = jnp.dot(first_low.T, grad_mid_pre, preferred_element_type=jnp.float32)
    grad_out = jnp.dot(upstream, second_act, precision=lax.Precision.HIGHEST)
    return (grad_input, grad_conv, grad_mid, grad_out)

def reference(feats, valid, owner_map, w_conv, w_mid, w_out):
    blocks_all = owner_map.shape[0]
    member_int = (owner_map[:, None] == jnp.arange(N_DP, dtype=jnp.int32)[None, :]).astype(jnp.int32)
    earlier = jnp.cumsum(member_int, 0) - member_int
    slots = lax.optimization_barrier(jnp.sum(earlier * member_int, 1)).astype(jnp.int32)
    tokens = lax.optimization_barrier(jnp.sum(member_int * valid[:, None], 0)).astype(jnp.float32)
    members = member_int.astype(jnp.float32)
    mask = (jnp.arange(BT, dtype=jnp.int32)[None, :] < valid[:, None]).astype(jnp.float32)
    scale_norm = jnp.sqrt(TAPS * tokens)
    saved_all = []
    totals = jnp.zeros((N_DP,), jnp.float32)
    for tap in range(TAPS):
        blocks = feats[tap].reshape(blocks_all, BT, D)
        saved, logits = forward_pass(blocks, mask, w_conv[tap], w_mid[tap], w_out[tap])
        saved_all.append(saved)
        block_sums = lax.optimization_barrier(jnp.sum(logits.reshape(blocks_all, BT) * mask, 1))
        totals = totals + jnp.dot(block_sums, members, precision=lax.Precision.HIGHEST)
    strength = totals / scale_norm
    factor = -BT * jax.nn.sigmoid(-strength) / scale_norm
    upstream = (jnp.dot(members, factor, precision=lax.Precision.HIGHEST)[:, None] * mask).reshape(-1)
    target = (owner_map * CAP + slots).astype(jnp.int32)
    feat_list, conv_list, mid_list, out_list = ([], [], [], [])
    for tap in range(TAPS):
        grad_input, grad_conv, grad_mid, grad_out = backward_pass(saved_all[tap], upstream, mask, w_conv[tap], w_mid[tap], w_out[tap])
        placed = jnp.zeros((N_DP * CAP, BT, D), jnp.bfloat16).at[target].set(grad_input)
        feat_list.append(placed.reshape(N_DP * CAP * BT, D))
        conv_list.append(grad_conv / blocks_all)
        mid_list.append(grad_mid / blocks_all)
        out_list.append(grad_out / blocks_all)
    return (jnp.stack(feat_list), jnp.stack(conv_list), jnp.stack(mid_list), jnp.stack(out_list))
```

```python
import functools

import jax
import jax.numpy as jnp
from jax import lax
from jax.experimental import pallas as pl
from jax.experimental.pallas import tpu as pltpu
from jax.sharding import Mesh
from jax.sharding import PartitionSpec as P

DP = ("dp_0", "dp_1", "dp_2")
CHIPS = ("dp_0", "dp_1")
WHOLE = ("head", "dp_1", "dp_0", "dp_2")
BF16 = jnp.bfloat16
F32 = jnp.float32
TAPS = 4
BT = 256
D = 384
ROWS = 56
GROUP = 2
VMEM_LIMIT = 56 * 1024 * 1024


def swapped(x):
    return lax.ppermute(x, "dp_2", [(0, 1), (1, 0)])


def turned(x, axis, shift):
    count = lax.axis_size(axis)
    return lax.ppermute(x, axis, [(i, (i + shift) % count) for i in range(count)])


def total_over(x, axes):
    for axis in axes:
        x = sum((turned(x, axis, r) for r in range(1, lax.axis_size(axis))), x)
    return x


def scattered_sum(parts, axis, dim):
    count, index = lax.axis_size(axis), lax.axis_index(axis)

    def piece(shift):
        return lax.dynamic_index_in_dim(parts, (index + shift) % count, dim, keepdims=False)

    total = piece(0).astype(F32)
    for r in range(1, count):
        total = total + turned(piece(r).astype(BF16), axis, r).astype(F32)
    return total


def gate(value):
    half = jnp.tanh(0.5 * value)
    act = jnp.maximum(value, 0.2 * value) - 0.8 * jnp.log(0.5 + 0.5 * jnp.abs(half))
    return act, 0.6 + 0.4 * half


def row_mask(valid_ref, step, blocks):
    rows = lax.broadcasted_iota(jnp.int32, (blocks * BT, 1), 0)
    limit = jnp.full_like(rows, valid_ref[step * blocks])
    for j in range(1, blocks):
        limit = jnp.where(rows < j * BT, limit, j * BT + valid_ref[step * blocks + j])
    return rows < limit


def neighbours(x):
    count = x.shape[0]
    place = lax.broadcasted_iota(jnp.int32, (count, 1), 0) % BT
    before = jnp.where(place == 0, 0.0, pltpu.roll(x, 1, 0))
    after = jnp.where(place == BT - 1, 0.0, pltpu.roll(x, count - 1, 0))
    return before, after


def forward_kernel(
    valid_ref, core_ref, feats_ref, own_ref, other_ref, out_w_ref,
    low_ref, mid_grad_ref, slope_ref, sums_ref, weights_ref, wide_ref,
):
    step = pl.program_id(0)

    def unpack(parity, source):
        for chip in range(source.shape[0]):
            tile = source[chip].astype(F32)
            at = 12 * (2 * chip + parity)
            for k in range(4):
                wide_ref[k, at : at + 12, :] = tile[12 * k : 12 * k + 12]

    @pl.when(step == 0)
    def _():
        @pl.when(core_ref[0] == 0)
        def _():
            unpack(0, own_ref)
            unpack(1, other_ref)

        @pl.when(core_ref[0] == 1)
        def _():
            unpack(1, own_ref)
            unpack(0, other_ref)

        weights_ref[...] = wide_ref[...].astype(BF16)

    keep = row_mask(valid_ref, step, GROUP)
    masked = jnp.where(keep, feats_ref[...].astype(F32), 0.0)
    before, after = neighbours(masked)
    first = jnp.dot(before.astype(BF16), weights_ref[0], preferred_element_type=F32)
    first += jnp.dot(masked.astype(BF16), weights_ref[1], preferred_element_type=F32)
    first += jnp.dot(after.astype(BF16), weights_ref[2], preferred_element_type=F32)
    first_act, slope = gate(first)
    low = first_act.astype(BF16)
    low_ref[...] = low
    slope_ref[...] = slope.astype(BF16)
    second = jnp.dot(low, weights_ref[3], preferred_element_type=F32)
    second_act, second_slope = gate(second)
    mid_grad_ref[...] = jnp.where(keep, out_w_ref[...] * second_slope, 0.0).astype(BF16)
    total = jnp.where(keep, second_act + first_act, 0.0)
    for j in range(GROUP):
        sums_ref[j] = jnp.sum(total[j * BT : (j + 1) * BT], 0, keepdims=True)


def backward_kernel(
    valid_ref, owner_ref, mid_grad_ref, slope_ref, weights_ref, out_w_ref, first_grad_ref, slots_ref
):
    step = pl.program_id(0)
    keep = row_mask(valid_ref, step, 1)
    turn = (((1,), (1,)), ((), ()))
    grad = lax.dot_general(mid_grad_ref[...], weights_ref[3], turn, preferred_element_type=F32)
    grad = (grad + jnp.where(keep, out_w_ref[...], 0.0)) * slope_ref[...].astype(F32)
    low = grad.astype(BF16)
    first_grad_ref[...] = low
    before, after = neighbours(low.astype(F32))
    total = lax.dot_general(low, weights_ref[1], turn, preferred_element_type=F32)
    total += lax.dot_general(after.astype(BF16), weights_ref[0], turn, preferred_element_type=F32)
    total += lax.dot_general(before.astype(BF16), weights_ref[2], turn, preferred_element_type=F32)
    slots_ref[0] = jnp.where(keep, total, 0.0).astype(BF16)


def weight_kernel(
    valid_ref, factor_ref, feats_ref, low_ref, mid_grad_ref, first_grad_ref, out_part_ref,
    parts_ref, conv_ref, mid_ref, stage_ref,
):
    step = pl.program_id(0)
    keep = row_mask(valid_ref, step, 1)
    factor = factor_ref[step]
    over_rows = (((0,), (0,)), ((), ()))
    masked = jnp.where(keep, feats_ref[...].astype(F32), 0.0).astype(BF16)
    grad = first_grad_ref[...].astype(F32) * factor
    before, after = neighbours(grad)
    wide = jnp.concatenate([after, grad, before], axis=1).astype(BF16)
    conv = lax.dot_general(masked, wide, over_rows, preferred_element_type=F32)
    mid_grad = (mid_grad_ref[...].astype(F32) * factor).astype(BF16)
    mid = lax.dot_general(low_ref[...], mid_grad, over_rows, preferred_element_type=F32)

    @pl.when(step == 0)
    def _():
        conv_ref[...] = conv
        mid_ref[...] = mid

    @pl.when(step > 0)
    def _():
        conv_ref[...] += conv
        mid_ref[...] += mid

    @pl.when(step == pl.num_programs(0) - 1)
    def _():
        stage_ref[48:56, :] = jnp.zeros((8, D), F32)
        for d in range(parts_ref.shape[0]):
            at = 12 * d
            for k in range(3):
                stage_ref[12 * k : 12 * k + 12, :] = conv_ref[at : at + 12, k * D : (k + 1) * D]
            stage_ref[36:48, :] = mid_ref[at : at + 12, :]
            stage_ref[48:49, :] = out_part_ref[d : d + 1, :]
            parts_ref[d] = stage_ref[...].astype(BF16)


def place_kernel(source_ref, count_ref, factor_ref, received_ref, placed_ref):
    slot = pl.program_id(0)

    @pl.when(slot < count_ref[0])
    def _():
        placed_ref[...] = (received_ref[0].astype(F32) * factor_ref[0]).astype(BF16)

    @pl.when(slot >= count_ref[0])
    def _():
        placed_ref[...] = jnp.zeros_like(placed_ref)


def params():
    return pltpu.CompilerParams(
        dimension_semantics=("arbitrary",), vmem_limit_bytes=VMEM_LIMIT
    )


def fixed(shape):
    return pl.BlockSpec(shape, lambda *_: (0,) * len(shape))


def rows(count):
    return pl.BlockSpec((count, D), lambda i, *_: (i, 0))


def per_device(feats, valid, owner_map, w_conv, w_mid, w_out):
    local = owner_map.shape[0]
    devices = lax.axis_size(DP)
    chips = devices // 2
    capacity = devices // 2
    tokens_here = local * BT
    me = lax.axis_index(DP)
    core = lax.axis_index("dp_2").astype(jnp.int32).reshape(1)

    extras = jnp.concatenate([w_out[0], owner_map.astype(BF16), valid.astype(BF16)])
    extras = jnp.pad(extras, (0, D - extras.shape[0]))[None]
    shard = jnp.concatenate([w_conv[0].reshape(-1, D), w_mid[0], extras], axis=0)
    shard = jnp.pad(shard, ((0, ROWS - shard.shape[0]), (0, 0)))
    copies = jnp.broadcast_to(shard[None], (chips, ROWS, D))
    own = lax.all_to_all(copies, CHIPS, split_axis=0, concat_axis=0, tiled=True)
    other = swapped(own)

    gathered = jnp.stack([own[:, 48, :32], other[:, 48, :32]])
    gathered = jnp.where(core[0] == 0, gathered, gathered[::-1])
    gathered = gathered.transpose(1, 0, 2).reshape(devices, 32).astype(F32)
    out_w = gathered[:, :12].reshape(1, D)
    owners = gathered[:, 12 : 12 + local].astype(jnp.int32)
    valids = gathered[:, 20 : 20 + local]

    low, mid_grad, slope, sums, weights = pl.pallas_call(
        forward_kernel,
        grid_spec=pltpu.PrefetchScalarGridSpec(
            num_scalar_prefetch=2,
            grid=(local // GROUP,),
            in_specs=[
                rows(GROUP * BT),
                fixed((chips, ROWS, D)),
                fixed((chips, ROWS, D)),
                fixed((1, D)),
            ],
            out_specs=[
                rows(GROUP * BT),
                rows(GROUP * BT),
                rows(GROUP * BT),
                pl.BlockSpec((GROUP, 1, D), lambda i, *_: (i, 0, 0)),
                fixed((4, D, D)),
            ],
            scratch_shapes=[pltpu.VMEM((4, D, D), F32)],
        ),
        out_shape=[
            jax.ShapeDtypeStruct((tokens_here, D), BF16),
            jax.ShapeDtypeStruct((tokens_here, D), BF16),
            jax.ShapeDtypeStruct((tokens_here, D), BF16),
            jax.ShapeDtypeStruct((local, 1, D), F32),
            jax.ShapeDtypeStruct((4, D, D), BF16),
        ],
        compiler_params=params(),
        name="forward",
    )(valid, core, feats[0], own, other, out_w)

    first_grad, slots = pl.pallas_call(
        backward_kernel,
        grid_spec=pltpu.PrefetchScalarGridSpec(
            num_scalar_prefetch=2,
            grid=(local,),
            in_specs=[rows(BT), rows(BT), fixed((4, D, D)), fixed((1, D))],
            out_specs=[
                rows(BT),
                pl.BlockSpec((1, BT, D), lambda i, valid_ref, owner_ref: (owner_ref[i], 0, 0)),
            ],
        ),
        out_shape=[
            jax.ShapeDtypeStruct((tokens_here, D), BF16),
            jax.ShapeDtypeStruct((devices, BT, D), BF16),
        ],
        compiler_params=params(),
        name="backward",
    )(valid, owner_map, mid_grad, slope, weights, out_w)

    received = lax.all_to_all(slots, DP, split_axis=0, concat_axis=0, tiled=True)

    images = jnp.arange(devices, dtype=jnp.int32)
    sums = sums[:, 0, :]
    block_sums = jnp.sum(sums * out_w, 1)
    members = (owner_map[:, None] == images[None, :]).astype(F32)
    totals = total_over(jnp.sum(block_sums[:, None] * members, 0)[None], WHOLE)[0]
    tokens = jnp.sum(
        jnp.where(owners.reshape(-1, 1) == images[None, :], valids.reshape(-1, 1), 0.0), 0
    )
    norm = jnp.sqrt(TAPS * tokens)
    factor = -BT * jax.nn.sigmoid(-totals / norm) / norm
    block_factor = jnp.sum(members * factor[None, :], 1)
    own_factor = jnp.sum(jnp.where(images == me, factor, 0.0)).reshape(1)

    out_part = jnp.sum(sums * block_factor[:, None], 0).reshape(devices, 12)
    out_part = jnp.pad(out_part, ((0, 0), (0, D - 12)))
    parts = pl.pallas_call(
        weight_kernel,
        grid_spec=pltpu.PrefetchScalarGridSpec(
            num_scalar_prefetch=2,
            grid=(local,),
            in_specs=[rows(BT)] * 4 + [fixed((devices, D))],
            out_specs=fixed((devices, ROWS, D)),
            scratch_shapes=[
                pltpu.VMEM((D, 3 * D), F32),
                pltpu.VMEM((D, D), F32),
                pltpu.VMEM((ROWS, D), F32),
            ],
        ),
        out_shape=jax.ShapeDtypeStruct((devices, ROWS, D), BF16),
        compiler_params=params(),
        name="weight_grads",
    )(valid, block_factor, feats[0], low, mid_grad, first_grad, out_part)
    parts = parts.reshape(4, 4, 2, ROWS, D)
    parts = scattered_sum(parts, "dp_2", 2)
    parts = scattered_sum(parts, "dp_0", 0)
    parts = scattered_sum(parts, "dp_1", 0) / (devices * local)

    present = jnp.sum((owners == me).astype(jnp.int32), 1)
    rank = jnp.cumsum(present) - present
    count = jnp.sum(present)
    wanted = jnp.minimum(jnp.arange(capacity, dtype=jnp.int32), count - 1)
    hit = (rank[None, :] == wanted[:, None]) & (present[None, :] > 0)
    source = jnp.sum(jnp.where(hit, images[None, :], 0), 1).astype(jnp.int32)
    placed = pl.pallas_call(
        place_kernel,
        grid_spec=pltpu.PrefetchScalarGridSpec(
            num_scalar_prefetch=3,
            grid=(capacity,),
            in_specs=[pl.BlockSpec((1, BT, D), lambda i, source_ref, *_: (source_ref[i], 0, 0))],
            out_specs=rows(BT),
        ),
        out_shape=jax.ShapeDtypeStruct((capacity * BT, D), BF16),
        compiler_params=params(),
        name="place",
    )(source, count.reshape(1), own_factor, received)

    return (
        placed[None],
        parts[:36].reshape(1, 3, 12, D),
        parts[36:48][None],
        parts[48, :12][None],
    )


def solution(mesh):
    split = Mesh(
        mesh.devices.reshape(4, 4, 2, mesh.shape["head"]), ("dp_0", "dp_1", "dp_2", "head")
    )
    in_specs = (
        P("head", DP, None),
        P(DP),
        P(DP),
        P("head", None, DP, None),
        P("head", DP, None),
        P("head", DP),
    )
    out_specs = (P("head", DP, None), P("head", None, DP, None), P("head", DP, None), P("head", DP))
    return jax.shard_map(
        per_device, mesh=split, in_specs=in_specs, out_specs=out_specs, check_vma=False
    )
```

```python
import jax
import jax.numpy as jnp
from jax import lax
from jax.experimental import pallas as pl
from jax.experimental.pallas import tpu as pltpu
from jax.sharding import Mesh
from jax.sharding import PartitionSpec as P

DP = ("dp_0", "dp_1", "dp_2")
CHIPS = ("dp_0", "dp_1")
BF16 = jnp.bfloat16
F32 = jnp.float32
TAPS = 4
BT = 256
D = 384
SHARD = 12
EXTRA = 4 * SHARD
ROWS = 56
GROUP = 2
VMEM_LIMIT = 20 * 1024 * 1024

IN_VMEM = pl.BlockSpec(memory_space=pltpu.VMEM)
IN_SMEM = pl.BlockSpec(memory_space=pltpu.SMEM)
IN_HBM = pl.BlockSpec(memory_space=pltpu.HBM)
OVER_LAST = (((1,), (1,)), ((), ()))
OVER_ROWS = (((0,), (0,)), ((), ()))


def swapped(x):
    return lax.ppermute(x, "dp_2", [(0, 1), (1, 0)])


def turned(x, axis, shift):
    count = lax.axis_size(axis)
    return lax.ppermute(x, axis, [(i, (i + shift) % count) for i in range(count)])


def total_over(x, axis):
    return sum((turned(x, axis, r) for r in range(1, lax.axis_size(axis))), x)


def scattered_sum(parts, axis, dim):
    count, index = lax.axis_size(axis), lax.axis_index(axis)

    def piece(shift):
        return lax.dynamic_index_in_dim(parts, (index + shift) % count, dim, keepdims=False)

    total = piece(0).astype(F32)
    for r in range(1, count):
        total = total + turned(piece(r).astype(BF16), axis, r).astype(F32)
    return total


def gate(value):
    half = jnp.tanh(0.5 * value)
    act = jnp.maximum(value, 0.2 * value) - 0.8 * jnp.log(0.5 + 0.5 * jnp.abs(half))
    return act, 0.6 + 0.4 * half


def row_mask(valid_ref, first, blocks):
    rows = lax.broadcasted_iota(jnp.int32, (blocks * BT, 1), 0)
    limit = jnp.full_like(rows, valid_ref[first])
    for j in range(1, blocks):
        limit = jnp.where(rows < j * BT, limit, j * BT + valid_ref[first + j])
    return rows < limit


def neighbours(x):
    count = x.shape[0]
    place = lax.broadcasted_iota(jnp.int32, (count, 1), 0) % BT
    before = jnp.where(place == 0, 0.0, pltpu.roll(x, 1, 0))
    after = jnp.where(place == BT - 1, 0.0, pltpu.roll(x, count - 1, 0))
    return before.astype(BF16), after.astype(BF16)


def pack_kernel(valid_ref, owner_ref, conv_ref, mid_ref, out_ref, copies_ref, stage_ref):
    local = valid_ref.shape[0]
    lane = lax.broadcasted_iota(jnp.int32, (1, D), 1)
    extras = jnp.zeros((1, D), F32)
    for j in range(local):
        extras = jnp.where(lane == SHARD + j, owner_ref[j].astype(F32), extras)
        extras = jnp.where(lane == SHARD + local + j, valid_ref[j].astype(F32), extras)
    stage_ref[EXTRA:ROWS, :] = jnp.zeros((ROWS - EXTRA, D), F32)
    for k in range(3):
        stage_ref[SHARD * k : SHARD * (k + 1), :] = conv_ref[k].astype(F32)
    stage_ref[3 * SHARD : EXTRA, :] = mid_ref[...].astype(F32)
    stage_ref[EXTRA : EXTRA + 1, :] = extras
    stage_ref[EXTRA : EXTRA + 1, 0:SHARD] = out_ref[...].astype(F32)
    packed = stage_ref[...].astype(BF16)
    for j in range(copies_ref.shape[0]):
        copies_ref[j] = packed


def forward_kernel(
    valid_ref, core_ref, feats_ref, own_ref, other_ref,
    masked_out, low_out, mid_grad_out, mid_grad_ref, slope_ref, sums_ref, weights_ref, out_w_ref,
    extras_ref, raw_ref, masked_ref, low_ref, wide_ref, sems, out_sems,
):
    local = valid_ref.shape[0]
    copies, departures = [], []

    def send(source, target, rows, sem):
        copy = pltpu.make_async_copy(source.at[rows], target.at[rows], sem)
        copy.start()
        departures.append(copy)

    for j in range(0, local, GROUP):
        rows = pl.ds(j * BT, GROUP * BT)
        copy = pltpu.make_async_copy(feats_ref.at[rows], raw_ref.at[rows], sems.at[j // GROUP])
        copy.start()
        copies.append(copy)

    def unpack(parity, source):
        for chip in range(source.shape[0]):
            tile = source[chip].astype(F32)
            device = 2 * chip + parity
            at = SHARD * device
            for k in range(4):
                wide_ref[k, at : at + SHARD, :] = tile[SHARD * k : SHARD * (k + 1)]
            extras_ref[device : device + 1, :] = tile[EXTRA : EXTRA + 1, :128]

    @pl.when(core_ref[0] == 0)
    def _():
        unpack(0, own_ref)
        unpack(1, other_ref)

    @pl.when(core_ref[0] == 1)
    def _():
        unpack(1, own_ref)
        unpack(0, other_ref)

    weights_ref[...] = wide_ref[...].astype(BF16)
    devices = extras_ref.shape[0]
    column = lax.broadcasted_iota(jnp.int32, (128, D), 1).astype(F32)
    place = lax.broadcasted_iota(jnp.int32, (128, D), 0).astype(F32)
    home = jnp.floor((column + 0.5) * (1.0 / SHARD))
    pick = jnp.where(column - SHARD * home == place, 1.0, 0.0).astype(BF16)
    spread = jnp.dot(extras_ref[...].astype(BF16), pick, preferred_element_type=F32)
    device = lax.broadcasted_iota(jnp.int32, (devices, D), 0).astype(F32)
    out_w = jnp.sum(jnp.where(home[:devices] == device, spread, 0.0), 0, keepdims=True)
    out_w_ref[...] = out_w

    for j in range(0, local, GROUP):
        rows = pl.ds(j * BT, GROUP * BT)
        copies[j // GROUP].wait()
        keep = row_mask(valid_ref, j, GROUP)
        masked = jnp.where(keep, raw_ref[rows, :].astype(F32), 0.0)
        before, after = neighbours(masked)
        masked = masked.astype(BF16)
        masked_ref[rows, :] = masked
        first = jnp.dot(before, weights_ref[0], preferred_element_type=F32)
        first += jnp.dot(masked, weights_ref[1], preferred_element_type=F32)
        first += jnp.dot(after, weights_ref[2], preferred_element_type=F32)
        first_act, slope = gate(first)
        low = first_act.astype(BF16)
        low_ref[rows, :] = low
        slope_ref[rows, :] = slope.astype(BF16)
        second = jnp.dot(low, weights_ref[3], preferred_element_type=F32)
        second_act, second_slope = gate(second)
        mid_grad_ref[rows, :] = jnp.where(keep, out_w * second_slope, 0.0).astype(BF16)
        total = jnp.where(keep, second_act + first_act, 0.0)
        for i in range(GROUP):
            block = jnp.sum(total[i * BT : (i + 1) * BT], 0, keepdims=True)
            sums_ref[j + i : j + i + 1, :] = block
        send(masked_ref, masked_out, rows, out_sems.at[0, j // GROUP])
        send(low_ref, low_out, rows, out_sems.at[1, j // GROUP])
        send(mid_grad_ref, mid_grad_out, rows, out_sems.at[2, j // GROUP])
    for copy in departures:
        copy.wait()


def backward_kernel(
    valid_ref, owner_ref, mid_grad_ref, slope_ref, weights_ref, out_w_ref,
    first_grad_out, slots_ref, first_grad_ref, ready_ref, sems, out_sems,
):
    local = valid_ref.shape[0]
    copies = []
    for j in range(local):
        rows = pl.ds(j * BT, BT)
        keep = row_mask(valid_ref, j, 1)
        grad = lax.dot_general(
            mid_grad_ref[rows, :], weights_ref[3], OVER_LAST, preferred_element_type=F32
        )
        grad = (grad + jnp.where(keep, out_w_ref[...], 0.0)) * slope_ref[rows, :].astype(F32)
        before, after = neighbours(grad)
        low = grad.astype(BF16)
        first_grad_ref[rows, :] = low
        copy = pltpu.make_async_copy(
            first_grad_ref.at[rows], first_grad_out.at[rows], out_sems.at[j]
        )
        copy.start()
        copies.append(copy)
        total = lax.dot_general(low, weights_ref[1], OVER_LAST, preferred_element_type=F32)
        total += lax.dot_general(after, weights_ref[0], OVER_LAST, preferred_element_type=F32)
        total += lax.dot_general(before, weights_ref[2], OVER_LAST, preferred_element_type=F32)
        ready_ref[j] = jnp.where(keep, total, 0.0).astype(BF16)
        copy = pltpu.make_async_copy(ready_ref.at[j], slots_ref.at[owner_ref[j]], sems.at[j])
        copy.start()
        copies.append(copy)
    for copy in copies:
        copy.wait()


def weight_kernel(
    factor_ref, masked_ref, low_ref, mid_grad_ref, first_grad_ref, sums_ref,
    parts_ref, conv_ref, mid_ref, stage_ref,
):
    local = factor_ref.shape[0]
    out = jnp.zeros((1, D), F32)
    for j in range(local):
        rows = pl.ds(j * BT, BT)
        factor = factor_ref[j]
        out += sums_ref[j : j + 1, :] * factor
        grad = first_grad_ref[rows, :].astype(F32) * factor
        before, after = neighbours(grad)
        mid_grad = (mid_grad_ref[rows, :].astype(F32) * factor).astype(BF16)
        masked = masked_ref[rows, :]
        terms = [
            lax.dot_general(masked, x, OVER_ROWS, preferred_element_type=F32)
            for x in (after, grad.astype(BF16), before)
        ]
        mid = lax.dot_general(low_ref[rows, :], mid_grad, OVER_ROWS, preferred_element_type=F32)
        for k in range(3):
            conv_ref[k] = terms[k] if j == 0 else conv_ref[k] + terms[k]
        mid_ref[...] = mid if j == 0 else mid_ref[...] + mid

    devices = parts_ref.shape[0]
    column = lax.broadcasted_iota(jnp.int32, (D, D), 0).astype(F32)
    place = lax.broadcasted_iota(jnp.int32, (D, D), 1).astype(F32)
    home = jnp.floor((column + 0.5) * (1.0 / SHARD))
    pick = jnp.where(column - SHARD * home == place, 1.0, 0.0).astype(BF16)
    device = lax.broadcasted_iota(jnp.int32, (devices, D), 0).astype(F32)
    lane = lax.broadcasted_iota(jnp.int32, (devices, D), 1).astype(F32)
    mine = jnp.floor((lane + 0.5) * (1.0 / SHARD)) == device
    out_rows = jnp.where(mine, out, 0.0).astype(BF16)
    out_rows = jnp.dot(out_rows, pick, preferred_element_type=F32)
    stage_ref[EXTRA:ROWS, :] = jnp.zeros((ROWS - EXTRA, D), F32)
    for d in range(devices):
        at = SHARD * d
        for k in range(3):
            stage_ref[SHARD * k : SHARD * (k + 1), :] = conv_ref[k, at : at + SHARD, :]
        stage_ref[3 * SHARD : EXTRA, :] = mid_ref[at : at + SHARD, :]
        stage_ref[EXTRA : EXTRA + 1, :] = out_rows[d : d + 1, :]
        parts_ref[d] = stage_ref[...].astype(BF16)


def place_kernel(
    source_ref, count_ref, factor_ref, received_ref, placed_ref, raw_ref, ready_ref, in_sems, out_sems
):
    capacity = source_ref.shape[0]
    arrivals, departures = [], []
    for slot in range(capacity):
        copy = pltpu.make_async_copy(
            received_ref.at[source_ref[slot]], raw_ref.at[slot], in_sems.at[slot]
        )
        copy.start()
        arrivals.append(copy)
    for slot in range(capacity):
        arrivals[slot].wait()
        factor = jnp.where(slot < count_ref[0], factor_ref[0], 0.0)
        ready_ref[slot] = (raw_ref[slot].astype(F32) * factor).astype(BF16)
        copy = pltpu.make_async_copy(
            ready_ref.at[slot], placed_ref.at[pl.ds(slot * BT, BT)], out_sems.at[slot]
        )
        copy.start()
        departures.append(copy)
    for copy in departures:
        copy.wait()


def in_hbm(x):
    return pltpu.with_memory_space_constraint(x, pltpu.HBM)


def in_vmem(x):
    return pltpu.with_memory_space_constraint(x, pltpu.VMEM)


def call(kernel, name, in_specs, outs, scratch=()):
    return pl.pallas_call(
        kernel,
        in_specs=in_specs,
        out_specs=[spec for spec, _, _ in outs],
        out_shape=[
            (pltpu.HBM if spec is IN_HBM else pltpu.VMEM)(shape, dtype) for spec, shape, dtype in outs
        ],
        scratch_shapes=list(scratch),
        compiler_params=pltpu.CompilerParams(vmem_limit_bytes=VMEM_LIMIT),
        name=name,
    )


def per_device(feats, valid, owner_map, w_conv, w_mid, w_out):
    local = owner_map.shape[0]
    devices = lax.axis_size(DP)
    chips = devices // 2
    capacity = devices // 2
    tokens_here = local * BT
    me = lax.axis_index(DP)
    core = lax.axis_index("dp_2").astype(jnp.int32).reshape(1)
    images = jnp.arange(devices, dtype=jnp.int32)

    (copies,) = call(
        pack_kernel,
        "pack",
        [IN_SMEM, IN_SMEM, IN_VMEM, IN_VMEM, IN_VMEM],
        [(IN_VMEM, (chips, ROWS, D), BF16)],
        [pltpu.VMEM((ROWS, D), F32)],
    )(valid, owner_map, w_conv[0], w_mid[0], w_out)
    own = lax.all_to_all(copies, CHIPS, split_axis=0, concat_axis=0, tiled=True)
    other = swapped(own)

    here = (IN_VMEM, (tokens_here, D), BF16)
    later = (IN_HBM, (tokens_here, D), BF16)
    masked, low, mid_grad, mid_grad_here, slope, sums, weights, out_w, extras = call(
        forward_kernel,
        "forward",
        [IN_SMEM, IN_SMEM, IN_HBM, IN_VMEM, IN_VMEM],
        [
            later,
            later,
            later,
            here,
            here,
            (IN_VMEM, (local, D), F32),
            (IN_VMEM, (4, D, D), BF16),
            (IN_VMEM, (1, D), F32),
            (IN_VMEM, (devices, 128), F32),
        ],
        [
            pltpu.VMEM((tokens_here, D), BF16),
            pltpu.VMEM((tokens_here, D), BF16),
            pltpu.VMEM((tokens_here, D), BF16),
            pltpu.VMEM((4, D, D), F32),
            pltpu.SemaphoreType.DMA((local // GROUP,)),
            pltpu.SemaphoreType.DMA((3, local // GROUP)),
        ],
    )(valid, core, in_hbm(feats[0]), in_vmem(own), in_vmem(other))

    members = (owner_map[:, None] == images[None, :]).astype(F32)
    block_sums = jnp.sum(sums * out_w, 1)
    totals = jnp.sum(block_sums[:, None] * members, 0)
    totals = jnp.broadcast_to(totals[None, None, :], (devices, 1, devices))
    totals = lax.all_to_all(totals, DP, split_axis=0, concat_axis=0, tiled=True)

    first_grad, slots = call(
        backward_kernel,
        "backward",
        [IN_SMEM, IN_SMEM, IN_VMEM, IN_VMEM, IN_VMEM, IN_VMEM],
        [later, (IN_HBM, (devices, BT, D), BF16)],
        [
            pltpu.VMEM((tokens_here, D), BF16),
            pltpu.VMEM((local, BT, D), BF16),
            pltpu.SemaphoreType.DMA((local,)),
            pltpu.SemaphoreType.DMA((local,)),
        ],
    )(valid, owner_map, in_vmem(mid_grad_here), in_vmem(slope), in_vmem(weights), out_w)

    slots, totals = lax.optimization_barrier((slots, totals))
    received = lax.all_to_all(slots, DP, split_axis=0, concat_axis=0, tiled=True)

    totals = total_over(jnp.sum(totals[:, 0, :], 0)[None], "head")[0]
    owners = extras[:, SHARD : SHARD + local].astype(jnp.int32)
    valids = extras[:, SHARD + local : SHARD + 2 * local]
    tokens = jnp.sum(jnp.where(owners[:, :, None] == images, valids[:, :, None], 0.0), (0, 1))
    norm = jnp.sqrt(TAPS * tokens)
    factor = -BT * jax.nn.sigmoid(-totals / norm) / norm
    block_factor = jnp.sum(members * factor[None, :], 1)
    own_factor = jnp.sum(jnp.where(images == me, factor, 0.0)).reshape(1)

    (parts,) = call(
        weight_kernel,
        "weight_grads",
        [IN_SMEM, IN_VMEM, IN_VMEM, IN_VMEM, IN_VMEM, IN_VMEM],
        [(IN_VMEM, (devices, ROWS, D), BF16)],
        [pltpu.VMEM((3, D, D), F32), pltpu.VMEM((D, D), F32), pltpu.VMEM((ROWS, D), F32)],
    )(block_factor, masked, low, mid_grad, first_grad, sums)
    parts = parts.reshape(4, 4, 2, ROWS, D)
    parts = scattered_sum(parts, "dp_2", 2)
    parts = scattered_sum(parts, "dp_0", 0)
    parts = scattered_sum(parts, "dp_1", 0) / (devices * local)

    present = jnp.sum((owners == me).astype(jnp.int32), 1)
    rank = jnp.sum(jnp.where(images[None, :] < images[:, None], present[None, :], 0), 1)
    count = jnp.sum(present)
    wanted = jnp.minimum(jnp.arange(capacity, dtype=jnp.int32), count - 1)
    hit = (rank[None, :] == wanted[:, None]) & (present[None, :] > 0)
    source = jnp.sum(jnp.where(hit, images[None, :], 0), 1).astype(jnp.int32)
    (placed,) = call(
        place_kernel,
        "place",
        [IN_SMEM, IN_SMEM, IN_SMEM, IN_HBM],
        [(IN_HBM, (capacity * BT, D), BF16)],
        [
            pltpu.VMEM((capacity, BT, D), BF16),
            pltpu.VMEM((capacity, BT, D), BF16),
            pltpu.SemaphoreType.DMA((capacity,)),
            pltpu.SemaphoreType.DMA((capacity,)),
        ],
    )(source, count.reshape(1), own_factor, received)

    return (
        placed[None],
        parts[: 3 * SHARD].reshape(1, 3, SHARD, D),
        parts[3 * SHARD : EXTRA][None],
        parts[EXTRA, :SHARD][None],
    )


def solution(mesh):
    split = Mesh(
        mesh.devices.reshape(4, 4, 2, mesh.shape["head"]), ("dp_0", "dp_1", "dp_2", "head")
    )
    in_specs = (
        P("head", DP, None),
        P(DP),
        P(DP),
        P("head", None, DP, None),
        P("head", DP, None),
        P("head", DP),
    )
    out_specs = (P("head", DP, None), P("head", None, DP, None), P("head", DP, None), P("head", DP))
    return jax.shard_map(
        per_device, mesh=split, in_specs=in_specs, out_specs=out_specs, check_vma=False
    )
```

```python
import jax
import jax.numpy as jnp
from jax import lax
from jax.experimental import pallas as pl
from jax.experimental.pallas import tpu as pltpu
from jax.sharding import Mesh
from jax.sharding import PartitionSpec as P

DP = ("dp_0", "dp_1", "dp_2")
CHIPS = ("dp_0", "dp_1")
BF16 = jnp.bfloat16
F32 = jnp.float32
TAPS = 4
BT = 256
D = 384
SHARD = 12
EXTRA = 4 * SHARD
ROWS = 56
GROUP = 2
VMEM_LIMIT = 20 * 1024 * 1024

IN_VMEM = pl.BlockSpec(memory_space=pltpu.VMEM)
IN_SMEM = pl.BlockSpec(memory_space=pltpu.SMEM)
IN_HBM = pl.BlockSpec(memory_space=pltpu.HBM)
OVER_LAST = (((1,), (1,)), ((), ()))
OVER_ROWS = (((0,), (0,)), ((), ()))


def swapped(x):
    return lax.ppermute(x, "dp_2", [(0, 1), (1, 0)])


def turned(x, axis, shift):
    count = lax.axis_size(axis)
    return lax.ppermute(x, axis, [(i, (i + shift) % count) for i in range(count)])


def total_over(x, axis):
    return sum((turned(x, axis, r) for r in range(1, lax.axis_size(axis))), x)


def scattered(parts, axis, dim):
    count, index = lax.axis_size(axis), lax.axis_index(axis)

    def piece(shift):
        return lax.dynamic_index_in_dim(parts, (index + shift) % count, dim, keepdims=False)

    return [piece(0)] + [turned(piece(r).astype(BF16), axis, r) for r in range(1, count)]


def scattered_sum(parts, axis, dim):
    return sum(piece.astype(F32) for piece in scattered(parts, axis, dim))


def gate(value):
    half = jnp.tanh(0.5 * value)
    act = jnp.maximum(value, 0.2 * value) - 0.8 * jnp.log(0.5 + 0.5 * jnp.abs(half))
    return act, 0.6 + 0.4 * half


def row_mask(valid_ref, first, blocks):
    rows = lax.broadcasted_iota(jnp.int32, (blocks * BT, 1), 0)
    limit = jnp.full_like(rows, valid_ref[first])
    for j in range(1, blocks):
        limit = jnp.where(rows < j * BT, limit, j * BT + valid_ref[first + j])
    return rows < limit


def neighbours(x):
    count = x.shape[0]
    place = lax.broadcasted_iota(jnp.int32, (count, 1), 0) % BT
    before = jnp.where(place == 0, 0.0, pltpu.roll(x, 1, 0))
    after = jnp.where(place == BT - 1, 0.0, pltpu.roll(x, count - 1, 0))
    return before.astype(BF16), after.astype(BF16)


def pack_kernel(
    valid_hbm, owner_hbm, conv_hbm, mid_hbm, out_hbm,
    copies_ref, valid_ref, owner_ref, conv_ref, mid_ref, out_ref, stage_ref, sems,
):
    sources = (valid_hbm, owner_hbm, conv_hbm, mid_hbm, out_hbm)
    targets = (valid_ref, owner_ref, conv_ref, mid_ref, out_ref)
    arrivals = [
        pltpu.make_async_copy(source, target, sems.at[i])
        for i, (source, target) in enumerate(zip(sources, targets))
    ]
    for copy in arrivals:
        copy.start()
    for copy in arrivals:
        copy.wait()
    local = valid_ref.shape[0]
    lane = lax.broadcasted_iota(jnp.int32, (1, D), 1)
    extras = jnp.zeros((1, D), F32)
    for j in range(local):
        extras = jnp.where(lane == SHARD + j, owner_ref[j].astype(F32), extras)
        extras = jnp.where(lane == SHARD + local + j, valid_ref[j].astype(F32), extras)
    stage_ref[EXTRA:ROWS, :] = jnp.zeros((ROWS - EXTRA, D), F32)
    for k in range(3):
        stage_ref[SHARD * k : SHARD * (k + 1), :] = conv_ref[k].astype(F32)
    stage_ref[3 * SHARD : EXTRA, :] = mid_ref[...].astype(F32)
    stage_ref[EXTRA : EXTRA + 1, :] = extras
    stage_ref[EXTRA : EXTRA + 1, 0:SHARD] = out_ref[...].astype(F32)
    packed = stage_ref[...].astype(BF16)
    for j in range(copies_ref.shape[0]):
        copies_ref[j] = packed


def forward_kernel(
    valid_ref, owner_ref, core_ref, feats_ref, own_hbm, other_ref,
    masked_out, low_out, mid_grad_out, weights_out, state_ref, sums_ref, out_w_ref,
    extras_ref, totals_ref, raw_ref, weights_ref, own_ref, masked_ref, low_ref, wide_ref,
    sems, out_sems, weight_sems,
):
    local = valid_ref.shape[0]
    copies, departures = [], []
    mid_grad_ref, slope_ref = state_ref.at[0], state_ref.at[1]
    arrival = pltpu.make_async_copy(own_hbm, own_ref, weight_sems.at[0])
    arrival.start()

    def send(source, target, rows, sem):
        copy = pltpu.make_async_copy(source.at[rows], target.at[rows], sem)
        copy.start()
        departures.append(copy)

    for j in range(0, local, GROUP):
        rows = pl.ds(j * BT, GROUP * BT)
        copy = pltpu.make_async_copy(feats_ref.at[rows], raw_ref.at[rows], sems.at[j // GROUP])
        copy.start()
        copies.append(copy)

    def unpack(parity, source):
        for chip in range(source.shape[0]):
            tile = source[chip].astype(F32)
            device = 2 * chip + parity
            at = SHARD * device
            for k in range(4):
                wide_ref[k, at : at + SHARD, :] = tile[SHARD * k : SHARD * (k + 1)]
            extras_ref[device : device + 1, :] = tile[EXTRA : EXTRA + 1, :128]

    arrival.wait()

    @pl.when(core_ref[0] == 0)
    def _():
        unpack(0, own_ref)
        unpack(1, other_ref)

    @pl.when(core_ref[0] == 1)
    def _():
        unpack(1, own_ref)
        unpack(0, other_ref)

    weights_ref[...] = wide_ref[...].astype(BF16)
    copy = pltpu.make_async_copy(weights_ref, weights_out, weight_sems.at[1])
    copy.start()
    departures.append(copy)
    devices = extras_ref.shape[0]
    column = lax.broadcasted_iota(jnp.int32, (128, D), 1).astype(F32)
    place = lax.broadcasted_iota(jnp.int32, (128, D), 0).astype(F32)
    home = jnp.floor((column + 0.5) * (1.0 / SHARD))
    pick = jnp.where(column - SHARD * home == place, 1.0, 0.0).astype(BF16)
    spread = jnp.dot(extras_ref[...].astype(BF16), pick, preferred_element_type=F32)
    row = lax.broadcasted_iota(jnp.int32, (devices, D), 0).astype(F32)
    out_w = jnp.sum(jnp.where(home[:devices] == row, spread, 0.0), 0, keepdims=True)
    out_w_ref[...] = out_w

    lane = lax.broadcasted_iota(jnp.int32, (1, 128), 1)
    totals = jnp.zeros((1, 128), F32)
    for j in range(0, local, GROUP):
        rows = pl.ds(j * BT, GROUP * BT)
        copies[j // GROUP].wait()
        keep = row_mask(valid_ref, j, GROUP)
        masked = jnp.where(keep, raw_ref[rows, :].astype(F32), 0.0)
        before, after = neighbours(masked)
        masked = masked.astype(BF16)
        masked_ref[rows, :] = masked
        first = jnp.dot(before, weights_ref[0], preferred_element_type=F32)
        first += jnp.dot(masked, weights_ref[1], preferred_element_type=F32)
        first += jnp.dot(after, weights_ref[2], preferred_element_type=F32)
        first_act, slope = gate(first)
        low = first_act.astype(BF16)
        low_ref[rows, :] = low
        slope_ref[rows, :] = slope.astype(BF16)
        second = jnp.dot(low, weights_ref[3], preferred_element_type=F32)
        second_act, second_slope = gate(second)
        mid_grad_ref[rows, :] = jnp.where(keep, out_w * second_slope, 0.0).astype(BF16)
        total = jnp.where(keep, second_act + first_act, 0.0)
        for i in range(GROUP):
            block = jnp.sum(total[i * BT : (i + 1) * BT], 0, keepdims=True)
            sums_ref[j + i : j + i + 1, :] = block
            block_sum = jnp.sum(block * out_w, 1, keepdims=True)
            totals += jnp.where(lane == owner_ref[j + i], block_sum, 0.0)
        send(masked_ref, masked_out, rows, out_sems.at[0, j // GROUP])
        send(low_ref, low_out, rows, out_sems.at[1, j // GROUP])
        send(mid_grad_ref, mid_grad_out, rows, out_sems.at[2, j // GROUP])
    for device in range(devices):
        totals_ref[device] = totals
    for copy in departures:
        copy.wait()


def backward_kernel(
    valid_ref, owner_ref, state_ref, weights_hbm, out_w_ref,
    first_grad_out, slots_ref, weights_ref, first_grad_ref, ready_ref, sems, out_sems, weight_sems,
):
    local = valid_ref.shape[0]
    arrivals = {}
    for k in (3, 1, 0, 2):
        arrivals[k] = pltpu.make_async_copy(
            weights_hbm.at[k], weights_ref.at[k], weight_sems.at[k]
        )
        arrivals[k].start()
    mid_grad_ref, slope_ref = state_ref.at[0], state_ref.at[1]
    copies = []
    for j in range(local):
        rows = pl.ds(j * BT, BT)
        keep = row_mask(valid_ref, j, 1)
        if j == 0:
            arrivals[3].wait()
        grad = lax.dot_general(
            mid_grad_ref[rows, :], weights_ref[3], OVER_LAST, preferred_element_type=F32
        )
        grad = (grad + jnp.where(keep, out_w_ref[...], 0.0)) * slope_ref[rows, :].astype(F32)
        before, after = neighbours(grad)
        low = grad.astype(BF16)
        first_grad_ref[rows, :] = low
        copy = pltpu.make_async_copy(
            first_grad_ref.at[rows], first_grad_out.at[rows], out_sems.at[j]
        )
        copy.start()
        copies.append(copy)
        if j == 0:
            for k in (1, 0, 2):
                arrivals[k].wait()
        total = lax.dot_general(low, weights_ref[1], OVER_LAST, preferred_element_type=F32)
        total += lax.dot_general(after, weights_ref[0], OVER_LAST, preferred_element_type=F32)
        total += lax.dot_general(before, weights_ref[2], OVER_LAST, preferred_element_type=F32)
        ready_ref[j] = jnp.where(keep, total, 0.0).astype(BF16)
        copy = pltpu.make_async_copy(ready_ref.at[j], slots_ref.at[owner_ref[j]], sems.at[j])
        copy.start()
        copies.append(copy)
    for copy in copies:
        copy.wait()


def weight_kernel(
    factor_ref, masked_ref, low_ref, mid_grad_ref, first_grad_ref, sums_ref,
    parts_ref, conv_ref, mid_ref, stage_ref,
):
    local = factor_ref.shape[0]
    out = jnp.zeros((1, D), F32)
    for j in range(local):
        rows = pl.ds(j * BT, BT)
        factor = factor_ref[j]
        out += sums_ref[j : j + 1, :] * factor
        grad = first_grad_ref[rows, :].astype(F32) * factor
        before, after = neighbours(grad)
        mid_grad = (mid_grad_ref[rows, :].astype(F32) * factor).astype(BF16)
        masked = masked_ref[rows, :]
        terms = [
            lax.dot_general(masked, x, OVER_ROWS, preferred_element_type=F32)
            for x in (after, grad.astype(BF16), before)
        ]
        mid = lax.dot_general(low_ref[rows, :], mid_grad, OVER_ROWS, preferred_element_type=F32)
        for k in range(3):
            conv_ref[k] = terms[k] if j == 0 else conv_ref[k] + terms[k]
        mid_ref[...] = mid if j == 0 else mid_ref[...] + mid

    devices = parts_ref.shape[0]
    column = lax.broadcasted_iota(jnp.int32, (D, D), 0).astype(F32)
    place = lax.broadcasted_iota(jnp.int32, (D, D), 1).astype(F32)
    home = jnp.floor((column + 0.5) * (1.0 / SHARD))
    pick = jnp.where(column - SHARD * home == place, 1.0, 0.0).astype(BF16)
    device = lax.broadcasted_iota(jnp.int32, (devices, D), 0).astype(F32)
    lane = lax.broadcasted_iota(jnp.int32, (devices, D), 1).astype(F32)
    mine = jnp.floor((lane + 0.5) * (1.0 / SHARD)) == device
    out_rows = jnp.where(mine, out, 0.0).astype(BF16)
    out_rows = jnp.dot(out_rows, pick, preferred_element_type=F32)
    stage_ref[EXTRA:ROWS, :] = jnp.zeros((ROWS - EXTRA, D), F32)
    for d in range(devices):
        at = SHARD * d
        for k in range(3):
            stage_ref[SHARD * k : SHARD * (k + 1), :] = conv_ref[k, at : at + SHARD, :]
        stage_ref[3 * SHARD : EXTRA, :] = mid_ref[at : at + SHARD, :]
        stage_ref[EXTRA : EXTRA + 1, :] = out_rows[d : d + 1, :]
        parts_ref[d] = stage_ref[...].astype(BF16)


def finish_kernel(own_ref, first_ref, second_ref, third_ref, conv_ref, mid_ref, out_ref, total_ref):
    total = own_ref[...]
    for piece in (first_ref, second_ref, third_ref):
        total += piece[...].astype(F32)
    total_ref[...] = total * (1.0 / BT)
    for row in range(3 * SHARD):
        conv_ref[row] = total_ref[row : row + 1, :]
    for row in range(SHARD):
        mid_ref[row] = total_ref[3 * SHARD + row : 3 * SHARD + row + 1, :]
    out_ref[...] = total_ref[EXTRA : EXTRA + 1, 0:SHARD]


def place_kernel(
    source_ref, count_ref, factor_ref, received_ref, placed_ref, raw_ref, ready_ref, in_sems, out_sems
):
    capacity = source_ref.shape[0]
    arrivals, departures = [], []
    for slot in range(capacity):
        copy = pltpu.make_async_copy(
            received_ref.at[source_ref[slot]], raw_ref.at[slot], in_sems.at[slot]
        )
        copy.start()
        arrivals.append(copy)
    for slot in range(capacity):
        arrivals[slot].wait()
        factor = jnp.where(slot < count_ref[0], factor_ref[0], 0.0)
        ready_ref[slot] = (raw_ref[slot].astype(F32) * factor).astype(BF16)
        copy = pltpu.make_async_copy(
            ready_ref.at[slot], placed_ref.at[pl.ds(slot * BT, BT)], out_sems.at[slot]
        )
        copy.start()
        departures.append(copy)
    for copy in departures:
        copy.wait()


def in_hbm(x):
    return pltpu.with_memory_space_constraint(x, pltpu.HBM)


def in_vmem(x):
    return pltpu.with_memory_space_constraint(x, pltpu.VMEM)


def call(kernel, name, in_specs, outs, scratch=(), megabytes=0):
    return pl.pallas_call(
        kernel,
        in_specs=in_specs,
        out_specs=[spec for spec, _, _ in outs],
        out_shape=[
            (pltpu.HBM if spec is IN_HBM else pltpu.VMEM)(shape, dtype) for spec, shape, dtype in outs
        ],
        scratch_shapes=list(scratch),
        compiler_params=pltpu.CompilerParams(vmem_limit_bytes=VMEM_LIMIT),
        cost_estimate=pl.CostEstimate(
            flops=0, transcendentals=0, bytes_accessed=megabytes * 1024 * 1024
        ),
        name=name,
    )


def per_device(feats, valid, owner_map, w_conv, w_mid, w_out):
    local = owner_map.shape[0]
    devices = lax.axis_size(DP)
    chips = devices // 2
    capacity = devices // 2
    tokens_here = local * BT
    me = lax.axis_index(DP)
    core = lax.axis_index("dp_2").astype(jnp.int32).reshape(1)
    images = jnp.arange(devices, dtype=jnp.int32)

    (copies,) = call(
        pack_kernel,
        "pack",
        [IN_HBM] * 5,
        [(IN_VMEM, (chips, ROWS, D), BF16)],
        [
            pltpu.SMEM((local,), jnp.int32),
            pltpu.SMEM((local,), jnp.int32),
            pltpu.VMEM((3, SHARD, D), BF16),
            pltpu.VMEM((SHARD, D), BF16),
            pltpu.VMEM((1, SHARD), BF16),
            pltpu.VMEM((ROWS, D), F32),
            pltpu.SemaphoreType.DMA((5,)),
        ],
    )(*(in_hbm(x) for x in (valid, owner_map, w_conv[0], w_mid[0], w_out)))
    own = lax.all_to_all(copies, CHIPS, split_axis=0, concat_axis=0, tiled=True)
    other = swapped(own)

    later = (IN_HBM, (tokens_here, D), BF16)
    masked, low, mid_grad, weights, state, sums, out_w, extras, totals = call(
        forward_kernel,
        "forward",
        [IN_SMEM, IN_SMEM, IN_SMEM, IN_HBM, IN_HBM, IN_VMEM],
        [
            later,
            later,
            later,
            (IN_HBM, (4, D, D), BF16),
            (IN_VMEM, (2, tokens_here, D), BF16),
            (IN_VMEM, (local, D), F32),
            (IN_VMEM, (1, D), F32),
            (IN_VMEM, (devices, 128), F32),
            (IN_VMEM, (devices, 1, 128), F32),
        ],
        [
            pltpu.VMEM((tokens_here, D), BF16),
            pltpu.VMEM((4, D, D), BF16),
            pltpu.VMEM((chips, ROWS, D), BF16),
            pltpu.VMEM((tokens_here, D), BF16),
            pltpu.VMEM((tokens_here, D), BF16),
            pltpu.VMEM((4, D, D), F32),
            pltpu.SemaphoreType.DMA((local // GROUP,)),
            pltpu.SemaphoreType.DMA((3, local // GROUP)),
            pltpu.SemaphoreType.DMA((2,)),
        ],
    )(valid, owner_map, core, in_hbm(feats[0]), in_hbm(own), in_vmem(other))

    totals = lax.all_to_all(totals, DP, split_axis=0, concat_axis=0, tiled=True)

    first_grad, slots = call(
        backward_kernel,
        "backward",
        [IN_SMEM, IN_SMEM, IN_VMEM, IN_HBM, IN_VMEM],
        [later, (IN_HBM, (devices, BT, D), BF16)],
        [
            pltpu.VMEM((4, D, D), BF16),
            pltpu.VMEM((tokens_here, D), BF16),
            pltpu.VMEM((local, BT, D), BF16),
            pltpu.SemaphoreType.DMA((local,)),
            pltpu.SemaphoreType.DMA((local,)),
            pltpu.SemaphoreType.DMA((4,)),
        ],
        megabytes=24,
    )(valid, owner_map, in_vmem(state), in_hbm(weights), in_vmem(out_w))

    slots, totals = lax.optimization_barrier((slots, totals))
    received = lax.all_to_all(slots, DP, split_axis=0, concat_axis=0, tiled=True)

    totals = total_over(jnp.sum(totals[:, 0, :devices], 0)[None], "head")[0]
    members = (owner_map[:, None] == images[None, :]).astype(F32)
    owners = extras[:, SHARD : SHARD + local].astype(jnp.int32)
    valids = extras[:, SHARD + local : SHARD + 2 * local]
    tokens = jnp.sum(jnp.where(owners[:, :, None] == images, valids[:, :, None], 0.0), (0, 1))
    norm = jnp.sqrt(TAPS * tokens)
    factor = -BT * jax.nn.sigmoid(-totals / norm) / norm
    block_factor = jnp.sum(members * factor[None, :], 1)
    own_factor = jnp.sum(jnp.where(images == me, factor, 0.0)).reshape(1)

    (parts,) = call(
        weight_kernel,
        "weight_grads",
        [IN_SMEM, IN_VMEM, IN_VMEM, IN_VMEM, IN_VMEM, IN_VMEM],
        [(IN_VMEM, (devices, ROWS, D), BF16)],
        [pltpu.VMEM((3, D, D), F32), pltpu.VMEM((D, D), F32), pltpu.VMEM((ROWS, D), F32)],
        megabytes=16,
    )(block_factor, masked, low, mid_grad, first_grad, sums)
    parts = parts.reshape(4, 4, 2, ROWS, D)
    parts = scattered_sum(parts, "dp_2", 2)
    parts = scattered_sum(parts, "dp_0", 0)
    parts, received = lax.optimization_barrier((parts, received))
    pieces = scattered(parts, "dp_1", 0)

    present = jnp.sum((owners == me).astype(jnp.int32), 1)
    rank = jnp.sum(jnp.where(images[None, :] < images[:, None], present[None, :], 0), 1)
    count = jnp.sum(present)
    wanted = jnp.minimum(jnp.arange(capacity, dtype=jnp.int32), count - 1)
    hit = (rank[None, :] == wanted[:, None]) & (present[None, :] > 0)
    source = jnp.sum(jnp.where(hit, images[None, :], 0), 1).astype(jnp.int32)
    (placed,) = call(
        place_kernel,
        "place",
        [IN_SMEM, IN_SMEM, IN_SMEM, IN_HBM],
        [(IN_HBM, (capacity * BT, D), BF16)],
        [
            pltpu.VMEM((capacity, BT, D), BF16),
            pltpu.VMEM((capacity, BT, D), BF16),
            pltpu.SemaphoreType.DMA((capacity,)),
            pltpu.SemaphoreType.DMA((capacity,)),
        ],
        megabytes=24,
    )(source, count.reshape(1), own_factor, received)

    conv, mid, out = pl.pallas_call(
        finish_kernel,
        in_specs=[IN_VMEM] * 4,
        out_specs=[IN_VMEM] * 3,
        out_shape=[
            jax.ShapeDtypeStruct((3 * SHARD, 1, D), F32),
            jax.ShapeDtypeStruct((SHARD, 1, D), F32),
            jax.ShapeDtypeStruct((1, SHARD), F32),
        ],
        scratch_shapes=[pltpu.VMEM((ROWS, D), F32)],
        name="finish",
    )(*(in_vmem(x) for x in pieces))
    return placed[None], conv.reshape(1, 3, SHARD, D), mid.reshape(1, SHARD, D), out


def solution(mesh):
    split = Mesh(
        mesh.devices.reshape(4, 4, 2, mesh.shape["head"]), ("dp_0", "dp_1", "dp_2", "head")
    )
    in_specs = (
        P("head", DP, None),
        P(DP),
        P(DP),
        P("head", None, DP, None),
        P("head", DP, None),
        P("head", DP),
    )
    out_specs = (P("head", DP, None), P("head", None, DP, None), P("head", DP, None), P("head", DP))
    return jax.shard_map(
        per_device, mesh=split, in_specs=in_specs, out_specs=out_specs, check_vma=False
    )
```

```python
import jax
import jax.numpy as jnp
from jax import lax
from jax.experimental import pallas as pl
from jax.experimental.pallas import tpu as pltpu
from jax.sharding import Mesh
from jax.sharding import PartitionSpec as P

DP = ("dp_0", "dp_1", "dp_2")
CHIPS = ("dp_0", "dp_1")
BF16 = jnp.bfloat16
F32 = jnp.float32
TAPS = 4
BT = 256
D = 384
SHARD = 12
EXTRA = 4 * SHARD
ROWS = 56
GROUP = 2
VMEM_LIMIT = 20 * 1024 * 1024

IN_VMEM = pl.BlockSpec(memory_space=pltpu.VMEM)
IN_SMEM = pl.BlockSpec(memory_space=pltpu.SMEM)
IN_HBM = pl.BlockSpec(memory_space=pltpu.HBM)
OVER_LAST = (((1,), (1,)), ((), ()))
OVER_ROWS = (((0,), (0,)), ((), ()))


def swapped(x):
    return lax.ppermute(x, "dp_2", [(0, 1), (1, 0)])


def turned(x, axis, shift):
    count = lax.axis_size(axis)
    return lax.ppermute(x, axis, [(i, (i + shift) % count) for i in range(count)])


def total_over(x, axis):
    return sum((turned(x, axis, r) for r in range(1, lax.axis_size(axis))), x)


def scattered(parts, axis, dim):
    count, index = lax.axis_size(axis), lax.axis_index(axis)

    def piece(shift):
        return lax.dynamic_index_in_dim(parts, (index + shift) % count, dim, keepdims=False)

    return [piece(0)] + [turned(piece(r).astype(BF16), axis, r) for r in range(1, count)]


def scattered_sum(parts, axis, dim):
    return sum(piece.astype(F32) for piece in scattered(parts, axis, dim))


def gate(value):
    half = jnp.tanh(0.5 * value)
    act = jnp.maximum(value, 0.2 * value) - 0.8 * jnp.log(0.5 + 0.5 * jnp.abs(half))
    return act, 0.6 + 0.4 * half


def row_mask(valid_ref, first, blocks):
    rows = lax.broadcasted_iota(jnp.int32, (blocks * BT, 1), 0)
    limit = jnp.full_like(rows, valid_ref[first])
    for j in range(1, blocks):
        limit = jnp.where(rows < j * BT, limit, j * BT + valid_ref[first + j])
    return rows < limit


def neighbours(x, place, last):
    count = x.shape[0]
    before = jnp.where(place == 0, 0.0, pltpu.roll(x, 1, 0))
    after = jnp.where(place == last, 0.0, pltpu.roll(x, count - 1, 0))
    return before.astype(BF16), after.astype(BF16)


def block_place(count):
    return lax.broadcasted_iota(jnp.int32, (count, 1), 0) % BT


def pack_kernel(
    valid_hbm, owner_hbm, conv_hbm, mid_hbm, out_hbm,
    copies_ref, valid_ref, owner_ref, conv_ref, mid_ref, out_ref, stage_ref, sems,
):
    sources = (valid_hbm, owner_hbm, conv_hbm, mid_hbm, out_hbm)
    targets = (valid_ref, owner_ref, conv_ref, mid_ref, out_ref)
    arrivals = [
        pltpu.make_async_copy(source, target, sems.at[i])
        for i, (source, target) in enumerate(zip(sources, targets))
    ]
    for copy in arrivals:
        copy.start()
    for copy in arrivals:
        copy.wait()
    local = valid_ref.shape[0]
    lane = lax.broadcasted_iota(jnp.int32, (1, D), 1)
    extras = jnp.zeros((1, D), F32)
    for j in range(local):
        extras = jnp.where(lane == SHARD + j, owner_ref[j].astype(F32), extras)
        extras = jnp.where(lane == SHARD + local + j, valid_ref[j].astype(F32), extras)
    stage_ref[EXTRA:ROWS, :] = jnp.zeros((ROWS - EXTRA, D), F32)
    for k in range(3):
        stage_ref[SHARD * k : SHARD * (k + 1), :] = conv_ref[k].astype(F32)
    stage_ref[3 * SHARD : EXTRA, :] = mid_ref[...].astype(F32)
    stage_ref[EXTRA : EXTRA + 1, :] = extras
    stage_ref[EXTRA : EXTRA + 1, 0:SHARD] = out_ref[...].astype(F32)
    packed = stage_ref[...].astype(BF16)
    for j in range(copies_ref.shape[0]):
        copies_ref[j] = packed


def state_rows(local):
    tokens = local * BT
    return pl.ds(0, tokens), pl.ds(tokens, 4 * D)


def weight(ref, k):
    return ref[k * D : (k + 1) * D, :]


def forward_kernel(
    valid_ref, owner_ref, core_ref, feats_ref, own_hbm, other_hbm,
    low_out, mid_grad_out, state_ref, sums_ref, out_w_ref, extras_ref, totals_ref,
    raw_ref, own_ref, other_ref, low_ref, mid_grad_ref, wide_ref, sems, out_sems, weight_sems,
):
    local = valid_ref.shape[0]
    slope_ref, weights_ref = (state_ref.at[rows] for rows in state_rows(local))
    arrivals = [
        pltpu.make_async_copy(own_hbm, own_ref, weight_sems.at[0]),
        pltpu.make_async_copy(other_hbm, other_ref, weight_sems.at[1]),
    ]
    for j in range(0, local, GROUP):
        rows = pl.ds(j * BT, GROUP * BT)
        arrivals.append(
            pltpu.make_async_copy(feats_ref.at[rows], raw_ref.at[rows], sems.at[j // GROUP])
        )
    for copy in arrivals:
        copy.start()

    def unpack(parity, source):
        for chip in range(source.shape[0]):
            tile = source[chip].astype(F32)
            device = 2 * chip + parity
            at = SHARD * device
            for k in range(4):
                wide_ref[k * D + at : k * D + at + SHARD, :] = tile[SHARD * k : SHARD * (k + 1)]
            extras_ref[device : device + 1, :] = tile[EXTRA : EXTRA + 1, :128]

    for copy in arrivals[:2]:
        copy.wait()

    @pl.when(core_ref[0] == 0)
    def _():
        unpack(0, own_ref)
        unpack(1, other_ref)

    @pl.when(core_ref[0] == 1)
    def _():
        unpack(1, own_ref)
        unpack(0, other_ref)

    weights_ref[...] = wide_ref[...].astype(BF16)
    devices = extras_ref.shape[0]
    column = lax.broadcasted_iota(jnp.int32, (128, D), 1).astype(F32)
    place = lax.broadcasted_iota(jnp.int32, (128, D), 0).astype(F32)
    home = jnp.floor((column + 0.5) * (1.0 / SHARD))
    pick = jnp.where(column - SHARD * home == place, 1.0, 0.0).astype(BF16)
    spread = jnp.dot(extras_ref[...].astype(BF16), pick, preferred_element_type=F32)
    row = lax.broadcasted_iota(jnp.int32, (devices, D), 0).astype(F32)
    out_w = jnp.sum(jnp.where(home[:devices] == row, spread, 0.0), 0, keepdims=True)
    out_w_ref[...] = out_w

    lane = lax.broadcasted_iota(jnp.int32, (1, 128), 1)
    totals = jnp.zeros((1, 128), F32)
    place = block_place(GROUP * BT)
    departures = []
    for j in range(0, local, GROUP):
        rows = pl.ds(j * BT, GROUP * BT)
        arrivals[2 + j // GROUP].wait()
        keep = row_mask(valid_ref, j, GROUP)
        masked = jnp.where(keep, raw_ref[rows, :].astype(F32), 0.0)
        before, after = neighbours(masked, place, BT - 1)
        first = jnp.dot(before, weight(weights_ref, 0), preferred_element_type=F32)
        first += jnp.dot(
            masked.astype(BF16), weight(weights_ref, 1), preferred_element_type=F32
        )
        first += jnp.dot(after, weight(weights_ref, 2), preferred_element_type=F32)
        first_act, slope = gate(first)
        low = first_act.astype(BF16)
        low_ref[rows, :] = low
        copy = pltpu.make_async_copy(low_ref.at[rows], low_out.at[rows], out_sems.at[0, j // GROUP])
        copy.start()
        departures.append(copy)
        slope_ref[rows, :] = slope.astype(BF16)
        second = jnp.dot(low, weight(weights_ref, 3), preferred_element_type=F32)
        second_act, second_slope = gate(second)
        mid_grad_ref[rows, :] = jnp.where(keep, out_w * second_slope, 0.0).astype(BF16)
        copy = pltpu.make_async_copy(
            mid_grad_ref.at[rows], mid_grad_out.at[rows], out_sems.at[1, j // GROUP]
        )
        copy.start()
        departures.append(copy)
        total = jnp.where(keep, second_act + first_act, 0.0)
        for i in range(GROUP):
            block = jnp.sum(total[i * BT : (i + 1) * BT], 0, keepdims=True)
            sums_ref[j + i : j + i + 1, :] = block
            block_sum = jnp.sum(block * out_w, 1, keepdims=True)
            totals += jnp.where(lane == owner_ref[j + i], block_sum, 0.0)
    for device in range(devices):
        totals_ref[device] = totals
    for copy in departures:
        copy.wait()


def backward_kernel(
    valid_ref, owner_ref, mid_grad_hbm, state_ref, out_w_ref,
    first_grad_out, slots_ref, mid_grad_ref, first_grad_ref, ready_ref, sems, out_sems, in_sems,
):
    local = valid_ref.shape[0]
    slope_ref, weights_ref = (state_ref.at[rows] for rows in state_rows(local))
    place = block_place(GROUP * BT)
    arrivals, copies = [], []
    for j in range(0, local, GROUP):
        rows = pl.ds(j * BT, GROUP * BT)
        copy = pltpu.make_async_copy(
            mid_grad_hbm.at[rows], mid_grad_ref.at[rows], in_sems.at[j // GROUP]
        )
        copy.start()
        arrivals.append(copy)
    for j in range(0, local, GROUP):
        rows = pl.ds(j * BT, GROUP * BT)
        arrivals[j // GROUP].wait()
        keep = row_mask(valid_ref, j, GROUP)
        grad = lax.dot_general(
            mid_grad_ref[rows, :], weight(weights_ref, 3), OVER_LAST, preferred_element_type=F32
        )
        grad = (grad + jnp.where(keep, out_w_ref[...], 0.0)) * slope_ref[rows, :].astype(F32)
        before, after = neighbours(grad, place, BT - 1)
        low = grad.astype(BF16)
        first_grad_ref[rows, :] = low
        total = lax.dot_general(low, weight(weights_ref, 1), OVER_LAST, preferred_element_type=F32)
        total += lax.dot_general(
            after, weight(weights_ref, 0), OVER_LAST, preferred_element_type=F32
        )
        total += lax.dot_general(
            before, weight(weights_ref, 2), OVER_LAST, preferred_element_type=F32
        )
        total = jnp.where(keep, total, 0.0).astype(BF16)
        for i in range(GROUP):
            ready_ref[j + i] = total[i * BT : (i + 1) * BT]
            copy = pltpu.make_async_copy(
                ready_ref.at[j + i], slots_ref.at[owner_ref[j + i]], sems.at[j + i]
            )
            copy.start()
            copies.append(copy)
        copy = pltpu.make_async_copy(
            first_grad_ref.at[rows], first_grad_out.at[rows], out_sems.at[j // GROUP]
        )
        copy.start()
        copies.append(copy)
    for copy in copies:
        copy.wait()


def weight_kernel(
    valid_ref, factor_ref, feats_hbm, low_hbm, mid_grad_hbm, first_grad_hbm, sums_ref,
    parts_ref, feats_ref, low_ref, mid_grad_ref, first_grad_ref, conv_ref, mid_ref, stage_ref, sems,
):
    local = valid_ref.shape[0]
    pairs = (
        (feats_hbm, feats_ref),
        (low_hbm, low_ref),
        (mid_grad_hbm, mid_grad_ref),
        (first_grad_hbm, first_grad_ref),
    )
    arrivals = []
    for j in range(local):
        rows = pl.ds(j * BT, BT)
        arrivals.append(
            [
                pltpu.make_async_copy(source.at[rows], target.at[rows], sems.at[i, j])
                for i, (source, target) in enumerate(pairs)
            ]
        )
        for copy in arrivals[j]:
            copy.start()
    out = jnp.zeros((1, D), F32)
    place = block_place(BT)
    for j in range(local):
        rows = pl.ds(j * BT, BT)
        for copy in arrivals[j]:
            copy.wait()
        factor = factor_ref[j]
        out += sums_ref[j : j + 1, :] * factor
        grad = first_grad_ref[rows, :].astype(F32) * factor
        before, after = neighbours(grad, place, BT - 1)
        mid_grad = (mid_grad_ref[rows, :].astype(F32) * factor).astype(BF16)
        keep = row_mask(valid_ref, j, 1)
        masked = jnp.where(keep, feats_ref[rows, :].astype(F32), 0.0).astype(BF16)
        terms = [
            lax.dot_general(masked, x, OVER_ROWS, preferred_element_type=F32)
            for x in (after, grad.astype(BF16), before)
        ]
        mid = lax.dot_general(low_ref[rows, :], mid_grad, OVER_ROWS, preferred_element_type=F32)
        for k in range(3):
            conv_ref[k] = terms[k] if j == 0 else conv_ref[k] + terms[k]
        mid_ref[...] = mid if j == 0 else mid_ref[...] + mid

    devices = parts_ref.shape[0]
    column = lax.broadcasted_iota(jnp.int32, (D, D), 0).astype(F32)
    place = lax.broadcasted_iota(jnp.int32, (D, D), 1).astype(F32)
    home = jnp.floor((column + 0.5) * (1.0 / SHARD))
    pick = jnp.where(column - SHARD * home == place, 1.0, 0.0).astype(BF16)
    device = lax.broadcasted_iota(jnp.int32, (devices, D), 0).astype(F32)
    lane = lax.broadcasted_iota(jnp.int32, (devices, D), 1).astype(F32)
    mine = jnp.floor((lane + 0.5) * (1.0 / SHARD)) == device
    out_rows = jnp.where(mine, out, 0.0).astype(BF16)
    out_rows = jnp.dot(out_rows, pick, preferred_element_type=F32)
    stage_ref[EXTRA:ROWS, :] = jnp.zeros((ROWS - EXTRA, D), F32)
    for d in range(devices):
        at = SHARD * d
        for k in range(3):
            stage_ref[SHARD * k : SHARD * (k + 1), :] = conv_ref[k, at : at + SHARD, :]
        stage_ref[3 * SHARD : EXTRA, :] = mid_ref[at : at + SHARD, :]
        stage_ref[EXTRA : EXTRA + 1, :] = out_rows[d : d + 1, :]
        parts_ref[d] = stage_ref[...].astype(BF16)


def finish_kernel(pieces_ref, conv_ref, mid_ref, out_ref, total_ref):
    total = pieces_ref[0].astype(F32)
    for i in range(1, pieces_ref.shape[0]):
        total += pieces_ref[i].astype(F32)
    total_ref[...] = total * (1.0 / BT)
    for row in range(3 * SHARD):
        conv_ref[row] = total_ref[row : row + 1, :]
    for row in range(SHARD):
        mid_ref[row] = total_ref[3 * SHARD + row : 3 * SHARD + row + 1, :]
    out_ref[...] = total_ref[EXTRA : EXTRA + 1, 0:SHARD]


def place_kernel(
    source_ref, count_ref, factor_ref, received_ref, placed_ref, raw_ref, ready_ref, in_sems, out_sems
):
    capacity = source_ref.shape[0]
    arrivals, departures = [], []
    for slot in range(capacity):
        copy = pltpu.make_async_copy(
            received_ref.at[source_ref[slot]], raw_ref.at[slot], in_sems.at[slot]
        )
        copy.start()
        arrivals.append(copy)
    for slot in range(capacity):
        arrivals[slot].wait()
        factor = jnp.where(slot < count_ref[0], factor_ref[0], 0.0)
        ready_ref[slot] = (raw_ref[slot].astype(F32) * factor).astype(BF16)
        rows = pl.ds(slot * BT, BT)
        copy = pltpu.make_async_copy(ready_ref.at[slot], placed_ref.at[rows], out_sems.at[slot])
        copy.start()
        departures.append(copy)
    for copy in departures:
        copy.wait()


def in_hbm(x):
    return pltpu.with_memory_space_constraint(x, pltpu.HBM)


def in_vmem(x):
    return pltpu.with_memory_space_constraint(x, pltpu.VMEM)


def call(kernel, name, in_specs, outs, scratch=(), megabytes=0):
    return pl.pallas_call(
        kernel,
        in_specs=in_specs,
        out_specs=[spec for spec, _, _ in outs],
        out_shape=[
            (pltpu.HBM if spec is IN_HBM else pltpu.VMEM)(shape, dtype) for spec, shape, dtype in outs
        ],
        scratch_shapes=list(scratch),
        compiler_params=pltpu.CompilerParams(vmem_limit_bytes=VMEM_LIMIT),
        cost_estimate=pl.CostEstimate(
            flops=0, transcendentals=0, bytes_accessed=megabytes * 1024 * 1024
        ),
        name=name,
    )


def per_device(feats, valid, owner_map, w_conv, w_mid, w_out):
    local = owner_map.shape[0]
    devices = lax.axis_size(DP)
    chips = devices // 2
    capacity = devices // 2
    tokens_here = local * BT
    me = lax.axis_index(DP)
    core = lax.axis_index("dp_2").astype(jnp.int32).reshape(1)
    images = jnp.arange(devices, dtype=jnp.int32)

    (copies,) = call(
        pack_kernel,
        "pack",
        [IN_HBM] * 5,
        [(IN_VMEM, (chips, ROWS, D), BF16)],
        [
            pltpu.SMEM((local,), jnp.int32),
            pltpu.SMEM((local,), jnp.int32),
            pltpu.VMEM((3, SHARD, D), BF16),
            pltpu.VMEM((SHARD, D), BF16),
            pltpu.VMEM((1, SHARD), BF16),
            pltpu.VMEM((ROWS, D), F32),
            pltpu.SemaphoreType.DMA((5,)),
        ],
    )(*(in_hbm(x) for x in (valid, owner_map, w_conv[0], w_mid[0], w_out)))
    own = lax.all_to_all(copies, CHIPS, split_axis=0, concat_axis=0, tiled=True)
    other = swapped(own)

    low, mid_grad, state, sums, out_w, extras, totals = call(
        forward_kernel,
        "forward",
        [IN_SMEM, IN_SMEM, IN_SMEM, IN_HBM, IN_HBM, IN_HBM],
        [
            (IN_HBM, (tokens_here, D), BF16),
            (IN_HBM, (tokens_here, D), BF16),
            (IN_VMEM, (tokens_here + 4 * D, D), BF16),
            (IN_VMEM, (local, D), F32),
            (IN_VMEM, (1, D), F32),
            (IN_VMEM, (devices, 128), F32),
            (IN_VMEM, (devices, 1, 128), F32),
        ],
        [
            pltpu.VMEM((tokens_here, D), BF16),
            pltpu.VMEM((chips, ROWS, D), BF16),
            pltpu.VMEM((chips, ROWS, D), BF16),
            pltpu.VMEM((tokens_here, D), BF16),
            pltpu.VMEM((tokens_here, D), BF16),
            pltpu.VMEM((4 * D, D), F32),
            pltpu.SemaphoreType.DMA((local // GROUP,)),
            pltpu.SemaphoreType.DMA((2, local // GROUP)),
            pltpu.SemaphoreType.DMA((2,)),
        ],
    )(valid, owner_map, core, in_hbm(feats[0]), in_hbm(own), in_hbm(other))

    totals = lax.all_to_all(totals, DP, split_axis=0, concat_axis=0, tiled=True)

    first_grad, slots = call(
        backward_kernel,
        "backward",
        [IN_SMEM, IN_SMEM, IN_HBM, IN_VMEM, IN_VMEM],
        [
            (IN_HBM, (tokens_here, D), BF16),
            (IN_HBM, (devices, BT, D), BF16),
        ],
        [
            pltpu.VMEM((tokens_here, D), BF16),
            pltpu.VMEM((tokens_here, D), BF16),
            pltpu.VMEM((local, BT, D), BF16),
            pltpu.SemaphoreType.DMA((local,)),
            pltpu.SemaphoreType.DMA((local // GROUP,)),
            pltpu.SemaphoreType.DMA((local // GROUP,)),
        ],
        megabytes=24,
    )(valid, owner_map, in_hbm(mid_grad), in_vmem(state), in_vmem(out_w))

    slots, totals = lax.optimization_barrier((slots, totals))
    received = lax.all_to_all(slots, DP, split_axis=0, concat_axis=0, tiled=True)

    totals = total_over(jnp.sum(totals[:, 0, :devices], 0)[None], "head")[0]
    members = (owner_map[:, None] == images[None, :]).astype(F32)
    owners = extras[:, SHARD : SHARD + local].astype(jnp.int32)
    valids = extras[:, SHARD + local : SHARD + 2 * local]
    tokens = jnp.sum(jnp.where(owners[:, :, None] == images, valids[:, :, None], 0.0), (0, 1))
    norm = jnp.sqrt(TAPS * tokens)
    factor = -BT * jax.nn.sigmoid(-totals / norm) / norm
    block_factor = jnp.sum(members * factor[None, :], 1)
    own_factor = jnp.sum(jnp.where(images == me, factor, 0.0)).reshape(1)

    (parts,) = call(
        weight_kernel,
        "weight_grads",
        [IN_SMEM, IN_SMEM, IN_HBM, IN_HBM, IN_HBM, IN_HBM, IN_VMEM],
        [(IN_VMEM, (devices, ROWS, D), BF16)],
        [pltpu.VMEM((tokens_here, D), BF16)] * 4
        + [
            pltpu.VMEM((3, D, D), F32),
            pltpu.VMEM((D, D), F32),
            pltpu.VMEM((ROWS, D), F32),
            pltpu.SemaphoreType.DMA((4, local)),
        ],
        megabytes=16,
    )(
        valid, block_factor, in_hbm(feats[0]), in_hbm(low), in_hbm(mid_grad),
        in_hbm(first_grad), in_vmem(sums),
    )
    parts = parts.reshape(4, 4, 2, ROWS, D)
    parts = scattered_sum(parts, "dp_2", 2)
    parts = scattered_sum(parts, "dp_0", 0)
    parts, received = lax.optimization_barrier((parts, received))
    pieces = lax.all_to_all(
        parts.astype(BF16), "dp_1", split_axis=0, concat_axis=0, tiled=True
    )

    present = jnp.sum((owners == me).astype(jnp.int32), 1)
    rank = jnp.sum(jnp.where(images[None, :] < images[:, None], present[None, :], 0), 1)
    count = jnp.sum(present)
    wanted = jnp.minimum(jnp.arange(capacity, dtype=jnp.int32), count - 1)
    hit = (rank[None, :] == wanted[:, None]) & (present[None, :] > 0)
    source = jnp.sum(jnp.where(hit, images[None, :], 0), 1).astype(jnp.int32)
    (placed,) = call(
        place_kernel,
        "place",
        [IN_SMEM, IN_SMEM, IN_SMEM, IN_HBM],
        [(IN_HBM, (capacity * BT, D), BF16)],
        [
            pltpu.VMEM((capacity, BT, D), BF16),
            pltpu.VMEM((capacity, BT, D), BF16),
            pltpu.SemaphoreType.DMA((capacity,)),
            pltpu.SemaphoreType.DMA((capacity,)),
        ],
        megabytes=24,
    )(source, count.reshape(1), own_factor, in_hbm(received))

    conv, mid, out = pl.pallas_call(
        finish_kernel,
        in_specs=[IN_VMEM],
        out_specs=[IN_VMEM] * 3,
        out_shape=[
            jax.ShapeDtypeStruct((3 * SHARD, 1, D), F32),
            jax.ShapeDtypeStruct((SHARD, 1, D), F32),
            jax.ShapeDtypeStruct((1, SHARD), F32),
        ],
        scratch_shapes=[pltpu.VMEM((ROWS, D), F32)],
        name="finish",
    )(in_vmem(pieces))
    return placed[None], conv.reshape(1, 3, SHARD, D), mid.reshape(1, SHARD, D), out


def solution(mesh):
    split = Mesh(
        mesh.devices.reshape(4, 4, 2, mesh.shape["head"]), ("dp_0", "dp_1", "dp_2", "head")
    )
    in_specs = (
        P("head", DP, None),
        P(DP),
        P(DP),
        P("head", None, DP, None),
        P("head", DP, None),
        P("head", DP),
    )
    out_specs = (P("head", DP, None), P("head", None, DP, None), P("head", DP, None), P("head", DP))
    return jax.shard_map(
        per_device, mesh=split, in_specs=in_specs, out_specs=out_specs, check_vma=False
    )
```

```python
import jax
import jax.numpy as jnp
from jax import lax
from jax.experimental import pallas as pl
from jax.experimental.pallas import tpu as pltpu
from jax.sharding import Mesh
from jax.sharding import PartitionSpec as P

DP = ("dp_0", "dp_1", "dp_2")
CHIPS = ("dp_0", "dp_1")
BF16 = jnp.bfloat16
F32 = jnp.float32
TAPS = 4
BT = 256
D = 384
SHARD = 12
EXTRA = 4 * SHARD
ROWS = 56
GROUP = 4
LOG_2 = 0.6931471805599453
VMEM_LIMIT = 20 * 1024 * 1024

IN_VMEM = pl.BlockSpec(memory_space=pltpu.VMEM)
IN_SMEM = pl.BlockSpec(memory_space=pltpu.SMEM)
IN_HBM = pl.BlockSpec(memory_space=pltpu.HBM)
OVER_LAST = (((1,), (1,)), ((), ()))
OVER_ROWS = (((0,), (0,)), ((), ()))


def swapped(x):
    return lax.ppermute(x, "dp_2", [(0, 1), (1, 0)])


def turned(x, axis, shift):
    count = lax.axis_size(axis)
    return lax.ppermute(x, axis, [(i, (i + shift) % count) for i in range(count)])


def total_over(x, axis):
    return sum((turned(x, axis, r) for r in range(1, lax.axis_size(axis))), x)


def scattered(parts, axis, dim):
    count, index = lax.axis_size(axis), lax.axis_index(axis)

    def piece(shift):
        return lax.dynamic_index_in_dim(parts, (index + shift) % count, dim, keepdims=False)

    return [piece(0)] + [turned(piece(r).astype(BF16), axis, r) for r in range(1, count)]


def scattered_sum(parts, axis, dim):
    return sum(piece.astype(F32) for piece in scattered(parts, axis, dim))


def gate(value):
    half = jnp.tanh(0.5 * value)
    tail = 0.8 * LOG_2 - (0.8 * LOG_2) * jnp.log2(1.0 + jnp.abs(half))
    return jnp.maximum(value, 0.2 * value) + tail, 0.6 + 0.4 * half


def row_mask(valid_ref, first, blocks):
    rows = lax.broadcasted_iota(jnp.int32, (blocks * BT, 1), 0)
    limit = jnp.full_like(rows, valid_ref[first])
    for j in range(1, blocks):
        limit = jnp.where(rows < j * BT, limit, j * BT + valid_ref[first + j])
    return rows < limit


def neighbours(x, place, last):
    count = x.shape[0]
    before = jnp.where(place == 0, 0.0, pltpu.roll(x, 1, 0))
    after = jnp.where(place == last, 0.0, pltpu.roll(x, count - 1, 0))
    return before.astype(BF16), after.astype(BF16)


def block_place(count):
    return lax.broadcasted_iota(jnp.int32, (count, 1), 0) % BT


def pack_kernel(
    valid_hbm, owner_hbm, conv_hbm, mid_hbm, out_hbm,
    copies_ref, valid_ref, owner_ref, conv_ref, mid_ref, out_ref, stage_ref, sems,
):
    sources = (valid_hbm, owner_hbm, conv_hbm, mid_hbm, out_hbm)
    targets = (valid_ref, owner_ref, conv_ref, mid_ref, out_ref)
    arrivals = [
        pltpu.make_async_copy(source, target, sems.at[i])
        for i, (source, target) in enumerate(zip(sources, targets))
    ]
    for copy in arrivals:
        copy.start()
    for copy in arrivals:
        copy.wait()
    local = valid_ref.shape[0]
    lane = lax.broadcasted_iota(jnp.int32, (1, D), 1)
    extras = jnp.zeros((1, D), F32)
    for j in range(local):
        extras = jnp.where(lane == SHARD + j, owner_ref[j].astype(F32), extras)
        extras = jnp.where(lane == SHARD + local + j, valid_ref[j].astype(F32), extras)
    stage_ref[EXTRA:ROWS, :] = jnp.zeros((ROWS - EXTRA, D), F32)
    for k in range(3):
        stage_ref[SHARD * k : SHARD * (k + 1), :] = conv_ref[k].astype(F32)
    stage_ref[3 * SHARD : EXTRA, :] = mid_ref[...].astype(F32)
    stage_ref[EXTRA : EXTRA + 1, :] = extras
    stage_ref[EXTRA : EXTRA + 1, 0:SHARD] = out_ref[...].astype(F32)
    packed = stage_ref[...].astype(BF16)
    for j in range(copies_ref.shape[0]):
        copies_ref[j] = packed


def chunks(local):
    half, quarter = local // 2, local // 4
    return ((0, half), (half, quarter), (half + quarter, quarter))


def state_rows(local):
    tokens = local * BT
    return pl.ds(0, tokens), pl.ds(tokens, 4 * D)


def weight(ref, k):
    return ref[k * D : (k + 1) * D, :]


def forward_kernel(
    valid_ref, owner_ref, core_ref, feats_ref, own_hbm, other_hbm,
    low_out, mid_grad_out, state_ref, sums_ref, out_w_ref, extras_ref, totals_ref,
    raw_ref, own_ref, other_ref, low_ref, mid_grad_ref, wide_ref, sems, out_sems, weight_sems,
):
    local = valid_ref.shape[0]
    slope_ref, weights_ref = (state_ref.at[rows] for rows in state_rows(local))
    arrivals = [
        pltpu.make_async_copy(own_hbm, own_ref, weight_sems.at[0]),
        pltpu.make_async_copy(other_hbm, other_ref, weight_sems.at[1]),
    ]
    for n, (j, group) in enumerate(chunks(local)):
        rows = pl.ds(j * BT, group * BT)
        arrivals.append(pltpu.make_async_copy(feats_ref.at[rows], raw_ref.at[rows], sems.at[n]))
    for copy in arrivals:
        copy.start()

    def unpack(parity, source):
        for chip in range(source.shape[0]):
            tile = source[chip].astype(F32)
            device = 2 * chip + parity
            at = SHARD * device
            for k in range(4):
                wide_ref[k * D + at : k * D + at + SHARD, :] = tile[SHARD * k : SHARD * (k + 1)]
            extras_ref[device : device + 1, :] = tile[EXTRA : EXTRA + 1, :128]

    for copy in arrivals[:2]:
        copy.wait()

    @pl.when(core_ref[0] == 0)
    def _():
        unpack(0, own_ref)
        unpack(1, other_ref)

    @pl.when(core_ref[0] == 1)
    def _():
        unpack(1, own_ref)
        unpack(0, other_ref)

    weights_ref[...] = wide_ref[...].astype(BF16)
    devices = extras_ref.shape[0]
    column = lax.broadcasted_iota(jnp.int32, (128, D), 1).astype(F32)
    place = lax.broadcasted_iota(jnp.int32, (128, D), 0).astype(F32)
    home = jnp.floor((column + 0.5) * (1.0 / SHARD))
    pick = jnp.where(column - SHARD * home == place, 1.0, 0.0).astype(BF16)
    spread = jnp.dot(extras_ref[...].astype(BF16), pick, preferred_element_type=F32)
    row = lax.broadcasted_iota(jnp.int32, (devices, D), 0).astype(F32)
    out_w = jnp.sum(jnp.where(home[:devices] == row, spread, 0.0), 0, keepdims=True)
    out_w_ref[...] = out_w

    lane = lax.broadcasted_iota(jnp.int32, (1, 128), 1)
    totals = jnp.zeros((1, 128), F32)
    departures = []
    for n, (j, group) in enumerate(chunks(local)):
        rows = pl.ds(j * BT, group * BT)
        arrivals[2 + n].wait()
        place = block_place(group * BT)
        keep = row_mask(valid_ref, j, group)
        masked = jnp.where(keep, raw_ref[rows, :].astype(F32), 0.0)
        before, after = neighbours(masked, place, BT - 1)
        first = jnp.dot(before, weight(weights_ref, 0), preferred_element_type=F32)
        first += jnp.dot(
            masked.astype(BF16), weight(weights_ref, 1), preferred_element_type=F32
        )
        first += jnp.dot(after, weight(weights_ref, 2), preferred_element_type=F32)
        first_act, slope = gate(first)
        low = first_act.astype(BF16)
        low_ref[rows, :] = low
        copy = pltpu.make_async_copy(low_ref.at[rows], low_out.at[rows], out_sems.at[0, n])
        copy.start()
        departures.append(copy)
        slope_ref[rows, :] = slope.astype(BF16)
        second = jnp.dot(low, weight(weights_ref, 3), preferred_element_type=F32)
        second_act, second_slope = gate(second)
        mid_grad_ref[rows, :] = jnp.where(keep, out_w * second_slope, 0.0).astype(BF16)
        copy = pltpu.make_async_copy(
            mid_grad_ref.at[rows], mid_grad_out.at[rows], out_sems.at[1, n]
        )
        copy.start()
        departures.append(copy)
        total = jnp.where(keep, second_act + first_act, 0.0)
        for i in range(group):
            block = jnp.sum(total[i * BT : (i + 1) * BT], 0, keepdims=True)
            sums_ref[j + i : j + i + 1, :] = block
            block_sum = jnp.sum(block * out_w, 1, keepdims=True)
            totals += jnp.where(lane == owner_ref[j + i], block_sum, 0.0)
    for device in range(devices):
        totals_ref[device] = totals
    for copy in departures:
        copy.wait()


def backward_kernel(
    valid_ref, owner_ref, mid_grad_hbm, state_ref, out_w_ref,
    first_grad_out, slots_ref, mid_grad_ref, first_grad_ref, ready_ref, sems, out_sems, in_sems,
):
    local = valid_ref.shape[0]
    slope_ref, weights_ref = (state_ref.at[rows] for rows in state_rows(local))
    place = block_place(GROUP * BT)
    arrivals, copies = [], []
    for j in range(0, local, GROUP):
        rows = pl.ds(j * BT, GROUP * BT)
        copy = pltpu.make_async_copy(
            mid_grad_hbm.at[rows], mid_grad_ref.at[rows], in_sems.at[j // GROUP]
        )
        copy.start()
        arrivals.append(copy)
    for j in range(0, local, GROUP):
        rows = pl.ds(j * BT, GROUP * BT)
        arrivals[j // GROUP].wait()
        keep = row_mask(valid_ref, j, GROUP)
        grad = lax.dot_general(
            mid_grad_ref[rows, :], weight(weights_ref, 3), OVER_LAST, preferred_element_type=F32
        )
        grad = (grad + jnp.where(keep, out_w_ref[...], 0.0)) * slope_ref[rows, :].astype(F32)
        before, after = neighbours(grad, place, BT - 1)
        low = grad.astype(BF16)
        first_grad_ref[rows, :] = low
        total = lax.dot_general(low, weight(weights_ref, 1), OVER_LAST, preferred_element_type=F32)
        total += lax.dot_general(
            after, weight(weights_ref, 0), OVER_LAST, preferred_element_type=F32
        )
        total += lax.dot_general(
            before, weight(weights_ref, 2), OVER_LAST, preferred_element_type=F32
        )
        total = jnp.where(keep, total, 0.0).astype(BF16)
        for i in range(GROUP):
            ready_ref[j + i] = total[i * BT : (i + 1) * BT]
            copy = pltpu.make_async_copy(
                ready_ref.at[j + i], slots_ref.at[owner_ref[j + i]], sems.at[j + i]
            )
            copy.start()
            copies.append(copy)
        copy = pltpu.make_async_copy(
            first_grad_ref.at[rows], first_grad_out.at[rows], out_sems.at[j // GROUP]
        )
        copy.start()
        copies.append(copy)
    for copy in copies:
        copy.wait()


def weight_kernel(
    valid_ref, factor_ref, feats_hbm, low_hbm, mid_grad_hbm, first_grad_hbm, sums_ref,
    parts_ref, feats_ref, low_ref, mid_grad_ref, first_grad_ref, conv_ref, mid_ref, stage_ref, sems,
):
    local = valid_ref.shape[0]
    pairs = (
        (feats_hbm, feats_ref),
        (low_hbm, low_ref),
        (mid_grad_hbm, mid_grad_ref),
        (first_grad_hbm, first_grad_ref),
    )
    arrivals = []
    for j in range(local):
        rows = pl.ds(j * BT, BT)
        arrivals.append(
            [
                pltpu.make_async_copy(source.at[rows], target.at[rows], sems.at[i, j])
                for i, (source, target) in enumerate(pairs)
            ]
        )
        for copy in arrivals[j]:
            copy.start()
    out = jnp.zeros((1, D), F32)
    place = block_place(BT)
    for j in range(local):
        rows = pl.ds(j * BT, BT)
        for copy in arrivals[j]:
            copy.wait()
        factor = factor_ref[j]
        out += sums_ref[j : j + 1, :] * factor
        grad = first_grad_ref[rows, :].astype(F32) * factor
        before, after = neighbours(grad, place, BT - 1)
        mid_grad = (mid_grad_ref[rows, :].astype(F32) * factor).astype(BF16)
        keep = row_mask(valid_ref, j, 1)
        masked = jnp.where(keep, feats_ref[rows, :].astype(F32), 0.0).astype(BF16)
        terms = [
            lax.dot_general(masked, x, OVER_ROWS, preferred_element_type=F32)
            for x in (after, grad.astype(BF16), before)
        ]
        mid = lax.dot_general(low_ref[rows, :], mid_grad, OVER_ROWS, preferred_element_type=F32)
        for k in range(3):
            conv_ref[k] = terms[k] if j == 0 else conv_ref[k] + terms[k]
        mid_ref[...] = mid if j == 0 else mid_ref[...] + mid

    devices = parts_ref.shape[0]
    column = lax.broadcasted_iota(jnp.int32, (D, D), 0).astype(F32)
    place = lax.broadcasted_iota(jnp.int32, (D, D), 1).astype(F32)
    home = jnp.floor((column + 0.5) * (1.0 / SHARD))
    pick = jnp.where(column - SHARD * home == place, 1.0, 0.0).astype(BF16)
    device = lax.broadcasted_iota(jnp.int32, (devices, D), 0).astype(F32)
    lane = lax.broadcasted_iota(jnp.int32, (devices, D), 1).astype(F32)
    mine = jnp.floor((lane + 0.5) * (1.0 / SHARD)) == device
    out_rows = jnp.where(mine, out, 0.0).astype(BF16)
    out_rows = jnp.dot(out_rows, pick, preferred_element_type=F32)
    stage_ref[EXTRA:ROWS, :] = jnp.zeros((ROWS - EXTRA, D), F32)
    for d in range(devices):
        at = SHARD * d
        for k in range(3):
            stage_ref[SHARD * k : SHARD * (k + 1), :] = conv_ref[k, at : at + SHARD, :]
        stage_ref[3 * SHARD : EXTRA, :] = mid_ref[at : at + SHARD, :]
        stage_ref[EXTRA : EXTRA + 1, :] = out_rows[d : d + 1, :]
        parts_ref[d] = stage_ref[...].astype(BF16)


def finish_kernel(own_ref, first_ref, second_ref, third_ref, conv_ref, mid_ref, out_ref, total_ref):
    total = own_ref[...]
    for piece in (first_ref, second_ref, third_ref):
        total += piece[...].astype(F32)
    total_ref[...] = total * (1.0 / BT)
    for row in range(3 * SHARD):
        conv_ref[row] = total_ref[row : row + 1, :]
    for row in range(SHARD):
        mid_ref[row] = total_ref[3 * SHARD + row : 3 * SHARD + row + 1, :]
    out_ref[...] = total_ref[EXTRA : EXTRA + 1, 0:SHARD]


def place_kernel(
    source_ref, count_ref, factor_ref, received_ref, placed_ref, raw_ref, ready_ref, in_sems, out_sems
):
    capacity = source_ref.shape[0]
    arrivals, departures = [], []
    for slot in range(capacity):
        copy = pltpu.make_async_copy(
            received_ref.at[source_ref[slot]], raw_ref.at[slot], in_sems.at[slot]
        )
        copy.start()
        arrivals.append(copy)
    for slot in range(capacity):
        arrivals[slot].wait()
        factor = jnp.where(slot < count_ref[0], factor_ref[0], 0.0)
        ready_ref[slot] = (raw_ref[slot].astype(F32) * factor).astype(BF16)
        rows = pl.ds(slot * BT, BT)
        copy = pltpu.make_async_copy(ready_ref.at[slot], placed_ref.at[rows], out_sems.at[slot])
        copy.start()
        departures.append(copy)
    for copy in departures:
        copy.wait()


def in_hbm(x):
    return pltpu.with_memory_space_constraint(x, pltpu.HBM)


def in_vmem(x):
    return pltpu.with_memory_space_constraint(x, pltpu.VMEM)


def call(kernel, name, in_specs, outs, scratch=(), megabytes=0):
    return pl.pallas_call(
        kernel,
        in_specs=in_specs,
        out_specs=[spec for spec, _, _ in outs],
        out_shape=[
            (pltpu.HBM if spec is IN_HBM else pltpu.VMEM)(shape, dtype) for spec, shape, dtype in outs
        ],
        scratch_shapes=list(scratch),
        compiler_params=pltpu.CompilerParams(vmem_limit_bytes=VMEM_LIMIT),
        cost_estimate=pl.CostEstimate(
            flops=0, transcendentals=0, bytes_accessed=megabytes * 1024 * 1024
        ),
        name=name,
    )


def per_device(feats, valid, owner_map, w_conv, w_mid, w_out):
    local = owner_map.shape[0]
    devices = lax.axis_size(DP)
    chips = devices // 2
    capacity = devices // 2
    tokens_here = local * BT
    me = lax.axis_index(DP)
    core = lax.axis_index("dp_2").astype(jnp.int32).reshape(1)
    images = jnp.arange(devices, dtype=jnp.int32)

    (copies,) = call(
        pack_kernel,
        "pack",
        [IN_HBM] * 5,
        [(IN_VMEM, (chips, ROWS, D), BF16)],
        [
            pltpu.SMEM((local,), jnp.int32),
            pltpu.SMEM((local,), jnp.int32),
            pltpu.VMEM((3, SHARD, D), BF16),
            pltpu.VMEM((SHARD, D), BF16),
            pltpu.VMEM((1, SHARD), BF16),
            pltpu.VMEM((ROWS, D), F32),
            pltpu.SemaphoreType.DMA((5,)),
        ],
    )(*(in_hbm(x) for x in (valid, owner_map, w_conv[0], w_mid[0], w_out)))
    own = lax.all_to_all(copies, CHIPS, split_axis=0, concat_axis=0, tiled=True)
    other = swapped(own)

    low, mid_grad, state, sums, out_w, extras, totals = call(
        forward_kernel,
        "forward",
        [IN_SMEM, IN_SMEM, IN_SMEM, IN_HBM, IN_HBM, IN_HBM],
        [
            (IN_HBM, (tokens_here, D), BF16),
            (IN_HBM, (tokens_here, D), BF16),
            (IN_VMEM, (tokens_here + 4 * D, D), BF16),
            (IN_VMEM, (local, D), F32),
            (IN_VMEM, (1, D), F32),
            (IN_VMEM, (devices, 128), F32),
            (IN_VMEM, (devices, 1, 128), F32),
        ],
        [
            pltpu.VMEM((tokens_here, D), BF16),
            pltpu.VMEM((chips, ROWS, D), BF16),
            pltpu.VMEM((chips, ROWS, D), BF16),
            pltpu.VMEM((tokens_here, D), BF16),
            pltpu.VMEM((tokens_here, D), BF16),
            pltpu.VMEM((4 * D, D), F32),
            pltpu.SemaphoreType.DMA((3,)),
            pltpu.SemaphoreType.DMA((2, 3)),
            pltpu.SemaphoreType.DMA((2,)),
        ],
    )(valid, owner_map, core, in_hbm(feats[0]), in_hbm(own), in_hbm(other))

    totals = lax.all_to_all(totals, DP, split_axis=0, concat_axis=0, tiled=True)

    first_grad, slots = call(
        backward_kernel,
        "backward",
        [IN_SMEM, IN_SMEM, IN_HBM, IN_VMEM, IN_VMEM],
        [
            (IN_HBM, (tokens_here, D), BF16),
            (IN_HBM, (devices, BT, D), BF16),
        ],
        [
            pltpu.VMEM((tokens_here, D), BF16),
            pltpu.VMEM((tokens_here, D), BF16),
            pltpu.VMEM((local, BT, D), BF16),
            pltpu.SemaphoreType.DMA((local,)),
            pltpu.SemaphoreType.DMA((local // GROUP,)),
            pltpu.SemaphoreType.DMA((local // GROUP,)),
        ],
        megabytes=24,
    )(valid, owner_map, in_hbm(mid_grad), in_vmem(state), in_vmem(out_w))

    slots, totals = lax.optimization_barrier((slots, totals))
    received = lax.all_to_all(slots, DP, split_axis=0, concat_axis=0, tiled=True)

    totals = total_over(jnp.sum(totals[:, 0, :devices], 0)[None], "head")[0]
    members = (owner_map[:, None] == images[None, :]).astype(F32)
    owners = extras[:, SHARD : SHARD + local].astype(jnp.int32)
    valids = extras[:, SHARD + local : SHARD + 2 * local]
    tokens = jnp.sum(jnp.where(owners[:, :, None] == images, valids[:, :, None], 0.0), (0, 1))
    norm = jnp.sqrt(TAPS * tokens)
    factor = -BT * jax.nn.sigmoid(-totals / norm) / norm
    block_factor = jnp.sum(members * factor[None, :], 1)
    own_factor = jnp.sum(jnp.where(images == me, factor, 0.0)).reshape(1)

    (parts,) = call(
        weight_kernel,
        "weight_grads",
        [IN_SMEM, IN_SMEM, IN_HBM, IN_HBM, IN_HBM, IN_HBM, IN_VMEM],
        [(IN_VMEM, (devices, ROWS, D), BF16)],
        [pltpu.VMEM((tokens_here, D), BF16)] * 4
        + [
            pltpu.VMEM((3, D, D), F32),
            pltpu.VMEM((D, D), F32),
            pltpu.VMEM((ROWS, D), F32),
            pltpu.SemaphoreType.DMA((4, local)),
        ],
        megabytes=16,
    )(
        valid, block_factor, in_hbm(feats[0]), in_hbm(low), in_hbm(mid_grad),
        in_hbm(first_grad), in_vmem(sums),
    )
    parts = parts.reshape(4, 4, 2, ROWS, D)
    parts = scattered_sum(parts, "dp_2", 2)
    pieces = scattered(parts, "dp_0", 0)

    present = jnp.sum((owners == me).astype(jnp.int32), 1)
    rank = jnp.sum(jnp.where(images[None, :] < images[:, None], present[None, :], 0), 1)
    count = jnp.sum(present)
    wanted = jnp.minimum(jnp.arange(capacity, dtype=jnp.int32), count - 1)
    hit = (rank[None, :] == wanted[:, None]) & (present[None, :] > 0)
    source = jnp.sum(jnp.where(hit, images[None, :], 0), 1).astype(jnp.int32)
    (placed,) = call(
        place_kernel,
        "place",
        [IN_SMEM, IN_SMEM, IN_SMEM, IN_HBM],
        [(IN_HBM, (capacity * BT, D), BF16)],
        [
            pltpu.VMEM((capacity, BT, D), BF16),
            pltpu.VMEM((capacity, BT, D), BF16),
            pltpu.SemaphoreType.DMA((capacity,)),
            pltpu.SemaphoreType.DMA((capacity,)),
        ],
        megabytes=24,
    )(source, count.reshape(1), own_factor, in_hbm(received))

    pieces, placed = lax.optimization_barrier((pieces, placed))
    pieces = scattered(sum(piece.astype(F32) for piece in pieces), "dp_1", 0)
    conv, mid, out = pl.pallas_call(
        finish_kernel,
        in_specs=[IN_VMEM] * 4,
        out_specs=[IN_VMEM] * 3,
        out_shape=[
            jax.ShapeDtypeStruct((3 * SHARD, 1, D), F32),
            jax.ShapeDtypeStruct((SHARD, 1, D), F32),
            jax.ShapeDtypeStruct((1, SHARD), F32),
        ],
        scratch_shapes=[pltpu.VMEM((ROWS, D), F32)],
        name="finish",
    )(*(in_vmem(x) for x in pieces))
    return placed[None], conv.reshape(1, 3, SHARD, D), mid.reshape(1, SHARD, D), out


def solution(mesh):
    split = Mesh(
        mesh.devices.reshape(4, 4, 2, mesh.shape["head"]), ("dp_0", "dp_1", "dp_2", "head")
    )
    in_specs = (
        P("head", DP, None),
        P(DP),
        P(DP),
        P("head", None, DP, None),
        P("head", DP, None),
        P("head", DP),
    )
    out_specs = (P("head", DP, None), P("head", None, DP, None), P("head", DP, None), P("head", DP))
    return jax.shard_map(
        per_device, mesh=split, in_specs=in_specs, out_specs=out_specs, check_vma=False
    )
```

```python
import jax
import jax.numpy as jnp
from jax import lax
from jax.experimental import pallas as pl
from jax.experimental.pallas import tpu as pltpu
from jax.sharding import Mesh
from jax.sharding import PartitionSpec as P

DP = ("dp_0", "dp_1", "dp_2")
CHIPS = ("dp_0", "dp_1")
BF16 = jnp.bfloat16
F32 = jnp.float32
TAPS = 4
BT = 256
D = 384
SHARD = 12
EXTRA = 4 * SHARD
ROWS = 56
GROUP = 4
LOG_2 = 0.6931471805599453
VMEM_LIMIT = 20 * 1024 * 1024

IN_VMEM = pl.BlockSpec(memory_space=pltpu.VMEM)
IN_SMEM = pl.BlockSpec(memory_space=pltpu.SMEM)
IN_HBM = pl.BlockSpec(memory_space=pltpu.HBM)
OVER_LAST = (((1,), (1,)), ((), ()))
OVER_ROWS = (((0,), (0,)), ((), ()))


def swapped(x):
    return lax.ppermute(x, "dp_2", [(0, 1), (1, 0)])


def turned(x, axis, shift):
    count = lax.axis_size(axis)
    return lax.ppermute(x, axis, [(i, (i + shift) % count) for i in range(count)])


def total_over(x, axis):
    return sum((turned(x, axis, r) for r in range(1, lax.axis_size(axis))), x)


def scattered_sum(parts, axis, dim):
    count, index = lax.axis_size(axis), lax.axis_index(axis)

    def piece(shift):
        return lax.dynamic_index_in_dim(parts, (index + shift) % count, dim, keepdims=False)

    total = piece(0).astype(F32)
    for r in range(1, count):
        total += turned(piece(r), axis, r).astype(F32)
    return total


def gate(value):
    half = jnp.tanh(0.5 * value)
    tail = 0.8 * LOG_2 - (0.8 * LOG_2) * jnp.log2(1.0 + jnp.abs(half))
    return jnp.maximum(value, 0.2 * value) + tail, 0.6 + 0.4 * half


def row_mask(valid_ref, first, blocks):
    rows = lax.broadcasted_iota(jnp.int32, (blocks * BT, 1), 0)
    limit = jnp.full_like(rows, valid_ref[first])
    for j in range(1, blocks):
        limit = jnp.where(rows < j * BT, limit, j * BT + valid_ref[first + j])
    return rows < limit


def neighbours(x, place, last):
    count = x.shape[0]
    before = jnp.where(place == 0, 0.0, pltpu.roll(x, 1, 0))
    after = jnp.where(place == last, 0.0, pltpu.roll(x, count - 1, 0))
    return before.astype(BF16), after.astype(BF16)


def block_place(count):
    return lax.broadcasted_iota(jnp.int32, (count, 1), 0) % BT


def pack_kernel(
    valid_hbm, owner_hbm, conv_hbm, mid_hbm, out_hbm,
    copies_ref, valid_ref, owner_ref, conv_ref, mid_ref, out_ref, stage_ref, sems,
):
    sources = (valid_hbm, owner_hbm, conv_hbm, mid_hbm, out_hbm)
    targets = (valid_ref, owner_ref, conv_ref, mid_ref, out_ref)
    arrivals = [
        pltpu.make_async_copy(source, target, sems.at[i])
        for i, (source, target) in enumerate(zip(sources, targets))
    ]
    for copy in arrivals:
        copy.start()
    for copy in arrivals:
        copy.wait()
    local = valid_ref.shape[0]
    lane = lax.broadcasted_iota(jnp.int32, (1, D), 1)
    extras = jnp.zeros((1, D), F32)
    for j in range(local):
        extras = jnp.where(lane == SHARD + j, owner_ref[j].astype(F32), extras)
        extras = jnp.where(lane == SHARD + local + j, valid_ref[j].astype(F32), extras)
    stage_ref[EXTRA:ROWS, :] = jnp.zeros((ROWS - EXTRA, D), F32)
    for k in range(3):
        stage_ref[SHARD * k : SHARD * (k + 1), :] = conv_ref[k].astype(F32)
    stage_ref[3 * SHARD : EXTRA, :] = mid_ref[...].astype(F32)
    stage_ref[EXTRA : EXTRA + 1, :] = extras
    stage_ref[EXTRA : EXTRA + 1, 0:SHARD] = out_ref[...].astype(F32)
    packed = stage_ref[...].astype(BF16)
    for j in range(copies_ref.shape[0]):
        copies_ref[j] = packed


def chunks(local):
    half, quarter = local // 2, local // 4
    return ((0, half), (half, quarter), (half + quarter, quarter))


def state_rows(local):
    tokens = local * BT
    return pl.ds(0, tokens), pl.ds(tokens, 4 * D)


def weight(ref, k):
    return ref[k * D : (k + 1) * D, :]


def forward_kernel(
    valid_ref, owner_ref, core_ref, feats_ref, own_hbm, other_hbm,
    low_out, mid_grad_out, state_ref, sums_ref, out_w_ref, extras_ref, totals_ref,
    raw_ref, own_ref, other_ref, low_ref, mid_grad_ref, wide_ref, sems, out_sems, weight_sems,
):
    local = valid_ref.shape[0]
    slope_ref, weights_ref = (state_ref.at[rows] for rows in state_rows(local))
    arrivals = [
        pltpu.make_async_copy(own_hbm, own_ref, weight_sems.at[0]),
        pltpu.make_async_copy(other_hbm, other_ref, weight_sems.at[1]),
    ]
    for n, (j, group) in enumerate(chunks(local)):
        rows = pl.ds(j * BT, group * BT)
        arrivals.append(pltpu.make_async_copy(feats_ref.at[rows], raw_ref.at[rows], sems.at[n]))
    for copy in arrivals:
        copy.start()

    def unpack(parity, source):
        for chip in range(source.shape[0]):
            tile = source[chip].astype(F32)
            device = 2 * chip + parity
            at = SHARD * device
            for k in range(4):
                wide_ref[k * D + at : k * D + at + SHARD, :] = tile[SHARD * k : SHARD * (k + 1)]
            extras_ref[device : device + 1, :] = tile[EXTRA : EXTRA + 1, :128]

    for copy in arrivals[:2]:
        copy.wait()

    @pl.when(core_ref[0] == 0)
    def _():
        unpack(0, own_ref)
        unpack(1, other_ref)

    @pl.when(core_ref[0] == 1)
    def _():
        unpack(1, own_ref)
        unpack(0, other_ref)

    weights_ref[...] = wide_ref[...].astype(BF16)
    devices = extras_ref.shape[0]
    column = lax.broadcasted_iota(jnp.int32, (128, D), 1).astype(F32)
    place = lax.broadcasted_iota(jnp.int32, (128, D), 0).astype(F32)
    home = jnp.floor((column + 0.5) * (1.0 / SHARD))
    pick = jnp.where(column - SHARD * home == place, 1.0, 0.0).astype(BF16)
    spread = jnp.dot(extras_ref[...].astype(BF16), pick, preferred_element_type=F32)
    row = lax.broadcasted_iota(jnp.int32, (devices, D), 0).astype(F32)
    out_w = jnp.sum(jnp.where(home[:devices] == row, spread, 0.0), 0, keepdims=True)
    out_w_ref[...] = out_w

    lane = lax.broadcasted_iota(jnp.int32, (1, 128), 1)
    totals = jnp.zeros((1, 128), F32)
    departures = []
    for n, (j, group) in enumerate(chunks(local)):
        rows = pl.ds(j * BT, group * BT)
        arrivals[2 + n].wait()
        place = block_place(group * BT)
        keep = row_mask(valid_ref, j, group)
        masked = jnp.where(keep, raw_ref[rows, :].astype(F32), 0.0)
        before, after = neighbours(masked, place, BT - 1)
        first = jnp.dot(before, weight(weights_ref, 0), preferred_element_type=F32)
        first += jnp.dot(
            masked.astype(BF16), weight(weights_ref, 1), preferred_element_type=F32
        )
        first += jnp.dot(after, weight(weights_ref, 2), preferred_element_type=F32)
        first_act, slope = gate(first)
        low = first_act.astype(BF16)
        low_ref[rows, :] = low
        copy = pltpu.make_async_copy(low_ref.at[rows], low_out.at[rows], out_sems.at[0, n])
        copy.start()
        departures.append(copy)
        slope_ref[rows, :] = slope.astype(BF16)
        second = jnp.dot(low, weight(weights_ref, 3), preferred_element_type=F32)
        second_act, second_slope = gate(second)
        mid_grad_ref[rows, :] = jnp.where(keep, out_w * second_slope, 0.0).astype(BF16)
        copy = pltpu.make_async_copy(
            mid_grad_ref.at[rows], mid_grad_out.at[rows], out_sems.at[1, n]
        )
        copy.start()
        departures.append(copy)
        total = jnp.where(keep, second_act + first_act, 0.0)
        for i in range(group):
            block = jnp.sum(total[i * BT : (i + 1) * BT], 0, keepdims=True)
            sums_ref[j + i : j + i + 1, :] = block
            block_sum = jnp.sum(block * out_w, 1, keepdims=True)
            totals += jnp.where(lane == owner_ref[j + i], block_sum, 0.0)
    for device in range(devices):
        totals_ref[device] = totals
    for copy in departures:
        copy.wait()


def backward_kernel(
    valid_ref, owner_ref, mid_grad_hbm, state_ref, out_w_ref,
    first_grad_out, slots_ref, mid_grad_ref, first_grad_ref, ready_ref, sems, out_sems, in_sems,
):
    local = valid_ref.shape[0]
    slope_ref, weights_ref = (state_ref.at[rows] for rows in state_rows(local))
    place = block_place(GROUP * BT)
    arrivals, copies = [], []
    for j in range(0, local, GROUP):
        rows = pl.ds(j * BT, GROUP * BT)
        copy = pltpu.make_async_copy(
            mid_grad_hbm.at[rows], mid_grad_ref.at[rows], in_sems.at[j // GROUP]
        )
        copy.start()
        arrivals.append(copy)
    for j in range(0, local, GROUP):
        rows = pl.ds(j * BT, GROUP * BT)
        arrivals[j // GROUP].wait()
        keep = row_mask(valid_ref, j, GROUP)
        grad = lax.dot_general(
            mid_grad_ref[rows, :], weight(weights_ref, 3), OVER_LAST, preferred_element_type=F32
        )
        grad = (grad + jnp.where(keep, out_w_ref[...], 0.0)) * slope_ref[rows, :].astype(F32)
        before, after = neighbours(grad, place, BT - 1)
        low = grad.astype(BF16)
        first_grad_ref[rows, :] = low
        total = lax.dot_general(low, weight(weights_ref, 1), OVER_LAST, preferred_element_type=F32)
        total += lax.dot_general(
            after, weight(weights_ref, 0), OVER_LAST, preferred_element_type=F32
        )
        total += lax.dot_general(
            before, weight(weights_ref, 2), OVER_LAST, preferred_element_type=F32
        )
        total = jnp.where(keep, total, 0.0).astype(BF16)
        for i in range(GROUP):
            ready_ref[j + i] = total[i * BT : (i + 1) * BT]
            copy = pltpu.make_async_copy(
                ready_ref.at[j + i], slots_ref.at[owner_ref[j + i]], sems.at[j + i]
            )
            copy.start()
            copies.append(copy)
        copy = pltpu.make_async_copy(
            first_grad_ref.at[rows], first_grad_out.at[rows], out_sems.at[j // GROUP]
        )
        copy.start()
        copies.append(copy)
    for copy in copies:
        copy.wait()


def weight_kernel(
    valid_ref, factor_ref, feats_hbm, low_hbm, mid_grad_hbm, first_grad_hbm, sums_ref,
    parts_ref, feats_ref, low_ref, mid_grad_ref, first_grad_ref, conv_ref, mid_ref, stage_ref, sems,
):
    local = valid_ref.shape[0]
    pairs = (
        (feats_hbm, feats_ref),
        (low_hbm, low_ref),
        (mid_grad_hbm, mid_grad_ref),
        (first_grad_hbm, first_grad_ref),
    )
    arrivals = []
    for j in range(local):
        rows = pl.ds(j * BT, BT)
        arrivals.append(
            [
                pltpu.make_async_copy(source.at[rows], target.at[rows], sems.at[i, j])
                for i, (source, target) in enumerate(pairs)
            ]
        )
        for copy in arrivals[j]:
            copy.start()
    out = jnp.zeros((1, D), F32)
    place = block_place(BT)
    for j in range(local):
        rows = pl.ds(j * BT, BT)
        for copy in arrivals[j]:
            copy.wait()
        factor = factor_ref[j]
        out += sums_ref[j : j + 1, :] * factor
        grad = first_grad_ref[rows, :].astype(F32) * factor
        before, after = neighbours(grad, place, BT - 1)
        mid_grad = (mid_grad_ref[rows, :].astype(F32) * factor).astype(BF16)
        keep = row_mask(valid_ref, j, 1)
        masked = jnp.where(keep, feats_ref[rows, :].astype(F32), 0.0).astype(BF16)
        terms = [
            lax.dot_general(masked, x, OVER_ROWS, preferred_element_type=F32)
            for x in (after, grad.astype(BF16), before)
        ]
        mid = lax.dot_general(low_ref[rows, :], mid_grad, OVER_ROWS, preferred_element_type=F32)
        for k in range(3):
            conv_ref[k] = terms[k] if j == 0 else conv_ref[k] + terms[k]
        mid_ref[...] = mid if j == 0 else mid_ref[...] + mid

    devices = parts_ref.shape[0]
    column = lax.broadcasted_iota(jnp.int32, (D, D), 0).astype(F32)
    place = lax.broadcasted_iota(jnp.int32, (D, D), 1).astype(F32)
    home = jnp.floor((column + 0.5) * (1.0 / SHARD))
    pick = jnp.where(column - SHARD * home == place, 1.0, 0.0).astype(BF16)
    device = lax.broadcasted_iota(jnp.int32, (devices, D), 0).astype(F32)
    lane = lax.broadcasted_iota(jnp.int32, (devices, D), 1).astype(F32)
    mine = jnp.floor((lane + 0.5) * (1.0 / SHARD)) == device
    out_rows = jnp.where(mine, out, 0.0).astype(BF16)
    out_rows = jnp.dot(out_rows, pick, preferred_element_type=F32)
    stage_ref[EXTRA:ROWS, :] = jnp.zeros((ROWS - EXTRA, D), F32)
    for d in range(devices):
        at = SHARD * d
        for k in range(3):
            stage_ref[SHARD * k : SHARD * (k + 1), :] = conv_ref[k, at : at + SHARD, :]
        stage_ref[3 * SHARD : EXTRA, :] = mid_ref[at : at + SHARD, :]
        stage_ref[EXTRA : EXTRA + 1, :] = out_rows[d : d + 1, :]
        parts_ref[d] = stage_ref[...].astype(BF16)


def finish_kernel(pieces_ref, conv_ref, mid_ref, out_ref, total_ref):
    total = pieces_ref[0].astype(F32)
    for i in range(1, pieces_ref.shape[0]):
        total += pieces_ref[i].astype(F32)
    total_ref[...] = total * (1.0 / BT)
    for row in range(3 * SHARD):
        conv_ref[row] = total_ref[row : row + 1, :]
    for row in range(SHARD):
        mid_ref[row] = total_ref[3 * SHARD + row : 3 * SHARD + row + 1, :]
    out_ref[...] = total_ref[EXTRA : EXTRA + 1, 0:SHARD]


def place_kernel(
    source_ref, count_ref, factor_ref, received_ref, placed_ref, raw_ref, ready_ref, in_sems, out_sems
):
    capacity = source_ref.shape[0]
    arrivals, departures = [], []
    for slot in range(capacity):
        copy = pltpu.make_async_copy(
            received_ref.at[source_ref[slot]], raw_ref.at[slot], in_sems.at[slot]
        )
        copy.start()
        arrivals.append(copy)
    for slot in range(capacity):
        arrivals[slot].wait()
        factor = jnp.where(slot < count_ref[0], factor_ref[0], 0.0)
        ready_ref[slot] = (raw_ref[slot].astype(F32) * factor).astype(BF16)
        rows = pl.ds(slot * BT, BT)
        copy = pltpu.make_async_copy(ready_ref.at[slot], placed_ref.at[rows], out_sems.at[slot])
        copy.start()
        departures.append(copy)
    for copy in departures:
        copy.wait()


def in_hbm(x):
    return pltpu.with_memory_space_constraint(x, pltpu.HBM)


def in_vmem(x):
    return pltpu.with_memory_space_constraint(x, pltpu.VMEM)


def call(kernel, name, in_specs, outs, scratch=(), megabytes=0):
    return pl.pallas_call(
        kernel,
        in_specs=in_specs,
        out_specs=[spec for spec, _, _ in outs],
        out_shape=[
            (pltpu.HBM if spec is IN_HBM else pltpu.VMEM)(shape, dtype) for spec, shape, dtype in outs
        ],
        scratch_shapes=list(scratch),
        compiler_params=pltpu.CompilerParams(vmem_limit_bytes=VMEM_LIMIT),
        cost_estimate=pl.CostEstimate(
            flops=0, transcendentals=0, bytes_accessed=megabytes * 1024 * 1024
        ),
        name=name,
    )


def per_device(feats, valid, owner_map, w_conv, w_mid, w_out):
    local = owner_map.shape[0]
    devices = lax.axis_size(DP)
    chips = devices // 2
    capacity = devices // 2
    tokens_here = local * BT
    me = lax.axis_index(DP)
    core = lax.axis_index("dp_2").astype(jnp.int32).reshape(1)
    images = jnp.arange(devices, dtype=jnp.int32)

    (copies,) = call(
        pack_kernel,
        "pack",
        [IN_HBM] * 5,
        [(IN_VMEM, (chips, ROWS, D), BF16)],
        [
            pltpu.SMEM((local,), jnp.int32),
            pltpu.SMEM((local,), jnp.int32),
            pltpu.VMEM((3, SHARD, D), BF16),
            pltpu.VMEM((SHARD, D), BF16),
            pltpu.VMEM((1, SHARD), BF16),
            pltpu.VMEM((ROWS, D), F32),
            pltpu.SemaphoreType.DMA((5,)),
        ],
    )(*(in_hbm(x) for x in (valid, owner_map, w_conv[0], w_mid[0], w_out)))
    own = lax.all_to_all(copies, CHIPS, split_axis=0, concat_axis=0, tiled=True)
    other = swapped(own)

    low, mid_grad, state, sums, out_w, extras, totals = call(
        forward_kernel,
        "forward",
        [IN_SMEM, IN_SMEM, IN_SMEM, IN_HBM, IN_HBM, IN_HBM],
        [
            (IN_HBM, (tokens_here, D), BF16),
            (IN_HBM, (tokens_here, D), BF16),
            (IN_VMEM, (tokens_here + 4 * D, D), BF16),
            (IN_VMEM, (local, D), F32),
            (IN_VMEM, (1, D), F32),
            (IN_VMEM, (devices, 128), F32),
            (IN_VMEM, (devices, 1, 128), F32),
        ],
        [
            pltpu.VMEM((tokens_here, D), BF16),
            pltpu.VMEM((chips, ROWS, D), BF16),
            pltpu.VMEM((chips, ROWS, D), BF16),
            pltpu.VMEM((tokens_here, D), BF16),
            pltpu.VMEM((tokens_here, D), BF16),
            pltpu.VMEM((4 * D, D), F32),
            pltpu.SemaphoreType.DMA((3,)),
            pltpu.SemaphoreType.DMA((2, 3)),
            pltpu.SemaphoreType.DMA((2,)),
        ],
    )(valid, owner_map, core, in_hbm(feats[0]), in_hbm(own), in_hbm(other))

    totals = lax.all_to_all(totals, DP, split_axis=0, concat_axis=0, tiled=True)

    first_grad, slots = call(
        backward_kernel,
        "backward",
        [IN_SMEM, IN_SMEM, IN_HBM, IN_VMEM, IN_VMEM],
        [
            (IN_HBM, (tokens_here, D), BF16),
            (IN_HBM, (devices, BT, D), BF16),
        ],
        [
            pltpu.VMEM((tokens_here, D), BF16),
            pltpu.VMEM((tokens_here, D), BF16),
            pltpu.VMEM((local, BT, D), BF16),
            pltpu.SemaphoreType.DMA((local,)),
            pltpu.SemaphoreType.DMA((local // GROUP,)),
            pltpu.SemaphoreType.DMA((local // GROUP,)),
        ],
        megabytes=24,
    )(valid, owner_map, in_hbm(mid_grad), in_vmem(state), in_vmem(out_w))

    slots, totals = lax.optimization_barrier((slots, totals))
    received = lax.all_to_all(slots, DP, split_axis=0, concat_axis=0, tiled=True)

    totals = total_over(jnp.sum(totals[:, 0, :devices], 0)[None], "head")[0]
    members = (owner_map[:, None] == images[None, :]).astype(F32)
    owners = extras[:, SHARD : SHARD + local].astype(jnp.int32)
    valids = extras[:, SHARD + local : SHARD + 2 * local]
    tokens = jnp.sum(jnp.where(owners[:, :, None] == images, valids[:, :, None], 0.0), (0, 1))
    norm = jnp.sqrt(TAPS * tokens)
    factor = -BT * jax.nn.sigmoid(-totals / norm) / norm
    block_factor = jnp.sum(members * factor[None, :], 1)
    own_factor = jnp.sum(jnp.where(images == me, factor, 0.0)).reshape(1)

    (parts,) = call(
        weight_kernel,
        "weight_grads",
        [IN_SMEM, IN_SMEM, IN_HBM, IN_HBM, IN_HBM, IN_HBM, IN_VMEM],
        [(IN_VMEM, (devices, ROWS, D), BF16)],
        [pltpu.VMEM((tokens_here, D), BF16)] * 4
        + [
            pltpu.VMEM((3, D, D), F32),
            pltpu.VMEM((D, D), F32),
            pltpu.VMEM((ROWS, D), F32),
            pltpu.SemaphoreType.DMA((4, local)),
        ],
        megabytes=16,
    )(
        valid, block_factor, in_hbm(feats[0]), in_hbm(low), in_hbm(mid_grad),
        in_hbm(first_grad), in_vmem(sums),
    )
    parts = scattered_sum(parts.reshape(chips, 2, ROWS, D), "dp_2", 1).astype(BF16)
    present = jnp.sum((owners == me).astype(jnp.int32), 1)
    rank = jnp.sum(jnp.where(images[None, :] < images[:, None], present[None, :], 0), 1)
    count = jnp.sum(present)
    wanted = jnp.minimum(jnp.arange(capacity, dtype=jnp.int32), count - 1)
    hit = (rank[None, :] == wanted[:, None]) & (present[None, :] > 0)
    source = jnp.sum(jnp.where(hit, images[None, :], 0), 1).astype(jnp.int32)
    table = (source, count.reshape(1), own_factor)
    parts, received, table = lax.optimization_barrier((parts, received, table))
    pieces = lax.all_to_all(parts, CHIPS, split_axis=0, concat_axis=0, tiled=True)
    (placed,) = call(
        place_kernel,
        "place",
        [IN_SMEM, IN_SMEM, IN_SMEM, IN_HBM],
        [(IN_HBM, (capacity * BT, D), BF16)],
        [
            pltpu.VMEM((capacity, BT, D), BF16),
            pltpu.VMEM((capacity, BT, D), BF16),
            pltpu.SemaphoreType.DMA((capacity,)),
            pltpu.SemaphoreType.DMA((capacity,)),
        ],
        megabytes=24,
    )(*table, in_hbm(received))

    conv, mid, out = pl.pallas_call(
        finish_kernel,
        in_specs=[IN_VMEM],
        out_specs=[IN_VMEM] * 3,
        out_shape=[
            jax.ShapeDtypeStruct((3 * SHARD, 1, D), F32),
            jax.ShapeDtypeStruct((SHARD, 1, D), F32),
            jax.ShapeDtypeStruct((1, SHARD), F32),
        ],
        scratch_shapes=[pltpu.VMEM((ROWS, D), F32)],
        name="finish",
    )(in_vmem(pieces))
    return placed[None], conv.reshape(1, 3, SHARD, D), mid.reshape(1, SHARD, D), out


def solution(mesh):
    split = Mesh(
        mesh.devices.reshape(4, 4, 2, mesh.shape["head"]), ("dp_0", "dp_1", "dp_2", "head")
    )
    in_specs = (
        P("head", DP, None),
        P(DP),
        P(DP),
        P("head", None, DP, None),
        P("head", DP, None),
        P("head", DP),
    )
    out_specs = (P("head", DP, None), P("head", None, DP, None), P("head", DP, None), P("head", DP))
    return jax.shard_map(
        per_device, mesh=split, in_specs=in_specs, out_specs=out_specs, check_vma=False
    )
```

```python
import jax
import jax.numpy as jnp
from jax import lax
from jax.experimental import pallas as pl
from jax.experimental.pallas import tpu as pltpu
from jax.sharding import Mesh
from jax.sharding import PartitionSpec as P

DP = ("dp_0", "dp_1", "dp_2")
CHIPS = ("dp_0", "dp_1")
BF16 = jnp.bfloat16
F32 = jnp.float32
TAPS = 4
BT = 256
D = 384
SHARD = 12
EXTRA = 4 * SHARD
ROWS = 56
GROUP = 4
HALF = BT // 2
LOG_2 = 0.6931471805599453
VMEM_LIMIT = 20 * 1024 * 1024

IN_VMEM = pl.BlockSpec(memory_space=pltpu.VMEM)
IN_SMEM = pl.BlockSpec(memory_space=pltpu.SMEM)
IN_HBM = pl.BlockSpec(memory_space=pltpu.HBM)
OVER_LAST = (((1,), (1,)), ((), ()))
OVER_ROWS = (((0,), (0,)), ((), ()))


def swapped(x):
    return lax.ppermute(x, "dp_2", [(0, 1), (1, 0)])


def turned(x, axis, shift):
    count = lax.axis_size(axis)
    return lax.ppermute(x, axis, [(i, (i + shift) % count) for i in range(count)])


def total_over(x, axis):
    return sum((turned(x, axis, r) for r in range(1, lax.axis_size(axis))), x)


def shares(parts, axis, dim):
    count, index = lax.axis_size(axis), lax.axis_index(axis)

    def share(shift):
        return lax.dynamic_index_in_dim(parts, (index + shift) % count, dim, keepdims=False)

    return [share(0)] + [share(r).astype(BF16) for r in range(1, count)]


def delivered(own, *others, axis):
    return [own] + [turned(other, axis, r) for r, other in enumerate(others, 1)]


def added(pieces):
    return sum(piece.astype(F32) for piece in pieces)


def gate(value):
    half = jnp.tanh(0.5 * value)
    tail = 0.8 * LOG_2 - (0.8 * LOG_2) * jnp.log2(1.0 + jnp.abs(half))
    return jnp.maximum(value, 0.2 * value) + tail, 0.6 + 0.4 * half


def row_mask(valid_ref, first, blocks):
    rows = lax.broadcasted_iota(jnp.int32, (blocks * BT, 1), 0)
    limit = jnp.full_like(rows, valid_ref[first])
    for j in range(1, blocks):
        limit = jnp.where(rows < j * BT, limit, j * BT + valid_ref[first + j])
    return rows < limit


def neighbours(x, place, last):
    count = x.shape[0]
    before = jnp.where(place == 0, 0.0, pltpu.roll(x, 1, 0))
    after = jnp.where(place == last, 0.0, pltpu.roll(x, count - 1, 0))
    return before.astype(BF16), after.astype(BF16)


def block_place(count):
    return lax.broadcasted_iota(jnp.int32, (count, 1), 0) % BT


def pack_kernel(
    valid_hbm, owner_hbm, conv_hbm, mid_hbm, out_hbm,
    copies_ref, valid_ref, owner_ref, conv_ref, mid_ref, out_ref, stage_ref, sems,
):
    sources = (valid_hbm, owner_hbm, conv_hbm, mid_hbm, out_hbm)
    targets = (valid_ref, owner_ref, conv_ref, mid_ref, out_ref)
    arrivals = [
        pltpu.make_async_copy(source, target, sems.at[i])
        for i, (source, target) in enumerate(zip(sources, targets))
    ]
    for copy in arrivals:
        copy.start()
    for copy in arrivals:
        copy.wait()
    local = valid_ref.shape[0]
    lane = lax.broadcasted_iota(jnp.int32, (1, D), 1)
    extras = jnp.zeros((1, D), F32)
    for j in range(local):
        extras = jnp.where(lane == SHARD + j, owner_ref[j].astype(F32), extras)
        extras = jnp.where(lane == SHARD + local + j, valid_ref[j].astype(F32), extras)
    stage_ref[EXTRA:ROWS, :] = jnp.zeros((ROWS - EXTRA, D), F32)
    for k in range(3):
        stage_ref[SHARD * k : SHARD * (k + 1), :] = conv_ref[k].astype(F32)
    stage_ref[3 * SHARD : EXTRA, :] = mid_ref[...].astype(F32)
    stage_ref[EXTRA : EXTRA + 1, :] = extras
    stage_ref[EXTRA : EXTRA + 1, 0:SHARD] = out_ref[...].astype(F32)
    packed = stage_ref[...].astype(BF16)
    for j in range(copies_ref.shape[0]):
        copies_ref[j] = packed


def chunks(local):
    half, quarter = local // 2, local // 4
    return ((0, half), (half, quarter), (half + quarter, quarter))


def state_rows(local):
    tokens = local * BT
    return pl.ds(0, tokens), pl.ds(tokens, 4 * D)


def weight(ref, k):
    return ref[k * D : (k + 1) * D, :]


def forward_kernel(
    valid_ref, owner_ref, core_ref, feats_ref, own_hbm, other_hbm,
    low_out, mid_grad_out, weights_out, state_ref, sums_ref, out_w_ref, extras_ref, totals_ref,
    raw_ref, own_ref, other_ref, low_ref, mid_grad_ref, wide_ref, sems, out_sems, weight_sems,
):
    local = valid_ref.shape[0]
    slope_ref, weights_ref = (state_ref.at[rows] for rows in state_rows(local))
    arrivals = [
        pltpu.make_async_copy(own_hbm, own_ref, weight_sems.at[0]),
        pltpu.make_async_copy(other_hbm, other_ref, weight_sems.at[1]),
    ]
    for n, (j, group) in enumerate(chunks(local)):
        rows = pl.ds(j * BT, group * BT)
        arrivals.append(pltpu.make_async_copy(feats_ref.at[rows], raw_ref.at[rows], sems.at[n]))
    for copy in arrivals:
        copy.start()

    def unpack(parity, source):
        for chip in range(source.shape[0]):
            tile = source[chip].astype(F32)
            device = 2 * chip + parity
            at = SHARD * device
            for k in range(4):
                wide_ref[k * D + at : k * D + at + SHARD, :] = tile[SHARD * k : SHARD * (k + 1)]
            extras_ref[device : device + 1, :] = tile[EXTRA : EXTRA + 1, :128]

    for copy in arrivals[:2]:
        copy.wait()

    @pl.when(core_ref[0] == 0)
    def _():
        unpack(0, own_ref)
        unpack(1, other_ref)

    @pl.when(core_ref[0] == 1)
    def _():
        unpack(1, own_ref)
        unpack(0, other_ref)

    weights_ref[...] = wide_ref[...].astype(BF16)
    departures = [pltpu.make_async_copy(weights_ref, weights_out, weight_sems.at[0])]
    departures[0].start()
    devices = extras_ref.shape[0]
    column = lax.broadcasted_iota(jnp.int32, (128, D), 1).astype(F32)
    place = lax.broadcasted_iota(jnp.int32, (128, D), 0).astype(F32)
    home = jnp.floor((column + 0.5) * (1.0 / SHARD))
    pick = jnp.where(column - SHARD * home == place, 1.0, 0.0).astype(BF16)
    spread = jnp.dot(extras_ref[...].astype(BF16), pick, preferred_element_type=F32)
    row = lax.broadcasted_iota(jnp.int32, (devices, D), 0).astype(F32)
    out_w = jnp.sum(jnp.where(home[:devices] == row, spread, 0.0), 0, keepdims=True)
    out_w_ref[...] = out_w

    lane = lax.broadcasted_iota(jnp.int32, (1, 128), 1)
    totals = jnp.zeros((1, 128), F32)
    for n, (j, group) in enumerate(chunks(local)):
        rows = pl.ds(j * BT, group * BT)
        arrivals[2 + n].wait()
        place = block_place(group * BT)
        keep = row_mask(valid_ref, j, group)
        masked = jnp.where(keep, raw_ref[rows, :].astype(F32), 0.0)
        before, after = neighbours(masked, place, BT - 1)
        first = jnp.dot(before, weight(weights_ref, 0), preferred_element_type=F32)
        first += jnp.dot(
            masked.astype(BF16), weight(weights_ref, 1), preferred_element_type=F32
        )
        first += jnp.dot(after, weight(weights_ref, 2), preferred_element_type=F32)
        first_act, slope = gate(first)
        low = first_act.astype(BF16)
        low_ref[rows, :] = low
        copy = pltpu.make_async_copy(low_ref.at[rows], low_out.at[rows], out_sems.at[0, n])
        copy.start()
        departures.append(copy)
        slope_ref[rows, :] = slope.astype(BF16)
        second = jnp.dot(low, weight(weights_ref, 3), preferred_element_type=F32)
        second_act, second_slope = gate(second)
        mid_grad_ref[rows, :] = jnp.where(keep, out_w * second_slope, 0.0).astype(BF16)
        copy = pltpu.make_async_copy(
            mid_grad_ref.at[rows], mid_grad_out.at[rows], out_sems.at[1, n]
        )
        copy.start()
        departures.append(copy)
        total = jnp.where(keep, second_act + first_act, 0.0)
        for i in range(group):
            block = jnp.sum(total[i * BT : (i + 1) * BT], 0, keepdims=True)
            sums_ref[j + i : j + i + 1, :] = block
            block_sum = jnp.sum(block * out_w, 1, keepdims=True)
            totals += jnp.where(lane == owner_ref[j + i], block_sum, 0.0)
    for chip in range(devices // 2):
        totals_ref[chip] = totals
    for copy in departures:
        copy.wait()


def input_grad(grad, weights_ref, keep, half):
    blocks = grad.shape[0] // BT
    before, after = neighbours(grad, block_place(blocks * BT), BT - 1)

    def part(x):
        starts = [i * BT + half * HALF for i in range(blocks)]
        return jnp.concatenate([x[at : at + HALF] for at in starts], axis=0)

    def product(x, k):
        return lax.dot_general(
            part(x), weight(weights_ref, k), OVER_LAST, preferred_element_type=F32
        )

    total = product(grad.astype(BF16), 1) + product(after, 0) + product(before, 2)
    return jnp.where(part(keep) > 0, total, 0.0).astype(BF16)


def send_half(total, first, ready_ref, slots_ref, owner_ref, sems):
    copies = []
    for i in range(total.shape[0] // HALF):
        ready_ref[first + i] = total[i * HALF : (i + 1) * HALF]
        copy = pltpu.make_async_copy(
            ready_ref.at[first + i], slots_ref.at[owner_ref[first + i]], sems.at[first + i]
        )
        copy.start()
        copies.append(copy)
    return copies


def backward_kernel(
    valid_ref, owner_ref, mid_grad_hbm, state_ref, out_w_ref,
    first_grad_out, slots_ref, mid_grad_ref, first_grad_ref, ready_ref, sems, out_sems, in_sems,
):
    local = valid_ref.shape[0]
    slope_ref, weights_ref = (state_ref.at[rows] for rows in state_rows(local))
    arrivals, copies = [], []
    for j in range(0, local, GROUP):
        rows = pl.ds(j * BT, GROUP * BT)
        copy = pltpu.make_async_copy(
            mid_grad_hbm.at[rows], mid_grad_ref.at[rows], in_sems.at[j // GROUP]
        )
        copy.start()
        arrivals.append(copy)
    for j in range(0, local, GROUP):
        rows = pl.ds(j * BT, GROUP * BT)
        arrivals[j // GROUP].wait()
        keep = row_mask(valid_ref, j, GROUP)
        grad = lax.dot_general(
            mid_grad_ref[rows, :], weight(weights_ref, 3), OVER_LAST, preferred_element_type=F32
        )
        grad = (grad + jnp.where(keep, out_w_ref[...], 0.0)) * slope_ref[rows, :].astype(F32)
        first_grad_ref[rows, :] = grad.astype(BF16)
        copy = pltpu.make_async_copy(
            first_grad_ref.at[rows], first_grad_out.at[rows], out_sems.at[j // GROUP]
        )
        copy.start()
        copies.append(copy)
        total = input_grad(grad, weights_ref, keep.astype(F32), 0)
        copies += send_half(total, j, ready_ref, slots_ref, owner_ref, sems)
    for copy in copies:
        copy.wait()


def second_half_kernel(
    valid_ref, owner_ref, first_grad_hbm, weights_hbm,
    slots_ref, first_grad_ref, weights_ref, ready_ref, sems, in_sems,
):
    local = valid_ref.shape[0]
    arrivals = [
        pltpu.make_async_copy(first_grad_hbm, first_grad_ref, in_sems.at[0]),
        pltpu.make_async_copy(weights_hbm, weights_ref, in_sems.at[1]),
    ]
    for copy in arrivals:
        copy.start()
    for copy in arrivals:
        copy.wait()
    copies = []
    for j in range(0, local, GROUP):
        rows = pl.ds(j * BT, GROUP * BT)
        keep = row_mask(valid_ref, j, GROUP).astype(F32)
        total = input_grad(first_grad_ref[rows, :].astype(F32), weights_ref, keep, 1)
        copies += send_half(total, j, ready_ref, slots_ref, owner_ref, sems)
    for copy in copies:
        copy.wait()


def weight_kernel(
    valid_ref, factor_ref, feats_hbm, low_hbm, mid_grad_hbm, first_grad_hbm, sums_ref,
    parts_ref, feats_ref, low_ref, mid_grad_ref, first_grad_ref, conv_ref, mid_ref, stage_ref, sems,
):
    local = valid_ref.shape[0]
    pairs = (
        (feats_hbm, feats_ref),
        (low_hbm, low_ref),
        (mid_grad_hbm, mid_grad_ref),
        (first_grad_hbm, first_grad_ref),
    )
    arrivals = []
    for j in range(local):
        rows = pl.ds(j * BT, BT)
        arrivals.append(
            [
                pltpu.make_async_copy(source.at[rows], target.at[rows], sems.at[i, j])
                for i, (source, target) in enumerate(pairs)
            ]
        )
        for copy in arrivals[j]:
            copy.start()
    out = jnp.zeros((1, D), F32)
    place = block_place(BT)
    for j in range(local):
        rows = pl.ds(j * BT, BT)
        for copy in arrivals[j]:
            copy.wait()
        factor = factor_ref[j]
        out += sums_ref[j : j + 1, :] * factor
        grad = first_grad_ref[rows, :].astype(F32) * factor
        before, after = neighbours(grad, place, BT - 1)
        mid_grad = (mid_grad_ref[rows, :].astype(F32) * factor).astype(BF16)
        keep = row_mask(valid_ref, j, 1)
        masked = jnp.where(keep, feats_ref[rows, :].astype(F32), 0.0).astype(BF16)
        terms = [
            lax.dot_general(masked, x, OVER_ROWS, preferred_element_type=F32)
            for x in (after, grad.astype(BF16), before)
        ]
        mid = lax.dot_general(low_ref[rows, :], mid_grad, OVER_ROWS, preferred_element_type=F32)
        for k in range(3):
            conv_ref[k] = terms[k] if j == 0 else conv_ref[k] + terms[k]
        mid_ref[...] = mid if j == 0 else mid_ref[...] + mid

    devices = parts_ref.shape[0]
    column = lax.broadcasted_iota(jnp.int32, (D, D), 0).astype(F32)
    place = lax.broadcasted_iota(jnp.int32, (D, D), 1).astype(F32)
    home = jnp.floor((column + 0.5) * (1.0 / SHARD))
    pick = jnp.where(column - SHARD * home == place, 1.0, 0.0).astype(BF16)
    device = lax.broadcasted_iota(jnp.int32, (devices, D), 0).astype(F32)
    lane = lax.broadcasted_iota(jnp.int32, (devices, D), 1).astype(F32)
    mine = jnp.floor((lane + 0.5) * (1.0 / SHARD)) == device
    out_rows = jnp.where(mine, out, 0.0).astype(BF16)
    out_rows = jnp.dot(out_rows, pick, preferred_element_type=F32)
    stage_ref[EXTRA:ROWS, :] = jnp.zeros((ROWS - EXTRA, D), F32)
    for d in range(devices):
        at = SHARD * d
        for k in range(3):
            stage_ref[SHARD * k : SHARD * (k + 1), :] = conv_ref[k, at : at + SHARD, :]
        stage_ref[3 * SHARD : EXTRA, :] = mid_ref[at : at + SHARD, :]
        stage_ref[EXTRA : EXTRA + 1, :] = out_rows[d : d + 1, :]
        parts_ref[d] = stage_ref[...].astype(BF16)


def finish_kernel(own_ref, first_ref, second_ref, third_ref, conv_ref, mid_ref, out_ref, total_ref):
    total = own_ref[...]
    for piece in (first_ref, second_ref, third_ref):
        total += piece[...].astype(F32)
    total_ref[...] = total * (1.0 / BT)
    for row in range(3 * SHARD):
        conv_ref[row] = total_ref[row : row + 1, :]
    for row in range(SHARD):
        mid_ref[row] = total_ref[3 * SHARD + row : 3 * SHARD + row + 1, :]
    out_ref[...] = total_ref[EXTRA : EXTRA + 1, 0:SHARD]


def place_half(half, read, count_ref, factor_ref, placed_ref, ready_ref, sems):
    copies = []
    for slot in range(ready_ref.shape[0]):
        factor = jnp.where(slot < count_ref[0], factor_ref[0], 0.0)
        ready_ref[slot] = (read(slot).astype(F32) * factor).astype(BF16)
        rows = pl.ds(slot * BT + half * HALF, HALF)
        copy = pltpu.make_async_copy(ready_ref.at[slot], placed_ref.at[rows], sems.at[slot])
        copy.start()
        copies.append(copy)
    for copy in copies:
        copy.wait()


def place_first_kernel(
    source_ref, count_ref, factor_ref, received_hbm, placed_ref, ready_ref, sems, raw_ref, in_sems
):
    arrivals = []
    for slot in range(raw_ref.shape[0]):
        copy = pltpu.make_async_copy(
            received_hbm.at[source_ref[slot]], raw_ref.at[slot], in_sems.at[slot]
        )
        copy.start()
        arrivals.append(copy)

    def read(slot):
        arrivals[slot].wait()
        return raw_ref[slot]

    place_half(0, read, count_ref, factor_ref, placed_ref, ready_ref, sems)


def place_second_kernel(
    source_ref, count_ref, factor_ref, received_ref, begun_ref, placed_ref, ready_ref, sems
):
    def read(slot):
        return received_ref[source_ref[slot]]

    place_half(1, read, count_ref, factor_ref, placed_ref, ready_ref, sems)


def in_hbm(x):
    return pltpu.with_memory_space_constraint(x, pltpu.HBM)


def in_vmem(x):
    return pltpu.with_memory_space_constraint(x, pltpu.VMEM)


def call(kernel, name, in_specs, outs, scratch=(), megabytes=0, aliases={}):
    return pl.pallas_call(
        kernel,
        in_specs=in_specs,
        out_specs=[spec for spec, _, _ in outs],
        out_shape=[
            (pltpu.HBM if spec is IN_HBM else pltpu.VMEM)(shape, dtype) for spec, shape, dtype in outs
        ],
        scratch_shapes=list(scratch),
        input_output_aliases=aliases,
        compiler_params=pltpu.CompilerParams(vmem_limit_bytes=VMEM_LIMIT),
        cost_estimate=pl.CostEstimate(
            flops=0, transcendentals=0, bytes_accessed=megabytes * 1024 * 1024
        ),
        name=name,
    )


def per_device(feats, valid, owner_map, w_conv, w_mid, w_out):
    local = owner_map.shape[0]
    devices = lax.axis_size(DP)
    chips = devices // 2
    capacity = devices // 2
    tokens_here = local * BT
    me = lax.axis_index(DP)
    core = lax.axis_index("dp_2").astype(jnp.int32).reshape(1)
    images = jnp.arange(devices, dtype=jnp.int32)

    (copies,) = call(
        pack_kernel,
        "pack",
        [IN_HBM] * 5,
        [(IN_VMEM, (chips, ROWS, D), BF16)],
        [
            pltpu.SMEM((local,), jnp.int32),
            pltpu.SMEM((local,), jnp.int32),
            pltpu.VMEM((3, SHARD, D), BF16),
            pltpu.VMEM((SHARD, D), BF16),
            pltpu.VMEM((1, SHARD), BF16),
            pltpu.VMEM((ROWS, D), F32),
            pltpu.SemaphoreType.DMA((5,)),
        ],
    )(*(in_hbm(x) for x in (valid, owner_map, w_conv[0], w_mid[0], w_out)))
    own = lax.all_to_all(copies, CHIPS, split_axis=0, concat_axis=0, tiled=True)
    other = swapped(own)

    low, mid_grad, weights, state, sums, out_w, extras, totals = call(
        forward_kernel,
        "forward",
        [IN_SMEM, IN_SMEM, IN_SMEM, IN_HBM, IN_HBM, IN_HBM],
        [
            (IN_HBM, (tokens_here, D), BF16),
            (IN_HBM, (tokens_here, D), BF16),
            (IN_HBM, (4 * D, D), BF16),
            (IN_VMEM, (tokens_here + 4 * D, D), BF16),
            (IN_VMEM, (local, D), F32),
            (IN_VMEM, (1, D), F32),
            (IN_VMEM, (devices, 128), F32),
            (IN_VMEM, (chips, 1, 128), F32),
        ],
        [
            pltpu.VMEM((tokens_here, D), BF16),
            pltpu.VMEM((chips, ROWS, D), BF16),
            pltpu.VMEM((chips, ROWS, D), BF16),
            pltpu.VMEM((tokens_here, D), BF16),
            pltpu.VMEM((tokens_here, D), BF16),
            pltpu.VMEM((4 * D, D), F32),
            pltpu.SemaphoreType.DMA((3,)),
            pltpu.SemaphoreType.DMA((2, 3)),
            pltpu.SemaphoreType.DMA((2,)),
        ],
    )(valid, owner_map, core, in_hbm(feats[0]), in_hbm(own), in_hbm(other))

    totals = lax.all_to_all(totals, CHIPS, split_axis=0, concat_axis=0, tiled=True)

    first_grad, first_slots = call(
        backward_kernel,
        "backward",
        [IN_SMEM, IN_SMEM, IN_HBM, IN_VMEM, IN_VMEM],
        [
            (IN_HBM, (tokens_here, D), BF16),
            (IN_HBM, (devices, HALF, D), BF16),
        ],
        [
            pltpu.VMEM((tokens_here, D), BF16),
            pltpu.VMEM((tokens_here, D), BF16),
            pltpu.VMEM((local, HALF, D), BF16),
            pltpu.SemaphoreType.DMA((local,)),
            pltpu.SemaphoreType.DMA((local // GROUP,)),
            pltpu.SemaphoreType.DMA((local // GROUP,)),
        ],
        megabytes=16,
    )(valid, owner_map, in_hbm(mid_grad), in_vmem(state), in_vmem(out_w))

    first_slots, totals = lax.optimization_barrier((first_slots, totals))
    first_received = lax.all_to_all(first_slots, DP, split_axis=0, concat_axis=0, tiled=True)

    (second_slots,) = call(
        second_half_kernel,
        "second_half",
        [IN_SMEM, IN_SMEM, IN_HBM, IN_HBM],
        [(IN_HBM, (devices, HALF, D), BF16)],
        [
            pltpu.VMEM((tokens_here, D), BF16),
            pltpu.VMEM((4 * D, D), BF16),
            pltpu.VMEM((local, HALF, D), BF16),
            pltpu.SemaphoreType.DMA((local,)),
            pltpu.SemaphoreType.DMA((2,)),
        ],
        megabytes=16,
    )(valid, owner_map, in_hbm(first_grad), in_hbm(weights))

    totals = total_over(jnp.sum(totals[:, 0, :devices], 0)[None], "dp_2")
    totals = total_over(totals, "head")[0]
    members = (owner_map[:, None] == images[None, :]).astype(F32)
    owners = extras[:, SHARD : SHARD + local].astype(jnp.int32)
    valids = extras[:, SHARD + local : SHARD + 2 * local]
    tokens = jnp.sum(jnp.where(owners[:, :, None] == images, valids[:, :, None], 0.0), (0, 1))
    norm = jnp.sqrt(TAPS * tokens)
    factor = -BT * jax.nn.sigmoid(-totals / norm) / norm
    block_factor = jnp.sum(members * factor[None, :], 1)
    own_factor = jnp.sum(jnp.where(images == me, factor, 0.0)).reshape(1)

    (parts,) = call(
        weight_kernel,
        "weight_grads",
        [IN_SMEM, IN_SMEM, IN_HBM, IN_HBM, IN_HBM, IN_HBM, IN_VMEM],
        [(IN_VMEM, (devices, ROWS, D), BF16)],
        [pltpu.VMEM((tokens_here, D), BF16)] * 4
        + [
            pltpu.VMEM((3, D, D), F32),
            pltpu.VMEM((D, D), F32),
            pltpu.VMEM((ROWS, D), F32),
            pltpu.SemaphoreType.DMA((4, local)),
        ],
        megabytes=16,
    )(
        valid, block_factor, in_hbm(feats[0]), in_hbm(low), in_hbm(mid_grad),
        in_hbm(first_grad), in_vmem(sums),
    )
    parts = parts.reshape(4, 4, 2, ROWS, D)
    parts = added(delivered(*shares(parts, "dp_2", 2), axis="dp_2"))
    ready = shares(parts, "dp_0", 0)
    pieces = delivered(*ready, axis="dp_0")

    present = jnp.sum((owners == me).astype(jnp.int32), 1)
    rank = jnp.sum(jnp.where(images[None, :] < images[:, None], present[None, :], 0), 1)
    count = jnp.sum(present)
    wanted = jnp.minimum(jnp.arange(capacity, dtype=jnp.int32), count - 1)
    hit = (rank[None, :] == wanted[:, None]) & (present[None, :] > 0)
    source = jnp.sum(jnp.where(hit, images[None, :], 0), 1).astype(jnp.int32)
    half_slots = pltpu.VMEM((capacity, HALF, D), BF16)
    slot_sems = pltpu.SemaphoreType.DMA((capacity,))
    result = [(IN_HBM, (capacity * BT, D), BF16)]
    second_slots, first_received, source, own_factor, _ = lax.optimization_barrier(
        (second_slots, first_received, source, own_factor, ready)
    )
    second_received = lax.all_to_all(second_slots, DP, split_axis=0, concat_axis=0, tiled=True)
    table = (source, count.reshape(1), own_factor)
    (placed,) = call(
        place_first_kernel,
        "place_first",
        [IN_SMEM, IN_SMEM, IN_SMEM, IN_HBM],
        result,
        [half_slots, slot_sems, half_slots, slot_sems],
        megabytes=12,
    )(*table, in_hbm(first_received))
    pieces = delivered(*shares(added(pieces), "dp_1", 0), axis="dp_1")
    pieces, placed = lax.optimization_barrier((pieces, placed))
    (placed,) = call(
        place_second_kernel,
        "place_second",
        [IN_SMEM, IN_SMEM, IN_SMEM, IN_VMEM, IN_HBM],
        result,
        [half_slots, slot_sems],
        megabytes=12,
        aliases={4: 0},
    )(*table, in_vmem(second_received), in_hbm(placed))
    conv, mid, out = pl.pallas_call(
        finish_kernel,
        in_specs=[IN_VMEM] * 4,
        out_specs=[IN_VMEM] * 3,
        out_shape=[
            jax.ShapeDtypeStruct((3 * SHARD, 1, D), F32),
            jax.ShapeDtypeStruct((SHARD, 1, D), F32),
            jax.ShapeDtypeStruct((1, SHARD), F32),
        ],
        scratch_shapes=[pltpu.VMEM((ROWS, D), F32)],
        name="finish",
    )(*(in_vmem(x) for x in pieces))
    return placed[None], conv.reshape(1, 3, SHARD, D), mid.reshape(1, SHARD, D), out


def solution(mesh):
    split = Mesh(
        mesh.devices.reshape(4, 4, 2, mesh.shape["head"]), ("dp_0", "dp_1", "dp_2", "head")
    )
    in_specs = (
        P("head", DP, None),
        P(DP),
        P(DP),
        P("head", None, DP, None),
        P("head", DP, None),
        P("head", DP),
    )
    out_specs = (P("head", DP, None), P("head", None, DP, None), P("head", DP, None), P("head", DP))
    return jax.shard_map(
        per_device, mesh=split, in_specs=in_specs, out_specs=out_specs, check_vma=False
    )
```

```python
import jax
import jax.numpy as jnp
from jax import lax
from jax.experimental import pallas as pl
from jax.experimental.pallas import tpu as pltpu
from jax.sharding import Mesh
from jax.sharding import PartitionSpec as P

DP = ("dp_0", "dp_1", "dp_2")
CHIPS = ("dp_0", "dp_1")
BF16 = jnp.bfloat16
F32 = jnp.float32
TAPS = 4
BT = 256
D = 384
SHARD = 12
EXTRA = 4 * SHARD
ROWS = 56
GROUP = 4
LOG_2 = 0.6931471805599453
VMEM_LIMIT = 20 * 1024 * 1024

IN_VMEM = pl.BlockSpec(memory_space=pltpu.VMEM)
IN_SMEM = pl.BlockSpec(memory_space=pltpu.SMEM)
IN_HBM = pl.BlockSpec(memory_space=pltpu.HBM)
OVER_LAST = (((1,), (1,)), ((), ()))
OVER_ROWS = (((0,), (0,)), ((), ()))


def swapped(x):
    return lax.ppermute(x, "dp_2", [(0, 1), (1, 0)])


def turned(x, axis, shift):
    count = lax.axis_size(axis)
    return lax.ppermute(x, axis, [(i, (i + shift) % count) for i in range(count)])


def total_over(x, axis):
    return sum((turned(x, axis, r) for r in range(1, lax.axis_size(axis))), x)


def scattered_sum(parts, axis, dim):
    count, index = lax.axis_size(axis), lax.axis_index(axis)

    def piece(shift):
        return lax.dynamic_index_in_dim(parts, (index + shift) % count, dim, keepdims=False)

    total = piece(0).astype(F32)
    for r in range(1, count):
        total += turned(piece(r).astype(BF16), axis, r).astype(F32)
    return total


def gate(value):
    half = jnp.tanh(0.5 * value)
    tail = 0.8 * LOG_2 - (0.8 * LOG_2) * jnp.log2(1.0 + jnp.abs(half))
    return jnp.maximum(value, 0.2 * value) + tail, 0.6 + 0.4 * half


def row_mask(valid_ref, first, blocks):
    rows = lax.broadcasted_iota(jnp.int32, (blocks * BT, 1), 0)
    limit = jnp.full_like(rows, valid_ref[first])
    for j in range(1, blocks):
        limit = jnp.where(rows < j * BT, limit, j * BT + valid_ref[first + j])
    return rows < limit


def neighbours(x, place, last):
    count = x.shape[0]
    before = jnp.where(place == 0, 0.0, pltpu.roll(x, 1, 0))
    after = jnp.where(place == last, 0.0, pltpu.roll(x, count - 1, 0))
    return before.astype(BF16), after.astype(BF16)


def block_place(count):
    return lax.broadcasted_iota(jnp.int32, (count, 1), 0) % BT


def pack_kernel(
    valid_hbm, owner_hbm, conv_hbm, mid_hbm, out_hbm,
    copies_ref, valid_ref, owner_ref, conv_ref, mid_ref, out_ref, stage_ref, sems,
):
    sources = (valid_hbm, owner_hbm, conv_hbm, mid_hbm, out_hbm)
    targets = (valid_ref, owner_ref, conv_ref, mid_ref, out_ref)
    arrivals = [
        pltpu.make_async_copy(source, target, sems.at[i])
        for i, (source, target) in enumerate(zip(sources, targets))
    ]
    for copy in arrivals:
        copy.start()
    for copy in arrivals:
        copy.wait()
    local = valid_ref.shape[0]
    lane = lax.broadcasted_iota(jnp.int32, (1, D), 1)
    extras = jnp.zeros((1, D), F32)
    for j in range(local):
        extras = jnp.where(lane == SHARD + j, owner_ref[j].astype(F32), extras)
        extras = jnp.where(lane == SHARD + local + j, valid_ref[j].astype(F32), extras)
    stage_ref[EXTRA:ROWS, :] = jnp.zeros((ROWS - EXTRA, D), F32)
    for k in range(3):
        stage_ref[SHARD * k : SHARD * (k + 1), :] = conv_ref[k].astype(F32)
    stage_ref[3 * SHARD : EXTRA, :] = mid_ref[...].astype(F32)
    stage_ref[EXTRA : EXTRA + 1, :] = extras
    stage_ref[EXTRA : EXTRA + 1, 0:SHARD] = out_ref[...].astype(F32)
    packed = stage_ref[...].astype(BF16)
    for j in range(copies_ref.shape[0]):
        copies_ref[j] = packed


def state_rows(local):
    tokens = local * BT
    return pl.ds(0, tokens), pl.ds(tokens, 4 * D)


def weight(ref, k):
    return ref[k * D : (k + 1) * D, :]


def forward_kernel(
    valid_ref, owner_ref, core_ref, feats_ref, own_hbm, other_hbm,
    low_out, mid_grad_out, state_ref, sums_ref, out_w_ref, extras_ref, totals_ref,
    raw_ref, own_ref, other_ref, low_ref, mid_grad_ref, wide_ref, sems, out_sems, weight_sems,
):
    local = valid_ref.shape[0]
    slope_ref, weights_ref = (state_ref.at[rows] for rows in state_rows(local))
    arrivals = [
        pltpu.make_async_copy(own_hbm, own_ref, weight_sems.at[0]),
        pltpu.make_async_copy(other_hbm, other_ref, weight_sems.at[1]),
    ]
    for n, j in enumerate(range(0, local, GROUP)):
        rows = pl.ds(j * BT, GROUP * BT)
        arrivals.append(pltpu.make_async_copy(feats_ref.at[rows], raw_ref.at[rows], sems.at[n]))
    for copy in arrivals:
        copy.start()

    def unpack(parity, source):
        for chip in range(source.shape[0]):
            tile = source[chip].astype(F32)
            device = 2 * chip + parity
            at = SHARD * device
            for k in range(4):
                wide_ref[k * D + at : k * D + at + SHARD, :] = tile[SHARD * k : SHARD * (k + 1)]
            extras_ref[device : device + 1, :] = tile[EXTRA : EXTRA + 1, :128]

    for copy in arrivals[:2]:
        copy.wait()

    @pl.when(core_ref[0] == 0)
    def _():
        unpack(0, own_ref)
        unpack(1, other_ref)

    @pl.when(core_ref[0] == 1)
    def _():
        unpack(1, own_ref)
        unpack(0, other_ref)

    weights_ref[...] = wide_ref[...].astype(BF16)
    devices = extras_ref.shape[0]
    column = lax.broadcasted_iota(jnp.int32, (128, D), 1).astype(F32)
    place = lax.broadcasted_iota(jnp.int32, (128, D), 0).astype(F32)
    home = jnp.floor((column + 0.5) * (1.0 / SHARD))
    pick = jnp.where(column - SHARD * home == place, 1.0, 0.0).astype(BF16)
    spread = jnp.dot(extras_ref[...].astype(BF16), pick, preferred_element_type=F32)
    row = lax.broadcasted_iota(jnp.int32, (devices, D), 0).astype(F32)
    out_w = jnp.sum(jnp.where(home[:devices] == row, spread, 0.0), 0, keepdims=True)
    out_w_ref[...] = out_w

    lane = lax.broadcasted_iota(jnp.int32, (1, 128), 1)
    totals = jnp.zeros((1, 128), F32)
    departures = []
    for n, j in enumerate(range(0, local, GROUP)):
        rows = pl.ds(j * BT, GROUP * BT)
        arrivals[2 + n].wait()
        place = block_place(GROUP * BT)
        keep = row_mask(valid_ref, j, GROUP)
        masked = jnp.where(keep, raw_ref[rows, :].astype(F32), 0.0)
        before, after = neighbours(masked, place, BT - 1)
        first = jnp.dot(before, weight(weights_ref, 0), preferred_element_type=F32)
        first += jnp.dot(
            masked.astype(BF16), weight(weights_ref, 1), preferred_element_type=F32
        )
        first += jnp.dot(after, weight(weights_ref, 2), preferred_element_type=F32)
        first_act, slope = gate(first)
        low = first_act.astype(BF16)
        low_ref[rows, :] = low
        copy = pltpu.make_async_copy(low_ref.at[rows], low_out.at[rows], out_sems.at[0, n])
        copy.start()
        departures.append(copy)
        slope_ref[rows, :] = slope.astype(BF16)
        second = jnp.dot(low, weight(weights_ref, 3), preferred_element_type=F32)
        second_act, second_slope = gate(second)
        mid_grad_ref[rows, :] = jnp.where(keep, out_w * second_slope, 0.0).astype(BF16)
        copy = pltpu.make_async_copy(
            mid_grad_ref.at[rows], mid_grad_out.at[rows], out_sems.at[1, n]
        )
        copy.start()
        departures.append(copy)
        total = jnp.where(keep, second_act + first_act, 0.0)
        for i in range(GROUP):
            block = jnp.sum(total[i * BT : (i + 1) * BT], 0, keepdims=True)
            sums_ref[j + i : j + i + 1, :] = block
            block_sum = jnp.sum(block * out_w, 1, keepdims=True)
            totals += jnp.where(lane == owner_ref[j + i], block_sum, 0.0)
    for chip in range(devices // 2):
        totals_ref[chip] = totals
    for copy in departures:
        copy.wait()


def backward_kernel(
    valid_ref, owner_ref, mid_grad_hbm, state_ref, out_w_ref,
    first_grad_out, slots_ref, mid_grad_ref, first_grad_ref, ready_ref, sems, out_sems, in_sems,
):
    local = valid_ref.shape[0]
    slope_ref, weights_ref = (state_ref.at[rows] for rows in state_rows(local))
    place = block_place(GROUP * BT)
    arrivals, copies = [], []
    for j in range(0, local, GROUP):
        rows = pl.ds(j * BT, GROUP * BT)
        copy = pltpu.make_async_copy(
            mid_grad_hbm.at[rows], mid_grad_ref.at[rows], in_sems.at[j // GROUP]
        )
        copy.start()
        arrivals.append(copy)
    for j in range(0, local, GROUP):
        rows = pl.ds(j * BT, GROUP * BT)
        arrivals[j // GROUP].wait()
        keep = row_mask(valid_ref, j, GROUP)
        grad = lax.dot_general(
            mid_grad_ref[rows, :], weight(weights_ref, 3), OVER_LAST, preferred_element_type=F32
        )
        grad = (grad + jnp.where(keep, out_w_ref[...], 0.0)) * slope_ref[rows, :].astype(F32)
        before, after = neighbours(grad, place, BT - 1)
        low = grad.astype(BF16)
        first_grad_ref[rows, :] = low
        total = lax.dot_general(low, weight(weights_ref, 1), OVER_LAST, preferred_element_type=F32)
        total += lax.dot_general(
            after, weight(weights_ref, 0), OVER_LAST, preferred_element_type=F32
        )
        total += lax.dot_general(
            before, weight(weights_ref, 2), OVER_LAST, preferred_element_type=F32
        )
        total = jnp.where(keep, total, 0.0).astype(BF16)
        for i in range(GROUP):
            ready_ref[j + i] = total[i * BT : (i + 1) * BT]
            copy = pltpu.make_async_copy(
                ready_ref.at[j + i], slots_ref.at[owner_ref[j + i]], sems.at[j + i]
            )
            copy.start()
            copies.append(copy)
        copy = pltpu.make_async_copy(
            first_grad_ref.at[rows], first_grad_out.at[rows], out_sems.at[j // GROUP]
        )
        copy.start()
        copies.append(copy)
    for copy in copies:
        copy.wait()


def weight_kernel(
    valid_ref, factor_ref, feats_hbm, low_hbm, mid_grad_hbm, first_grad_hbm, sums_ref,
    parts_ref, feats_ref, low_ref, mid_grad_ref, first_grad_ref, conv_ref, mid_ref, stage_ref, sems,
):
    local = valid_ref.shape[0]
    pairs = (
        (feats_hbm, feats_ref),
        (low_hbm, low_ref),
        (mid_grad_hbm, mid_grad_ref),
        (first_grad_hbm, first_grad_ref),
    )
    arrivals = []
    for j in range(local):
        rows = pl.ds(j * BT, BT)
        arrivals.append(
            [
                pltpu.make_async_copy(source.at[rows], target.at[rows], sems.at[i, j])
                for i, (source, target) in enumerate(pairs)
            ]
        )
        for copy in arrivals[j]:
            copy.start()
    out = jnp.zeros((1, D), F32)
    place = block_place(BT)
    for j in range(local):
        rows = pl.ds(j * BT, BT)
        for copy in arrivals[j]:
            copy.wait()
        factor = factor_ref[j]
        out += sums_ref[j : j + 1, :] * factor
        grad = first_grad_ref[rows, :].astype(F32) * factor
        before, after = neighbours(grad, place, BT - 1)
        mid_grad = (mid_grad_ref[rows, :].astype(F32) * factor).astype(BF16)
        keep = row_mask(valid_ref, j, 1)
        masked = jnp.where(keep, feats_ref[rows, :].astype(F32), 0.0).astype(BF16)
        terms = [
            lax.dot_general(masked, x, OVER_ROWS, preferred_element_type=F32)
            for x in (after, grad.astype(BF16), before)
        ]
        mid = lax.dot_general(low_ref[rows, :], mid_grad, OVER_ROWS, preferred_element_type=F32)
        for k in range(3):
            conv_ref[k] = terms[k] if j == 0 else conv_ref[k] + terms[k]
        mid_ref[...] = mid if j == 0 else mid_ref[...] + mid

    devices = parts_ref.shape[0]
    column = lax.broadcasted_iota(jnp.int32, (D, D), 0).astype(F32)
    place = lax.broadcasted_iota(jnp.int32, (D, D), 1).astype(F32)
    home = jnp.floor((column + 0.5) * (1.0 / SHARD))
    pick = jnp.where(column - SHARD * home == place, 1.0, 0.0).astype(BF16)
    device = lax.broadcasted_iota(jnp.int32, (devices, D), 0).astype(F32)
    lane = lax.broadcasted_iota(jnp.int32, (devices, D), 1).astype(F32)
    mine = jnp.floor((lane + 0.5) * (1.0 / SHARD)) == device
    out_rows = jnp.where(mine, out, 0.0).astype(BF16)
    out_rows = jnp.dot(out_rows, pick, preferred_element_type=F32)
    stage_ref[EXTRA:ROWS, :] = jnp.zeros((ROWS - EXTRA, D), F32)
    for d in range(devices):
        at = SHARD * d
        for k in range(3):
            stage_ref[SHARD * k : SHARD * (k + 1), :] = conv_ref[k, at : at + SHARD, :]
        stage_ref[3 * SHARD : EXTRA, :] = mid_ref[at : at + SHARD, :]
        stage_ref[EXTRA : EXTRA + 1, :] = out_rows[d : d + 1, :]
        parts_ref[d] = stage_ref[...].astype(BF16)


def finish_kernel(pieces_ref, conv_ref, mid_ref, out_ref, total_ref):
    total = pieces_ref[0].astype(F32)
    for i in range(1, pieces_ref.shape[0]):
        total += pieces_ref[i].astype(F32)
    total_ref[...] = total * (1.0 / BT)
    for row in range(3 * SHARD):
        conv_ref[row] = total_ref[row : row + 1, :]
    for row in range(SHARD):
        mid_ref[row] = total_ref[3 * SHARD + row : 3 * SHARD + row + 1, :]
    out_ref[...] = total_ref[EXTRA : EXTRA + 1, 0:SHARD]


def place_kernel(
    source_ref, count_ref, factor_ref, received_ref, placed_ref, raw_ref, ready_ref, in_sems, out_sems
):
    capacity = source_ref.shape[0]
    arrivals, departures = [], []
    for slot in range(capacity):
        copy = pltpu.make_async_copy(
            received_ref.at[source_ref[slot]], raw_ref.at[slot], in_sems.at[slot]
        )
        copy.start()
        arrivals.append(copy)
    for slot in range(capacity):
        arrivals[slot].wait()
        factor = jnp.where(slot < count_ref[0], factor_ref[0], 0.0)
        ready_ref[slot] = (raw_ref[slot].astype(F32) * factor).astype(BF16)
        rows = pl.ds(slot * BT, BT)
        copy = pltpu.make_async_copy(ready_ref.at[slot], placed_ref.at[rows], out_sems.at[slot])
        copy.start()
        departures.append(copy)
    for copy in departures:
        copy.wait()


def in_hbm(x):
    return pltpu.with_memory_space_constraint(x, pltpu.HBM)


def in_vmem(x):
    return pltpu.with_memory_space_constraint(x, pltpu.VMEM)


def call(kernel, name, in_specs, outs, scratch=(), megabytes=0):
    return pl.pallas_call(
        kernel,
        in_specs=in_specs,
        out_specs=[spec for spec, _, _ in outs],
        out_shape=[
            (pltpu.HBM if spec is IN_HBM else pltpu.VMEM)(shape, dtype) for spec, shape, dtype in outs
        ],
        scratch_shapes=list(scratch),
        compiler_params=pltpu.CompilerParams(vmem_limit_bytes=VMEM_LIMIT),
        cost_estimate=pl.CostEstimate(
            flops=0, transcendentals=0, bytes_accessed=megabytes * 1024 * 1024
        ),
        name=name,
    )


def per_device(feats, valid, owner_map, w_conv, w_mid, w_out):
    local = owner_map.shape[0]
    devices = lax.axis_size(DP)
    chips = devices // 2
    capacity = devices // 2
    tokens_here = local * BT
    me = lax.axis_index(DP)
    core = lax.axis_index("dp_2").astype(jnp.int32).reshape(1)
    images = jnp.arange(devices, dtype=jnp.int32)

    (copies,) = call(
        pack_kernel,
        "pack",
        [IN_HBM] * 5,
        [(IN_VMEM, (chips, ROWS, D), BF16)],
        [
            pltpu.SMEM((local,), jnp.int32),
            pltpu.SMEM((local,), jnp.int32),
            pltpu.VMEM((3, SHARD, D), BF16),
            pltpu.VMEM((SHARD, D), BF16),
            pltpu.VMEM((1, SHARD), BF16),
            pltpu.VMEM((ROWS, D), F32),
            pltpu.SemaphoreType.DMA((5,)),
        ],
    )(*(in_hbm(x) for x in (valid, owner_map, w_conv[0], w_mid[0], w_out)))
    own = lax.all_to_all(copies, CHIPS, split_axis=0, concat_axis=0, tiled=True)
    other = swapped(own)

    low, mid_grad, state, sums, out_w, extras, totals = call(
        forward_kernel,
        "forward",
        [IN_SMEM, IN_SMEM, IN_SMEM, IN_HBM, IN_HBM, IN_HBM],
        [
            (IN_HBM, (tokens_here, D), BF16),
            (IN_HBM, (tokens_here, D), BF16),
            (IN_VMEM, (tokens_here + 4 * D, D), BF16),
            (IN_VMEM, (local, D), F32),
            (IN_VMEM, (1, D), F32),
            (IN_VMEM, (devices, 128), F32),
            (IN_VMEM, (chips, 1, 128), F32),
        ],
        [
            pltpu.VMEM((tokens_here, D), BF16),
            pltpu.VMEM((chips, ROWS, D), BF16),
            pltpu.VMEM((chips, ROWS, D), BF16),
            pltpu.VMEM((tokens_here, D), BF16),
            pltpu.VMEM((tokens_here, D), BF16),
            pltpu.VMEM((4 * D, D), F32),
            pltpu.SemaphoreType.DMA((local // GROUP,)),
            pltpu.SemaphoreType.DMA((2, local // GROUP)),
            pltpu.SemaphoreType.DMA((2,)),
        ],
    )(valid, owner_map, core, in_hbm(feats[0]), in_hbm(own), in_hbm(other))

    totals = lax.all_to_all(totals, CHIPS, split_axis=0, concat_axis=0, tiled=True)

    first_grad, slots = call(
        backward_kernel,
        "backward",
        [IN_SMEM, IN_SMEM, IN_HBM, IN_VMEM, IN_VMEM],
        [
            (IN_HBM, (tokens_here, D), BF16),
            (IN_HBM, (devices, BT, D), BF16),
        ],
        [
            pltpu.VMEM((tokens_here, D), BF16),
            pltpu.VMEM((tokens_here, D), BF16),
            pltpu.VMEM((local, BT, D), BF16),
            pltpu.SemaphoreType.DMA((local,)),
            pltpu.SemaphoreType.DMA((local // GROUP,)),
            pltpu.SemaphoreType.DMA((local // GROUP,)),
        ],
        megabytes=24,
    )(valid, owner_map, in_hbm(mid_grad), in_vmem(state), in_vmem(out_w))

    slots, totals = lax.optimization_barrier((slots, totals))
    received = lax.all_to_all(slots, DP, split_axis=0, concat_axis=0, tiled=True)

    totals = total_over(jnp.sum(totals[:, 0, :devices], 0)[None], "dp_2")
    totals = total_over(totals, "head")[0]
    members = (owner_map[:, None] == images[None, :]).astype(F32)
    owners = extras[:, SHARD : SHARD + local].astype(jnp.int32)
    valids = extras[:, SHARD + local : SHARD + 2 * local]
    tokens = jnp.sum(jnp.where(owners[:, :, None] == images, valids[:, :, None], 0.0), (0, 1))
    norm = jnp.sqrt(TAPS * tokens)
    factor = -BT * jax.nn.sigmoid(-totals / norm) / norm
    block_factor = jnp.sum(members * factor[None, :], 1)
    own_factor = jnp.sum(jnp.where(images == me, factor, 0.0)).reshape(1)

    (parts,) = call(
        weight_kernel,
        "weight_grads",
        [IN_SMEM, IN_SMEM, IN_HBM, IN_HBM, IN_HBM, IN_HBM, IN_VMEM],
        [(IN_VMEM, (devices, ROWS, D), BF16)],
        [pltpu.VMEM((tokens_here, D), BF16)] * 4
        + [
            pltpu.VMEM((3, D, D), F32),
            pltpu.VMEM((D, D), F32),
            pltpu.VMEM((ROWS, D), F32),
            pltpu.SemaphoreType.DMA((4, local)),
        ],
        megabytes=16,
    )(
        valid, block_factor, in_hbm(feats[0]), in_hbm(low), in_hbm(mid_grad),
        in_hbm(first_grad), in_vmem(sums),
    )
    parts = parts.reshape(4, 4, 2, ROWS, D)
    parts = scattered_sum(parts, "dp_2", 2)
    parts = scattered_sum(parts, "dp_0", 0).astype(BF16)

    present = jnp.sum((owners == me).astype(jnp.int32), 1)
    rank = jnp.sum(jnp.where(images[None, :] < images[:, None], present[None, :], 0), 1)
    count = jnp.sum(present)
    wanted = jnp.minimum(jnp.arange(capacity, dtype=jnp.int32), count - 1)
    hit = (rank[None, :] == wanted[:, None]) & (present[None, :] > 0)
    source = jnp.sum(jnp.where(hit, images[None, :], 0), 1).astype(jnp.int32)
    table = (source, count.reshape(1), own_factor)
    parts, received, table = lax.optimization_barrier((parts, received, table))
    pieces = lax.all_to_all(parts, "dp_1", split_axis=0, concat_axis=0, tiled=True)
    (placed,) = call(
        place_kernel,
        "place",
        [IN_SMEM, IN_SMEM, IN_SMEM, IN_HBM],
        [(IN_HBM, (capacity * BT, D), BF16)],
        [
            pltpu.VMEM((capacity, BT, D), BF16),
            pltpu.VMEM((capacity, BT, D), BF16),
            pltpu.SemaphoreType.DMA((capacity,)),
            pltpu.SemaphoreType.DMA((capacity,)),
        ],
        megabytes=24,
    )(*table, in_hbm(received))

    conv, mid, out = pl.pallas_call(
        finish_kernel,
        in_specs=[IN_VMEM],
        out_specs=[IN_VMEM] * 3,
        out_shape=[
            jax.ShapeDtypeStruct((3 * SHARD, 1, D), F32),
            jax.ShapeDtypeStruct((SHARD, 1, D), F32),
            jax.ShapeDtypeStruct((1, SHARD), F32),
        ],
        scratch_shapes=[pltpu.VMEM((ROWS, D), F32)],
        name="finish",
    )(in_vmem(pieces))
    return placed[None], conv.reshape(1, 3, SHARD, D), mid.reshape(1, SHARD, D), out


def solution(mesh):
    split = Mesh(
        mesh.devices.reshape(4, 4, 2, mesh.shape["head"]), ("dp_0", "dp_1", "dp_2", "head")
    )
    in_specs = (
        P("head", DP, None),
        P(DP),
        P(DP),
        P("head", None, DP, None),
        P("head", DP, None),
        P("head", DP),
    )
    out_specs = (P("head", DP, None), P("head", None, DP, None), P("head", DP, None), P("head", DP))
    return jax.shard_map(
        per_device, mesh=split, in_specs=in_specs, out_specs=out_specs, check_vma=False
    )
```

```python
import jax
import jax.numpy as jnp
from jax import lax
from jax.experimental import pallas as pl
from jax.experimental.pallas import tpu as pltpu
from jax.sharding import Mesh
from jax.sharding import PartitionSpec as P

DP = ("dp_0", "dp_1", "dp_2")
CHIPS = ("dp_0", "dp_1")
BF16 = jnp.bfloat16
F32 = jnp.float32
TAPS = 4
BT = 256
D = 384
SHARD = 12
EXTRA = 4 * SHARD
ROWS = 56
GROUP = 4
LOG_2 = 0.6931471805599453
VMEM_LIMIT = 20 * 1024 * 1024

IN_VMEM = pl.BlockSpec(memory_space=pltpu.VMEM)
IN_SMEM = pl.BlockSpec(memory_space=pltpu.SMEM)
IN_HBM = pl.BlockSpec(memory_space=pltpu.HBM)
OVER_LAST = (((1,), (1,)), ((), ()))
OVER_ROWS = (((0,), (0,)), ((), ()))


def swapped(x):
    return lax.ppermute(x, "dp_2", [(0, 1), (1, 0)])


def turned(x, axis, shift):
    count = lax.axis_size(axis)
    return lax.ppermute(x, axis, [(i, (i + shift) % count) for i in range(count)])


def total_over(x, axis):
    return sum((turned(x, axis, r) for r in range(1, lax.axis_size(axis))), x)


def shares(parts, index):
    count = parts.shape[0]

    def share(shift):
        return lax.dynamic_index_in_dim(parts, (index + shift) % count, 0, keepdims=False)

    return [share(0)] + [share(r).astype(BF16) for r in range(1, count)]


def crossed(x, shift, stage):
    tall, wide = lax.axis_size("dp_0"), lax.axis_size("dp_1")
    pairs = []
    for y in range(tall):
        for x_at in range(wide):
            for core in range(2):
                along_first = core == stage
                to_y = (y + shift) % tall if along_first else y
                to_x = x_at if along_first else (x_at + shift) % wide
                pairs.append(((y * wide + x_at) * 2 + core, (to_y * wide + to_x) * 2 + core))
    return lax.ppermute(x, DP, pairs)


def delivered(own, *others, stage):
    return [own] + [crossed(other, r, stage) for r, other in enumerate(others, 1)]


def added(pieces):
    return sum(piece.astype(F32) for piece in pieces)


def gate(value):
    half = jnp.tanh(0.5 * value)
    tail = 0.8 * LOG_2 - (0.8 * LOG_2) * jnp.log2(1.0 + jnp.abs(half))
    return jnp.maximum(value, 0.2 * value) + tail, 0.6 + 0.4 * half


def row_mask(valid_ref, first, blocks):
    rows = lax.broadcasted_iota(jnp.int32, (blocks * BT, 1), 0)
    limit = jnp.full_like(rows, valid_ref[first])
    for j in range(1, blocks):
        limit = jnp.where(rows < j * BT, limit, j * BT + valid_ref[first + j])
    return rows < limit


def neighbours(x, place, last):
    count = x.shape[0]
    before = jnp.where(place == 0, 0.0, pltpu.roll(x, 1, 0))
    after = jnp.where(place == last, 0.0, pltpu.roll(x, count - 1, 0))
    return before.astype(BF16), after.astype(BF16)


def block_place(count):
    return lax.broadcasted_iota(jnp.int32, (count, 1), 0) % BT


def pack_kernel(
    valid_hbm, owner_hbm, conv_hbm, mid_hbm, out_hbm,
    copies_ref, valid_ref, owner_ref, conv_ref, mid_ref, out_ref, stage_ref, sems,
):
    sources = (valid_hbm, owner_hbm, conv_hbm, mid_hbm, out_hbm)
    targets = (valid_ref, owner_ref, conv_ref, mid_ref, out_ref)
    arrivals = [
        pltpu.make_async_copy(source, target, sems.at[i])
        for i, (source, target) in enumerate(zip(sources, targets))
    ]
    for copy in arrivals:
        copy.start()
    for copy in arrivals:
        copy.wait()
    local = valid_ref.shape[0]
    lane = lax.broadcasted_iota(jnp.int32, (1, D), 1)
    extras = jnp.zeros((1, D), F32)
    for j in range(local):
        extras = jnp.where(lane == SHARD + j, owner_ref[j].astype(F32), extras)
        extras = jnp.where(lane == SHARD + local + j, valid_ref[j].astype(F32), extras)
    stage_ref[EXTRA:ROWS, :] = jnp.zeros((ROWS - EXTRA, D), F32)
    for k in range(3):
        stage_ref[SHARD * k : SHARD * (k + 1), :] = conv_ref[k].astype(F32)
    stage_ref[3 * SHARD : EXTRA, :] = mid_ref[...].astype(F32)
    stage_ref[EXTRA : EXTRA + 1, :] = extras
    stage_ref[EXTRA : EXTRA + 1, 0:SHARD] = out_ref[...].astype(F32)
    packed = stage_ref[...].astype(BF16)
    for j in range(copies_ref.shape[0]):
        copies_ref[j] = packed


def state_rows(local):
    tokens = local * BT
    return pl.ds(0, tokens), pl.ds(tokens, 4 * D)


def weight(ref, k):
    return ref[k * D : (k + 1) * D, :]


def forward_kernel(
    valid_ref, owner_ref, core_ref, feats_ref, own_hbm, other_hbm,
    low_out, mid_grad_out, state_ref, sums_ref, out_w_ref, extras_ref, totals_ref,
    raw_ref, own_ref, other_ref, low_ref, mid_grad_ref, wide_ref, sems, out_sems, weight_sems,
):
    local = valid_ref.shape[0]
    slope_ref, weights_ref = (state_ref.at[rows] for rows in state_rows(local))
    arrivals = [
        pltpu.make_async_copy(own_hbm, own_ref, weight_sems.at[0]),
        pltpu.make_async_copy(other_hbm, other_ref, weight_sems.at[1]),
    ]
    for n, j in enumerate(range(0, local, GROUP)):
        rows = pl.ds(j * BT, GROUP * BT)
        arrivals.append(pltpu.make_async_copy(feats_ref.at[rows], raw_ref.at[rows], sems.at[n]))
    for copy in arrivals:
        copy.start()

    def unpack(parity, source):
        for chip in range(source.shape[0]):
            tile = source[chip].astype(F32)
            device = 2 * chip + parity
            at = SHARD * device
            for k in range(4):
                wide_ref[k * D + at : k * D + at + SHARD, :] = tile[SHARD * k : SHARD * (k + 1)]
            extras_ref[device : device + 1, :] = tile[EXTRA : EXTRA + 1, :128]

    for copy in arrivals[:2]:
        copy.wait()

    @pl.when(core_ref[0] == 0)
    def _():
        unpack(0, own_ref)
        unpack(1, other_ref)

    @pl.when(core_ref[0] == 1)
    def _():
        unpack(1, own_ref)
        unpack(0, other_ref)

    weights_ref[...] = wide_ref[...].astype(BF16)
    devices = extras_ref.shape[0]
    column = lax.broadcasted_iota(jnp.int32, (128, D), 1).astype(F32)
    place = lax.broadcasted_iota(jnp.int32, (128, D), 0).astype(F32)
    home = jnp.floor((column + 0.5) * (1.0 / SHARD))
    pick = jnp.where(column - SHARD * home == place, 1.0, 0.0).astype(BF16)
    spread = jnp.dot(extras_ref[...].astype(BF16), pick, preferred_element_type=F32)
    row = lax.broadcasted_iota(jnp.int32, (devices, D), 0).astype(F32)
    out_w = jnp.sum(jnp.where(home[:devices] == row, spread, 0.0), 0, keepdims=True)
    out_w_ref[...] = out_w

    lane = lax.broadcasted_iota(jnp.int32, (1, 128), 1)
    totals = jnp.zeros((1, 128), F32)
    departures = []
    for n, j in enumerate(range(0, local, GROUP)):
        rows = pl.ds(j * BT, GROUP * BT)
        arrivals[2 + n].wait()
        place = block_place(GROUP * BT)
        keep = row_mask(valid_ref, j, GROUP)
        masked = jnp.where(keep, raw_ref[rows, :].astype(F32), 0.0)
        before, after = neighbours(masked, place, BT - 1)
        first = jnp.dot(before, weight(weights_ref, 0), preferred_element_type=F32)
        first += jnp.dot(
            masked.astype(BF16), weight(weights_ref, 1), preferred_element_type=F32
        )
        first += jnp.dot(after, weight(weights_ref, 2), preferred_element_type=F32)
        first_act, slope = gate(first)
        low = first_act.astype(BF16)
        low_ref[rows, :] = low
        copy = pltpu.make_async_copy(low_ref.at[rows], low_out.at[rows], out_sems.at[0, n])
        copy.start()
        departures.append(copy)
        slope_ref[rows, :] = slope.astype(BF16)
        second = jnp.dot(low, weight(weights_ref, 3), preferred_element_type=F32)
        second_act, second_slope = gate(second)
        mid_grad_ref[rows, :] = jnp.where(keep, out_w * second_slope, 0.0).astype(BF16)
        copy = pltpu.make_async_copy(
            mid_grad_ref.at[rows], mid_grad_out.at[rows], out_sems.at[1, n]
        )
        copy.start()
        departures.append(copy)
        total = jnp.where(keep, second_act + first_act, 0.0)
        for i in range(GROUP):
            block = jnp.sum(total[i * BT : (i + 1) * BT], 0, keepdims=True)
            sums_ref[j + i : j + i + 1, :] = block
            block_sum = jnp.sum(block * out_w, 1, keepdims=True)
            totals += jnp.where(lane == owner_ref[j + i], block_sum, 0.0)
    for chip in range(devices // 2):
        totals_ref[chip] = totals
    for copy in departures:
        copy.wait()


def backward_kernel(
    valid_ref, owner_ref, mid_grad_hbm, state_ref, out_w_ref,
    first_grad_out, slots_ref, mid_grad_ref, first_grad_ref, ready_ref, sems, out_sems, in_sems,
):
    local = valid_ref.shape[0]
    slope_ref, weights_ref = (state_ref.at[rows] for rows in state_rows(local))
    place = block_place(GROUP * BT)
    arrivals, copies = [], []
    for j in range(0, local, GROUP):
        rows = pl.ds(j * BT, GROUP * BT)
        copy = pltpu.make_async_copy(
            mid_grad_hbm.at[rows], mid_grad_ref.at[rows], in_sems.at[j // GROUP]
        )
        copy.start()
        arrivals.append(copy)
    for j in range(0, local, GROUP):
        rows = pl.ds(j * BT, GROUP * BT)
        arrivals[j // GROUP].wait()
        keep = row_mask(valid_ref, j, GROUP)
        grad = lax.dot_general(
            mid_grad_ref[rows, :], weight(weights_ref, 3), OVER_LAST, preferred_element_type=F32
        )
        grad = (grad + jnp.where(keep, out_w_ref[...], 0.0)) * slope_ref[rows, :].astype(F32)
        before, after = neighbours(grad, place, BT - 1)
        low = grad.astype(BF16)
        first_grad_ref[rows, :] = low
        total = lax.dot_general(low, weight(weights_ref, 1), OVER_LAST, preferred_element_type=F32)
        total += lax.dot_general(
            after, weight(weights_ref, 0), OVER_LAST, preferred_element_type=F32
        )
        total += lax.dot_general(
            before, weight(weights_ref, 2), OVER_LAST, preferred_element_type=F32
        )
        total = jnp.where(keep, total, 0.0).astype(BF16)
        for i in range(GROUP):
            ready_ref[j + i] = total[i * BT : (i + 1) * BT]
            copy = pltpu.make_async_copy(
                ready_ref.at[j + i], slots_ref.at[owner_ref[j + i]], sems.at[j + i]
            )
            copy.start()
            copies.append(copy)
        copy = pltpu.make_async_copy(
            first_grad_ref.at[rows], first_grad_out.at[rows], out_sems.at[j // GROUP]
        )
        copy.start()
        copies.append(copy)
    for copy in copies:
        copy.wait()


def weight_kernel(
    valid_ref, factor_ref, feats_hbm, low_hbm, mid_grad_hbm, first_grad_hbm, sums_ref,
    parts_ref, feats_ref, low_ref, mid_grad_ref, first_grad_ref, conv_ref, mid_ref, stage_ref, sems,
):
    local = valid_ref.shape[0]
    pairs = (
        (feats_hbm, feats_ref),
        (low_hbm, low_ref),
        (mid_grad_hbm, mid_grad_ref),
        (first_grad_hbm, first_grad_ref),
    )
    arrivals = []
    for j in range(local):
        rows = pl.ds(j * BT, BT)
        arrivals.append(
            [
                pltpu.make_async_copy(source.at[rows], target.at[rows], sems.at[i, j])
                for i, (source, target) in enumerate(pairs)
            ]
        )
        for copy in arrivals[j]:
            copy.start()
    out = jnp.zeros((1, D), F32)
    place = block_place(BT)
    for j in range(local):
        rows = pl.ds(j * BT, BT)
        for copy in arrivals[j]:
            copy.wait()
        factor = factor_ref[j]
        out += sums_ref[j : j + 1, :] * factor
        grad = first_grad_ref[rows, :].astype(F32) * factor
        before, after = neighbours(grad, place, BT - 1)
        mid_grad = (mid_grad_ref[rows, :].astype(F32) * factor).astype(BF16)
        keep = row_mask(valid_ref, j, 1)
        masked = jnp.where(keep, feats_ref[rows, :].astype(F32), 0.0).astype(BF16)
        terms = [
            lax.dot_general(masked, x, OVER_ROWS, preferred_element_type=F32)
            for x in (after, grad.astype(BF16), before)
        ]
        mid = lax.dot_general(low_ref[rows, :], mid_grad, OVER_ROWS, preferred_element_type=F32)
        for k in range(3):
            conv_ref[k] = terms[k] if j == 0 else conv_ref[k] + terms[k]
        mid_ref[...] = mid if j == 0 else mid_ref[...] + mid

    devices = parts_ref.shape[0]
    column = lax.broadcasted_iota(jnp.int32, (D, D), 0).astype(F32)
    place = lax.broadcasted_iota(jnp.int32, (D, D), 1).astype(F32)
    home = jnp.floor((column + 0.5) * (1.0 / SHARD))
    pick = jnp.where(column - SHARD * home == place, 1.0, 0.0).astype(BF16)
    device = lax.broadcasted_iota(jnp.int32, (devices, D), 0).astype(F32)
    lane = lax.broadcasted_iota(jnp.int32, (devices, D), 1).astype(F32)
    mine = jnp.floor((lane + 0.5) * (1.0 / SHARD)) == device
    out_rows = jnp.where(mine, out, 0.0).astype(BF16)
    out_rows = jnp.dot(out_rows, pick, preferred_element_type=F32)
    stage_ref[EXTRA:ROWS, :] = jnp.zeros((ROWS - EXTRA, D), F32)
    for d in range(devices):
        at = SHARD * d
        for k in range(3):
            stage_ref[SHARD * k : SHARD * (k + 1), :] = conv_ref[k, at : at + SHARD, :]
        stage_ref[3 * SHARD : EXTRA, :] = mid_ref[at : at + SHARD, :]
        stage_ref[EXTRA : EXTRA + 1, :] = out_rows[d : d + 1, :]
        parts_ref[d] = stage_ref[...].astype(BF16)


def finish_kernel(own_ref, first_ref, second_ref, third_ref, conv_ref, mid_ref, out_ref, total_ref):
    total = own_ref[...]
    for piece in (first_ref, second_ref, third_ref):
        total += piece[...].astype(F32)
    total_ref[...] = total * (1.0 / BT)
    for row in range(3 * SHARD):
        conv_ref[row] = total_ref[row : row + 1, :]
    for row in range(SHARD):
        mid_ref[row] = total_ref[3 * SHARD + row : 3 * SHARD + row + 1, :]
    out_ref[...] = total_ref[EXTRA : EXTRA + 1, 0:SHARD]


def place_kernel(
    source_ref, count_ref, factor_ref, received_ref, placed_ref, raw_ref, ready_ref, in_sems, out_sems
):
    capacity = source_ref.shape[0]
    arrivals, departures = [], []
    for slot in range(capacity):
        copy = pltpu.make_async_copy(
            received_ref.at[source_ref[slot]], raw_ref.at[slot], in_sems.at[slot]
        )
        copy.start()
        arrivals.append(copy)
    for slot in range(capacity):
        arrivals[slot].wait()
        factor = jnp.where(slot < count_ref[0], factor_ref[0], 0.0)
        ready_ref[slot] = (raw_ref[slot].astype(F32) * factor).astype(BF16)
        rows = pl.ds(slot * BT, BT)
        copy = pltpu.make_async_copy(ready_ref.at[slot], placed_ref.at[rows], out_sems.at[slot])
        copy.start()
        departures.append(copy)
    for copy in departures:
        copy.wait()


def in_hbm(x):
    return pltpu.with_memory_space_constraint(x, pltpu.HBM)


def in_vmem(x):
    return pltpu.with_memory_space_constraint(x, pltpu.VMEM)


def call(kernel, name, in_specs, outs, scratch=(), megabytes=0):
    return pl.pallas_call(
        kernel,
        in_specs=in_specs,
        out_specs=[spec for spec, _, _ in outs],
        out_shape=[
            (pltpu.HBM if spec is IN_HBM else pltpu.VMEM)(shape, dtype) for spec, shape, dtype in outs
        ],
        scratch_shapes=list(scratch),
        compiler_params=pltpu.CompilerParams(vmem_limit_bytes=VMEM_LIMIT),
        cost_estimate=pl.CostEstimate(
            flops=0, transcendentals=0, bytes_accessed=megabytes * 1024 * 1024
        ),
        name=name,
    )


def per_device(feats, valid, owner_map, w_conv, w_mid, w_out):
    local = owner_map.shape[0]
    devices = lax.axis_size(DP)
    chips = devices // 2
    capacity = devices // 2
    tokens_here = local * BT
    me = lax.axis_index(DP)
    core = lax.axis_index("dp_2").astype(jnp.int32).reshape(1)
    images = jnp.arange(devices, dtype=jnp.int32)

    (copies,) = call(
        pack_kernel,
        "pack",
        [IN_HBM] * 5,
        [(IN_VMEM, (chips, ROWS, D), BF16)],
        [
            pltpu.SMEM((local,), jnp.int32),
            pltpu.SMEM((local,), jnp.int32),
            pltpu.VMEM((3, SHARD, D), BF16),
            pltpu.VMEM((SHARD, D), BF16),
            pltpu.VMEM((1, SHARD), BF16),
            pltpu.VMEM((ROWS, D), F32),
            pltpu.SemaphoreType.DMA((5,)),
        ],
    )(*(in_hbm(x) for x in (valid, owner_map, w_conv[0], w_mid[0], w_out)))
    own = lax.all_to_all(copies, CHIPS, split_axis=0, concat_axis=0, tiled=True)
    other = swapped(own)

    low, mid_grad, state, sums, out_w, extras, totals = call(
        forward_kernel,
        "forward",
        [IN_SMEM, IN_SMEM, IN_SMEM, IN_HBM, IN_HBM, IN_HBM],
        [
            (IN_HBM, (tokens_here, D), BF16),
            (IN_HBM, (tokens_here, D), BF16),
            (IN_VMEM, (tokens_here + 4 * D, D), BF16),
            (IN_VMEM, (local, D), F32),
            (IN_VMEM, (1, D), F32),
            (IN_VMEM, (devices, 128), F32),
            (IN_VMEM, (chips, 1, 128), F32),
        ],
        [
            pltpu.VMEM((tokens_here, D), BF16),
            pltpu.VMEM((chips, ROWS, D), BF16),
            pltpu.VMEM((chips, ROWS, D), BF16),
            pltpu.VMEM((tokens_here, D), BF16),
            pltpu.VMEM((tokens_here, D), BF16),
            pltpu.VMEM((4 * D, D), F32),
            pltpu.SemaphoreType.DMA((local // GROUP,)),
            pltpu.SemaphoreType.DMA((2, local // GROUP)),
            pltpu.SemaphoreType.DMA((2,)),
        ],
    )(valid, owner_map, core, in_hbm(feats[0]), in_hbm(own), in_hbm(other))

    totals = lax.all_to_all(totals, CHIPS, split_axis=0, concat_axis=0, tiled=True)

    first_grad, slots = call(
        backward_kernel,
        "backward",
        [IN_SMEM, IN_SMEM, IN_HBM, IN_VMEM, IN_VMEM],
        [
            (IN_HBM, (tokens_here, D), BF16),
            (IN_HBM, (devices, BT, D), BF16),
        ],
        [
            pltpu.VMEM((tokens_here, D), BF16),
            pltpu.VMEM((tokens_here, D), BF16),
            pltpu.VMEM((local, BT, D), BF16),
            pltpu.SemaphoreType.DMA((local,)),
            pltpu.SemaphoreType.DMA((local // GROUP,)),
            pltpu.SemaphoreType.DMA((local // GROUP,)),
        ],
        megabytes=24,
    )(valid, owner_map, in_hbm(mid_grad), in_vmem(state), in_vmem(out_w))

    slots, totals = lax.optimization_barrier((slots, totals))
    received = lax.all_to_all(slots, DP, split_axis=0, concat_axis=0, tiled=True)

    totals = total_over(jnp.sum(totals[:, 0, :devices], 0)[None], "dp_2")
    totals = total_over(totals, "head")[0]
    members = (owner_map[:, None] == images[None, :]).astype(F32)
    owners = extras[:, SHARD : SHARD + local].astype(jnp.int32)
    valids = extras[:, SHARD + local : SHARD + 2 * local]
    tokens = jnp.sum(jnp.where(owners[:, :, None] == images, valids[:, :, None], 0.0), (0, 1))
    norm = jnp.sqrt(TAPS * tokens)
    factor = -BT * jax.nn.sigmoid(-totals / norm) / norm
    block_factor = jnp.sum(members * factor[None, :], 1)
    own_factor = jnp.sum(jnp.where(images == me, factor, 0.0)).reshape(1)

    (parts,) = call(
        weight_kernel,
        "weight_grads",
        [IN_SMEM, IN_SMEM, IN_HBM, IN_HBM, IN_HBM, IN_HBM, IN_VMEM],
        [(IN_VMEM, (devices, ROWS, D), BF16)],
        [pltpu.VMEM((tokens_here, D), BF16)] * 4
        + [
            pltpu.VMEM((3, D, D), F32),
            pltpu.VMEM((D, D), F32),
            pltpu.VMEM((ROWS, D), F32),
            pltpu.SemaphoreType.DMA((4, local)),
        ],
        megabytes=16,
    )(
        valid, block_factor, in_hbm(feats[0]), in_hbm(low), in_hbm(mid_grad),
        in_hbm(first_grad), in_vmem(sums),
    )
    own_parts, other_parts = shares(jnp.moveaxis(parts.reshape(chips, 2, ROWS, D), 1, 0), core[0])
    parts = added([own_parts, swapped(other_parts)]).reshape(4, 4, ROWS, D)
    parts = jnp.where(core[0] == 0, parts, jnp.swapaxes(parts, 0, 1))
    row, column = lax.axis_index("dp_0"), lax.axis_index("dp_1")
    ready = shares(parts, jnp.where(core[0] == 0, row, column))
    parts = added(delivered(*ready, stage=0))

    present = jnp.sum((owners == me).astype(jnp.int32), 1)
    rank = jnp.sum(jnp.where(images[None, :] < images[:, None], present[None, :], 0), 1)
    count = jnp.sum(present)
    wanted = jnp.minimum(jnp.arange(capacity, dtype=jnp.int32), count - 1)
    hit = (rank[None, :] == wanted[:, None]) & (present[None, :] > 0)
    source = jnp.sum(jnp.where(hit, images[None, :], 0), 1).astype(jnp.int32)
    table = (source, count.reshape(1), own_factor)
    parts, received, table = lax.optimization_barrier((parts, received, table))
    ready = shares(parts, jnp.where(core[0] == 0, column, row))
    pieces = delivered(*ready, stage=1)
    (placed,) = call(
        place_kernel,
        "place",
        [IN_SMEM, IN_SMEM, IN_SMEM, IN_HBM],
        [(IN_HBM, (capacity * BT, D), BF16)],
        [
            pltpu.VMEM((capacity, BT, D), BF16),
            pltpu.VMEM((capacity, BT, D), BF16),
            pltpu.SemaphoreType.DMA((capacity,)),
            pltpu.SemaphoreType.DMA((capacity,)),
        ],
        megabytes=24,
    )(*table, in_hbm(received))

    conv, mid, out = pl.pallas_call(
        finish_kernel,
        in_specs=[IN_VMEM] * 4,
        out_specs=[IN_VMEM] * 3,
        out_shape=[
            jax.ShapeDtypeStruct((3 * SHARD, 1, D), F32),
            jax.ShapeDtypeStruct((SHARD, 1, D), F32),
            jax.ShapeDtypeStruct((1, SHARD), F32),
        ],
        scratch_shapes=[pltpu.VMEM((ROWS, D), F32)],
        name="finish",
    )(*(in_vmem(x) for x in pieces))
    return placed[None], conv.reshape(1, 3, SHARD, D), mid.reshape(1, SHARD, D), out


def solution(mesh):
    split = Mesh(
        mesh.devices.reshape(4, 4, 2, mesh.shape["head"]), ("dp_0", "dp_1", "dp_2", "head")
    )
    in_specs = (
        P("head", DP, None),
        P(DP),
        P(DP),
        P("head", None, DP, None),
        P("head", DP, None),
        P("head", DP),
    )
    out_specs = (P("head", DP, None), P("head", None, DP, None), P("head", DP, None), P("head", DP))
    return jax.shard_map(
        per_device, mesh=split, in_specs=in_specs, out_specs=out_specs, check_vma=False
    )
```

```python
import jax
import jax.numpy as jnp
from jax import lax
from jax.experimental import pallas as pl
from jax.experimental.pallas import tpu as pltpu
from jax.sharding import Mesh
from jax.sharding import PartitionSpec as P

DP = ("dp_0", "dp_1", "dp_2")
CHIPS = ("dp_0", "dp_1")
BF16 = jnp.bfloat16
F32 = jnp.float32
TAPS = 4
BT = 256
D = 384
SHARD = 12
EXTRA = 4 * SHARD
ROWS = 56
GROUP = 4
LOG_2 = 0.6931471805599453
VMEM_LIMIT = 20 * 1024 * 1024

IN_VMEM = pl.BlockSpec(memory_space=pltpu.VMEM)
IN_SMEM = pl.BlockSpec(memory_space=pltpu.SMEM)
IN_HBM = pl.BlockSpec(memory_space=pltpu.HBM)
OVER_LAST = (((1,), (1,)), ((), ()))
OVER_ROWS = (((0,), (0,)), ((), ()))


def swapped(x):
    return lax.ppermute(x, "dp_2", [(0, 1), (1, 0)])


def turned(x, axis, shift):
    count = lax.axis_size(axis)
    return lax.ppermute(x, axis, [(i, (i + shift) % count) for i in range(count)])


def total_over(x, axis):
    return sum((turned(x, axis, r) for r in range(1, lax.axis_size(axis))), x)


def shares(parts, index):
    count = parts.shape[0]

    def share(shift):
        return lax.dynamic_index_in_dim(parts, (index + shift) % count, 0, keepdims=False)

    return [share(0)] + [share(r).astype(BF16) for r in range(1, count)]


def crossed(x, shift, stage):
    tall, wide = lax.axis_size("dp_0"), lax.axis_size("dp_1")
    pairs = []
    for y in range(tall):
        for x_at in range(wide):
            for core in range(2):
                along_first = core == stage
                to_y = (y + shift) % tall if along_first else y
                to_x = x_at if along_first else (x_at + shift) % wide
                pairs.append(((y * wide + x_at) * 2 + core, (to_y * wide + to_x) * 2 + core))
    return lax.ppermute(x, DP, pairs)


def delivered(own, *others, stage):
    return [own] + [crossed(other, r, stage) for r, other in enumerate(others, 1)]


def added(pieces):
    return sum(piece.astype(F32) for piece in pieces)


def gate(value):
    half = jnp.tanh(0.5 * value)
    tail = 0.8 * LOG_2 - (0.8 * LOG_2) * jnp.log2(1.0 + jnp.abs(half))
    return jnp.maximum(value, 0.2 * value) + tail, 0.6 + 0.4 * half


def row_mask(valid_ref, first, blocks):
    rows = lax.broadcasted_iota(jnp.int32, (blocks * BT, 1), 0)
    limit = jnp.full_like(rows, valid_ref[first])
    for j in range(1, blocks):
        limit = jnp.where(rows < j * BT, limit, j * BT + valid_ref[first + j])
    return rows < limit


def neighbours(x, place, last):
    count = x.shape[0]
    before = jnp.where(place == 0, 0.0, pltpu.roll(x, 1, 0))
    after = jnp.where(place == last, 0.0, pltpu.roll(x, count - 1, 0))
    return before.astype(BF16), after.astype(BF16)


def block_place(count):
    return lax.broadcasted_iota(jnp.int32, (count, 1), 0) % BT


def pack_kernel(
    valid_hbm, owner_hbm, conv_hbm, mid_hbm, out_hbm,
    copies_ref, valid_ref, owner_ref, conv_ref, mid_ref, out_ref, stage_ref, sems,
):
    sources = (valid_hbm, owner_hbm, conv_hbm, mid_hbm, out_hbm)
    targets = (valid_ref, owner_ref, conv_ref, mid_ref, out_ref)
    arrivals = [
        pltpu.make_async_copy(source, target, sems.at[i])
        for i, (source, target) in enumerate(zip(sources, targets))
    ]
    for copy in arrivals:
        copy.start()
    for copy in arrivals:
        copy.wait()
    local = valid_ref.shape[0]
    lane = lax.broadcasted_iota(jnp.int32, (1, D), 1)
    extras = jnp.zeros((1, D), F32)
    for j in range(local):
        extras = jnp.where(lane == SHARD + j, owner_ref[j].astype(F32), extras)
        extras = jnp.where(lane == SHARD + local + j, valid_ref[j].astype(F32), extras)
    stage_ref[EXTRA:ROWS, :] = jnp.zeros((ROWS - EXTRA, D), F32)
    for k in range(3):
        stage_ref[SHARD * k : SHARD * (k + 1), :] = conv_ref[k].astype(F32)
    stage_ref[3 * SHARD : EXTRA, :] = mid_ref[...].astype(F32)
    stage_ref[EXTRA : EXTRA + 1, :] = extras
    stage_ref[EXTRA : EXTRA + 1, 0:SHARD] = out_ref[...].astype(F32)
    packed = stage_ref[...].astype(BF16)
    for j in range(copies_ref.shape[0]):
        copies_ref[j] = packed


def state_rows(local):
    tokens = local * BT
    return pl.ds(0, tokens), pl.ds(tokens, 4 * D)


def weight(ref, k):
    return ref[k * D : (k + 1) * D, :]


def forward_kernel(
    valid_ref, owner_ref, core_ref, feats_ref, own_hbm, other_hbm,
    low_out, mid_grad_out, state_ref, sums_ref, out_w_ref, extras_ref, totals_ref,
    raw_ref, own_ref, other_ref, low_ref, mid_grad_ref, wide_ref, sems, out_sems, weight_sems,
):
    local = valid_ref.shape[0]
    slope_ref, weights_ref = (state_ref.at[rows] for rows in state_rows(local))
    arrivals = [
        pltpu.make_async_copy(own_hbm, own_ref, weight_sems.at[0]),
        pltpu.make_async_copy(other_hbm, other_ref, weight_sems.at[1]),
    ]
    for n, j in enumerate(range(0, local, GROUP)):
        rows = pl.ds(j * BT, GROUP * BT)
        arrivals.append(pltpu.make_async_copy(feats_ref.at[rows], raw_ref.at[rows], sems.at[n]))
    for copy in arrivals:
        copy.start()

    def unpack(parity, source):
        for chip in range(source.shape[0]):
            tile = source[chip].astype(F32)
            device = 2 * chip + parity
            at = SHARD * device
            for k in range(4):
                wide_ref[k * D + at : k * D + at + SHARD, :] = tile[SHARD * k : SHARD * (k + 1)]
            extras_ref[device : device + 1, :] = tile[EXTRA : EXTRA + 1, :128]

    for copy in arrivals[:2]:
        copy.wait()

    @pl.when(core_ref[0] == 0)
    def _():
        unpack(0, own_ref)
        unpack(1, other_ref)

    @pl.when(core_ref[0] == 1)
    def _():
        unpack(1, own_ref)
        unpack(0, other_ref)

    weights_ref[...] = wide_ref[...].astype(BF16)
    devices = extras_ref.shape[0]
    column = lax.broadcasted_iota(jnp.int32, (128, D), 1).astype(F32)
    place = lax.broadcasted_iota(jnp.int32, (128, D), 0).astype(F32)
    home = jnp.floor((column + 0.5) * (1.0 / SHARD))
    pick = jnp.where(column - SHARD * home == place, 1.0, 0.0).astype(BF16)
    spread = jnp.dot(extras_ref[...].astype(BF16), pick, preferred_element_type=F32)
    row = lax.broadcasted_iota(jnp.int32, (devices, D), 0).astype(F32)
    out_w = jnp.sum(jnp.where(home[:devices] == row, spread, 0.0), 0, keepdims=True)
    out_w_ref[...] = out_w

    lane = lax.broadcasted_iota(jnp.int32, (1, 128), 1)
    totals = jnp.zeros((1, 128), F32)
    departures = []
    for n, j in enumerate(range(0, local, GROUP)):
        rows = pl.ds(j * BT, GROUP * BT)
        arrivals[2 + n].wait()
        place = block_place(GROUP * BT)
        keep = row_mask(valid_ref, j, GROUP)
        masked = jnp.where(keep, raw_ref[rows, :].astype(F32), 0.0)
        before, after = neighbours(masked, place, BT - 1)
        first = jnp.dot(before, weight(weights_ref, 0), preferred_element_type=F32)
        first += jnp.dot(
            masked.astype(BF16), weight(weights_ref, 1), preferred_element_type=F32
        )
        first += jnp.dot(after, weight(weights_ref, 2), preferred_element_type=F32)
        first_act, slope = gate(first)
        low = first_act.astype(BF16)
        low_ref[rows, :] = low
        copy = pltpu.make_async_copy(low_ref.at[rows], low_out.at[rows], out_sems.at[0, n])
        copy.start()
        departures.append(copy)
        slope_ref[rows, :] = slope.astype(BF16)
        second = jnp.dot(low, weight(weights_ref, 3), preferred_element_type=F32)
        second_act, second_slope = gate(second)
        mid_grad_ref[rows, :] = jnp.where(keep, out_w * second_slope, 0.0).astype(BF16)
        copy = pltpu.make_async_copy(
            mid_grad_ref.at[rows], mid_grad_out.at[rows], out_sems.at[1, n]
        )
        copy.start()
        departures.append(copy)
        total = jnp.where(keep, second_act + first_act, 0.0)
        for i in range(GROUP):
            block = jnp.sum(total[i * BT : (i + 1) * BT], 0, keepdims=True)
            sums_ref[j + i : j + i + 1, :] = block
            block_sum = jnp.sum(block * out_w, 1, keepdims=True)
            totals += jnp.where(lane == owner_ref[j + i], block_sum, 0.0)
    for chip in range(devices // 2):
        totals_ref[chip] = totals
    for copy in departures:
        copy.wait()


def backward_kernel(
    valid_ref, owner_ref, mid_grad_hbm, state_ref, out_w_ref,
    first_grad_out, slots_ref, mid_grad_ref, first_grad_ref, ready_ref, sems, out_sems, in_sems,
):
    local = valid_ref.shape[0]
    slope_ref, weights_ref = (state_ref.at[rows] for rows in state_rows(local))
    place = block_place(GROUP * BT)
    arrivals, copies = [], []
    for j in range(0, local, GROUP):
        rows = pl.ds(j * BT, GROUP * BT)
        copy = pltpu.make_async_copy(
            mid_grad_hbm.at[rows], mid_grad_ref.at[rows], in_sems.at[j // GROUP]
        )
        copy.start()
        arrivals.append(copy)
    for j in range(0, local, GROUP):
        rows = pl.ds(j * BT, GROUP * BT)
        arrivals[j // GROUP].wait()
        keep = row_mask(valid_ref, j, GROUP)
        grad = lax.dot_general(
            mid_grad_ref[rows, :], weight(weights_ref, 3), OVER_LAST, preferred_element_type=F32
        )
        grad = (grad + jnp.where(keep, out_w_ref[...], 0.0)) * slope_ref[rows, :].astype(F32)
        before, after = neighbours(grad, place, BT - 1)
        low = grad.astype(BF16)
        first_grad_ref[rows, :] = low
        total = lax.dot_general(low, weight(weights_ref, 1), OVER_LAST, preferred_element_type=F32)
        total += lax.dot_general(
            after, weight(weights_ref, 0), OVER_LAST, preferred_element_type=F32
        )
        total += lax.dot_general(
            before, weight(weights_ref, 2), OVER_LAST, preferred_element_type=F32
        )
        total = jnp.where(keep, total, 0.0).astype(BF16)
        for i in range(GROUP):
            ready_ref[j + i] = total[i * BT : (i + 1) * BT]
            copy = pltpu.make_async_copy(
                ready_ref.at[j + i], slots_ref.at[owner_ref[j + i]], sems.at[j + i]
            )
            copy.start()
            copies.append(copy)
        copy = pltpu.make_async_copy(
            first_grad_ref.at[rows], first_grad_out.at[rows], out_sems.at[j // GROUP]
        )
        copy.start()
        copies.append(copy)
    for copy in copies:
        copy.wait()


def weight_kernel(
    valid_ref, factor_ref, feats_hbm, low_hbm, mid_grad_hbm, first_grad_hbm, sums_ref,
    parts_ref, feats_ref, low_ref, mid_grad_ref, first_grad_ref, conv_ref, mid_ref, stage_ref, sems,
):
    local = valid_ref.shape[0]
    pairs = (
        (feats_hbm, feats_ref),
        (low_hbm, low_ref),
        (mid_grad_hbm, mid_grad_ref),
        (first_grad_hbm, first_grad_ref),
    )
    arrivals = []
    for j in range(local):
        rows = pl.ds(j * BT, BT)
        arrivals.append(
            [
                pltpu.make_async_copy(source.at[rows], target.at[rows], sems.at[i, j])
                for i, (source, target) in enumerate(pairs)
            ]
        )
        for copy in arrivals[j]:
            copy.start()
    out = jnp.zeros((1, D), F32)
    place = block_place(BT)
    for j in range(local):
        rows = pl.ds(j * BT, BT)
        for copy in arrivals[j]:
            copy.wait()
        factor = factor_ref[j]
        out += sums_ref[j : j + 1, :] * factor
        grad = first_grad_ref[rows, :].astype(F32) * factor
        before, after = neighbours(grad, place, BT - 1)
        mid_grad = (mid_grad_ref[rows, :].astype(F32) * factor).astype(BF16)
        keep = row_mask(valid_ref, j, 1)
        masked = jnp.where(keep, feats_ref[rows, :].astype(F32), 0.0).astype(BF16)
        terms = [
            lax.dot_general(masked, x, OVER_ROWS, preferred_element_type=F32)
            for x in (after, grad.astype(BF16), before)
        ]
        mid = lax.dot_general(low_ref[rows, :], mid_grad, OVER_ROWS, preferred_element_type=F32)
        for k in range(3):
            conv_ref[k] = terms[k] if j == 0 else conv_ref[k] + terms[k]
        mid_ref[...] = mid if j == 0 else mid_ref[...] + mid

    devices = parts_ref.shape[0]
    column = lax.broadcasted_iota(jnp.int32, (D, D), 0).astype(F32)
    place = lax.broadcasted_iota(jnp.int32, (D, D), 1).astype(F32)
    home = jnp.floor((column + 0.5) * (1.0 / SHARD))
    pick = jnp.where(column - SHARD * home == place, 1.0, 0.0).astype(BF16)
    device = lax.broadcasted_iota(jnp.int32, (devices, D), 0).astype(F32)
    lane = lax.broadcasted_iota(jnp.int32, (devices, D), 1).astype(F32)
    mine = jnp.floor((lane + 0.5) * (1.0 / SHARD)) == device
    out_rows = jnp.where(mine, out, 0.0).astype(BF16)
    out_rows = jnp.dot(out_rows, pick, preferred_element_type=F32)
    stage_ref[EXTRA:ROWS, :] = jnp.zeros((ROWS - EXTRA, D), F32)
    for d in range(devices):
        at = SHARD * d
        for k in range(3):
            stage_ref[SHARD * k : SHARD * (k + 1), :] = conv_ref[k, at : at + SHARD, :]
        stage_ref[3 * SHARD : EXTRA, :] = mid_ref[at : at + SHARD, :]
        stage_ref[EXTRA : EXTRA + 1, :] = out_rows[d : d + 1, :]
        parts_ref[d] = stage_ref[...].astype(BF16)


def finish_kernel(own_ref, first_ref, second_ref, third_ref, conv_ref, mid_ref, out_ref, total_ref):
    total = own_ref[...]
    for piece in (first_ref, second_ref, third_ref):
        total += piece[...].astype(F32)
    total_ref[...] = total * (1.0 / BT)
    for row in range(3 * SHARD):
        conv_ref[row] = total_ref[row : row + 1, :]
    for row in range(SHARD):
        mid_ref[row] = total_ref[3 * SHARD + row : 3 * SHARD + row + 1, :]
    out_ref[...] = total_ref[EXTRA : EXTRA + 1, 0:SHARD]


def place_kernel(
    source_ref, count_ref, factor_ref, received_ref, placed_ref, raw_ref, ready_ref, in_sems, out_sems
):
    capacity = source_ref.shape[0]
    arrivals, departures = [], []
    for slot in range(capacity):
        copy = pltpu.make_async_copy(
            received_ref.at[source_ref[slot]], raw_ref.at[slot], in_sems.at[slot]
        )
        copy.start()
        arrivals.append(copy)
    for slot in range(capacity):
        arrivals[slot].wait()
        factor = jnp.where(slot < count_ref[0], factor_ref[0], 0.0)
        ready_ref[slot] = (raw_ref[slot].astype(F32) * factor).astype(BF16)
        rows = pl.ds(slot * BT, BT)
        copy = pltpu.make_async_copy(ready_ref.at[slot], placed_ref.at[rows], out_sems.at[slot])
        copy.start()
        departures.append(copy)
    for copy in departures:
        copy.wait()


def in_hbm(x):
    return pltpu.with_memory_space_constraint(x, pltpu.HBM)


def in_vmem(x):
    return pltpu.with_memory_space_constraint(x, pltpu.VMEM)


def call(kernel, name, in_specs, outs, scratch=(), megabytes=0):
    return pl.pallas_call(
        kernel,
        in_specs=in_specs,
        out_specs=[spec for spec, _, _ in outs],
        out_shape=[
            (pltpu.HBM if spec is IN_HBM else pltpu.VMEM)(shape, dtype) for spec, shape, dtype in outs
        ],
        scratch_shapes=list(scratch),
        compiler_params=pltpu.CompilerParams(vmem_limit_bytes=VMEM_LIMIT),
        cost_estimate=pl.CostEstimate(
            flops=0, transcendentals=0, bytes_accessed=megabytes * 1024 * 1024
        ),
        name=name,
    )


def per_device(feats, valid, owner_map, w_conv, w_mid, w_out):
    local = owner_map.shape[0]
    devices = lax.axis_size(DP)
    chips = devices // 2
    capacity = devices // 2
    tokens_here = local * BT
    me = lax.axis_index(DP)
    core = lax.axis_index("dp_2").astype(jnp.int32).reshape(1)
    images = jnp.arange(devices, dtype=jnp.int32)

    (copies,) = call(
        pack_kernel,
        "pack",
        [IN_HBM] * 5,
        [(IN_VMEM, (chips, ROWS, D), BF16)],
        [
            pltpu.SMEM((local,), jnp.int32),
            pltpu.SMEM((local,), jnp.int32),
            pltpu.VMEM((3, SHARD, D), BF16),
            pltpu.VMEM((SHARD, D), BF16),
            pltpu.VMEM((1, SHARD), BF16),
            pltpu.VMEM((ROWS, D), F32),
            pltpu.SemaphoreType.DMA((5,)),
        ],
    )(*(in_hbm(x) for x in (valid, owner_map, w_conv[0], w_mid[0], w_out)))
    own = lax.all_to_all(copies, CHIPS, split_axis=0, concat_axis=0, tiled=True)
    other = swapped(own)

    low, mid_grad, state, sums, out_w, extras, totals = call(
        forward_kernel,
        "forward",
        [IN_SMEM, IN_SMEM, IN_SMEM, IN_HBM, IN_HBM, IN_HBM],
        [
            (IN_HBM, (tokens_here, D), BF16),
            (IN_HBM, (tokens_here, D), BF16),
            (IN_VMEM, (tokens_here + 4 * D, D), BF16),
            (IN_VMEM, (local, D), F32),
            (IN_VMEM, (1, D), F32),
            (IN_VMEM, (devices, 128), F32),
            (IN_VMEM, (chips, 1, 128), F32),
        ],
        [
            pltpu.VMEM((tokens_here, D), BF16),
            pltpu.VMEM((chips, ROWS, D), BF16),
            pltpu.VMEM((chips, ROWS, D), BF16),
            pltpu.VMEM((tokens_here, D), BF16),
            pltpu.VMEM((tokens_here, D), BF16),
            pltpu.VMEM((4 * D, D), F32),
            pltpu.SemaphoreType.DMA((local // GROUP,)),
            pltpu.SemaphoreType.DMA((2, local // GROUP)),
            pltpu.SemaphoreType.DMA((2,)),
        ],
    )(valid, owner_map, core, in_hbm(feats[0]), in_hbm(own), in_hbm(other))

    totals = lax.all_to_all(totals, CHIPS, split_axis=0, concat_axis=0, tiled=True)

    first_grad, slots = call(
        backward_kernel,
        "backward",
        [IN_SMEM, IN_SMEM, IN_HBM, IN_VMEM, IN_VMEM],
        [
            (IN_HBM, (tokens_here, D), BF16),
            (IN_HBM, (devices, BT, D), BF16),
        ],
        [
            pltpu.VMEM((tokens_here, D), BF16),
            pltpu.VMEM((tokens_here, D), BF16),
            pltpu.VMEM((local, BT, D), BF16),
            pltpu.SemaphoreType.DMA((local,)),
            pltpu.SemaphoreType.DMA((local // GROUP,)),
            pltpu.SemaphoreType.DMA((local // GROUP,)),
        ],
        megabytes=24,
    )(valid, owner_map, in_hbm(mid_grad), in_vmem(state), in_vmem(out_w))

    slots, totals = lax.optimization_barrier((slots, totals))
    received = lax.all_to_all(slots, DP, split_axis=0, concat_axis=0, tiled=True)

    totals = total_over(jnp.sum(totals[:, 0, :devices], 0)[None], "dp_2")
    totals = total_over(totals, "head")[0]
    members = (owner_map[:, None] == images[None, :]).astype(F32)
    owners = extras[:, SHARD : SHARD + local].astype(jnp.int32)
    valids = extras[:, SHARD + local : SHARD + 2 * local]
    tokens = jnp.sum(jnp.where(owners[:, :, None] == images, valids[:, :, None], 0.0), (0, 1))
    norm = jnp.sqrt(TAPS * tokens)
    factor = -BT * jax.nn.sigmoid(-totals / norm) / norm
    block_factor = jnp.sum(members * factor[None, :], 1)
    own_factor = jnp.sum(jnp.where(images == me, factor, 0.0)).reshape(1)

    (parts,) = call(
        weight_kernel,
        "weight_grads",
        [IN_SMEM, IN_SMEM, IN_HBM, IN_HBM, IN_HBM, IN_HBM, IN_VMEM],
        [(IN_VMEM, (devices, ROWS, D), BF16)],
        [pltpu.VMEM((tokens_here, D), BF16)] * 4
        + [
            pltpu.VMEM((3, D, D), F32),
            pltpu.VMEM((D, D), F32),
            pltpu.VMEM((ROWS, D), F32),
            pltpu.SemaphoreType.DMA((4, local)),
        ],
        megabytes=16,
    )(
        valid, block_factor, in_hbm(feats[0]), in_hbm(low), in_hbm(mid_grad),
        in_hbm(first_grad), in_vmem(sums),
    )
    own_parts, other_parts = shares(jnp.moveaxis(parts.reshape(chips, 2, ROWS, D), 1, 0), core[0])
    parts = added([own_parts, swapped(other_parts)]).reshape(4, 4, ROWS, D)
    parts = jnp.where(core[0] == 0, parts, jnp.swapaxes(parts, 0, 1))
    row, column = lax.axis_index("dp_0"), lax.axis_index("dp_1")
    ready = shares(parts, jnp.where(core[0] == 0, row, column))
    parts = added(delivered(*ready, stage=0))

    present = jnp.sum((owners == me).astype(jnp.int32), 1)
    rank = jnp.sum(jnp.where(images[None, :] < images[:, None], present[None, :], 0), 1)
    count = jnp.sum(present)
    wanted = jnp.minimum(jnp.arange(capacity, dtype=jnp.int32), count - 1)
    hit = (rank[None, :] == wanted[:, None]) & (present[None, :] > 0)
    source = jnp.sum(jnp.where(hit, images[None, :], 0), 1).astype(jnp.int32)
    table = (source, count.reshape(1), own_factor)
    ready = shares(parts, jnp.where(core[0] == 0, column, row))
    pieces = delivered(*ready, stage=1)
    received, table, _ = lax.optimization_barrier((received, table, ready))
    (placed,) = call(
        place_kernel,
        "place",
        [IN_SMEM, IN_SMEM, IN_SMEM, IN_HBM],
        [(IN_HBM, (capacity * BT, D), BF16)],
        [
            pltpu.VMEM((capacity, BT, D), BF16),
            pltpu.VMEM((capacity, BT, D), BF16),
            pltpu.SemaphoreType.DMA((capacity,)),
            pltpu.SemaphoreType.DMA((capacity,)),
        ],
        megabytes=24,
    )(*table, in_hbm(received))

    pieces, placed = lax.optimization_barrier((pieces, placed))
    conv, mid, out = pl.pallas_call(
        finish_kernel,
        in_specs=[IN_VMEM] * 4,
        out_specs=[IN_VMEM] * 3,
        out_shape=[
            jax.ShapeDtypeStruct((3 * SHARD, 1, D), F32),
            jax.ShapeDtypeStruct((SHARD, 1, D), F32),
            jax.ShapeDtypeStruct((1, SHARD), F32),
        ],
        scratch_shapes=[pltpu.VMEM((ROWS, D), F32)],
        name="finish",
    )(*(in_vmem(x) for x in pieces))
    return placed[None], conv.reshape(1, 3, SHARD, D), mid.reshape(1, SHARD, D), out


def solution(mesh):
    split = Mesh(
        mesh.devices.reshape(4, 4, 2, mesh.shape["head"]), ("dp_0", "dp_1", "dp_2", "head")
    )
    in_specs = (
        P("head", DP, None),
        P(DP),
        P(DP),
        P("head", None, DP, None),
        P("head", DP, None),
        P("head", DP),
    )
    out_specs = (P("head", DP, None), P("head", None, DP, None), P("head", DP, None), P("head", DP))
    return jax.shard_map(
        per_device, mesh=split, in_specs=in_specs, out_specs=out_specs, check_vma=False
    )
```
